256 devices in a mesh: gx: 32 (over z, x), gy: 8 (over y, core).
Axes of the slice: x: 4, y: 4, z: 8, core: 2. Of those that a mesh axis runs over, the one named last changes fastest.
Arguments:
- field: bfloat16 [20, 256, 128, 256], P(None, 'gx', 'gy'), may hold values from -6 to 6
- cotangent: bfloat16 [20, 256, 128, 256], P(None, 'gx', 'gy'), may hold values from -6 to 6
- spectral_weight: bfloat16 [2, 20, 20, 24, 2304], P(None, None, None, 'gy', 'gx'), may hold values from -6 to 6
- pointwise_weight: bfloat16 [20, 20], replicated, may hold values from -1.25 to 1.25
- bias: float32 [20], replicated, may hold values from -1 to 1
Outputs:
- output: bfloat16 [20, 256, 128, 256], P(None, 'gx', 'gy')
- grad_field: bfloat16 [20, 256, 128, 256], P(None, 'gx', 'gy')
- grad_spectral: float32 [2, 20, 20, 24, 2304], P(None, None, None, 'gy', 'gx')
- grad_pointwise: float32 [20, 20], replicated
- grad_bias: float32 [20], replicated
The draws below stay inside these ranges and needn't reach their ends.
All inputs are finite; a program needn't handle non-finite values.
Results may differ from the reference program's by a relative error of at most 0.0013.
Values sent between devices are 32-bit elements; how exact they have to be, the bound alone decides.
A program may use at most 128 MiB of HBM per device.

```python
import math
import jax
import jax.numpy as jnp
from jax import lax

C = 20
MX = 24
MY = 24
MZ = 24
NZ = 256
CX = 8
NX = 256
NY = 128
PAIRS = 2304


def levels(rng, shape, pieces, smallest, high):
    factor_of, own = 1.0, jax.random.fold_in(rng, 6)
    for axis_at, blocks in pieces:
        heights = jnp.exp(jax.random.uniform(jax.random.fold_in(own, axis_at), (blocks,), jnp.float32, smallest / len(pieces), high / len(pieces)))
        factor_of = factor_of * jnp.repeat(heights, shape[axis_at] // blocks).reshape([-1 if axis == axis_at else 1 for axis in range(len(shape))])
    return factor_of


def scatter_about(key, shape, scale, most, cuts=(), kind=jnp.bfloat16):
    array = jax.random.normal(key, shape, jnp.float32) * scale
    if len(cuts) > 0:
        array = levels(key, shape, cuts, -0.22, 0.18) * array
    return jnp.clip(array, min=-most, max=most).astype(kind)


def setup_inputs(seed: int = 0) -> dict:
    key_of = jax.random.split(jax.random.key(seed), 6)
    field = scatter_about(key_of[0], (C, NX, NY, NZ), 1.0, 6.0, ((1, 32), (2, 8)))
    cotangent = scatter_about(key_of[1], (C, NX, NY, NZ), 1.0, 6.0, ((1, 32), (2, 8)))
    spectral_weight = scatter_about(key_of[2], (2, C, C, MZ, PAIRS), 1.0, 6.0, ((3, 8), (4, 32)))
    pointwise_weight = scatter_about(key_of[3], (C, C), C ** -0.5, 1.25)
    bias = jnp.clip(jax.random.uniform(key_of[4], (C,), jnp.float32, -1.0, 1.0), -1.0, 1.0)
    return dict(field=field, cotangent=cotangent, spectral_weight=spectral_weight, pointwise_weight=pointwise_weight, bias=bias)


PRECISE = lax.Precision.HIGHEST
TWO_PI = 2.0 * math.pi

def angles(frequencies, places, length):
    product = places[:, None] * frequencies[None, :] % length
    return product.astype(jnp.float32) * (TWO_PI / length)

def frequency(position, kept_modes, length):
    return jnp.where(position < kept_modes, position, position - 2 * kept_modes + length).astype(jnp.int32)

def forward_y(values, phases):
    cosine_table = jnp.cos(phases)
    sine_table = jnp.sin(phases)
    with_cos = jnp.einsum('cxymr,yj->cxjmr', values, cosine_table, precision=PRECISE)
    with_sin = jnp.einsum('cxymr,yj->cxjmr', values, sine_table, precision=PRECISE)
    real_part = with_cos[..., 0] + with_sin[..., 1]
    imag_part = with_cos[..., 1] - with_sin[..., 0]
    return jnp.stack([real_part, imag_part], axis=-1)

def inverse_y(values, phases):
    cosine_table = jnp.cos(phases)
    sine_table = jnp.sin(phases)
    with_cos = jnp.einsum('cxjmr,yj->cxymr', values, cosine_table, precision=PRECISE)
    with_sin = jnp.einsum('cxjmr,yj->cxymr', values, sine_table, precision=PRECISE)
    real_part = with_cos[..., 0] - with_sin[..., 1]
    imag_part = with_sin[..., 0] + with_cos[..., 1]
    return jnp.stack([real_part, imag_part], axis=-1)

def forward_x(values, phases):
    cosine_table = jnp.cos(phases)
    sine_table = jnp.sin(phases)
    real_part = jnp.einsum('cxjm,xi->cijm', values[..., 0], cosine_table, precision=PRECISE) + jnp.einsum('cxjm,xi->cijm', values[..., 1], sine_table, precision=PRECISE)
    imag_part = jnp.einsum('cxjm,xi->cijm', values[..., 1], cosine_table, precision=PRECISE) - jnp.einsum('cxjm,xi->cijm', values[..., 0], sine_table, precision=PRECISE)
    return jnp.stack([real_part, imag_part], axis=-1)

def inverse_x(values, phases):
    cosine_table = jnp.cos(phases)
    sine_table = jnp.sin(phases)
    real_part = jnp.einsum('cijm,xi->cxjm', values[..., 0], cosine_table, precision=PRECISE) - jnp.einsum('cijm,xi->cxjm', values[..., 1], sine_table, precision=PRECISE)
    imag_part = jnp.einsum('cijm,xi->cxjm', values[..., 0], sine_table, precision=PRECISE) + jnp.einsum('cijm,xi->cxjm', values[..., 1], cosine_table, precision=PRECISE)
    return jnp.stack([real_part, imag_part], axis=-1)

def reference(field, cotangent, spectral_weight, pointwise_weight, bias):
    width_x = 2 * MX
    width_y = 2 * MY
    cell_count = float(NX * NY * NZ)
    freq_x = frequency(jnp.arange(width_x, dtype=jnp.int32), MX, NX)
    freq_y = frequency(jnp.arange(width_y, dtype=jnp.int32), MY, NY)
    phases_y = angles(freq_y, jnp.arange(NY, dtype=jnp.int32), NY)
    z_phases = angles(jnp.arange(MZ, dtype=jnp.int32), jnp.arange(NZ, dtype=jnp.int32), NZ)
    table_z = jnp.stack([jnp.cos(z_phases), -jnp.sin(z_phases)], axis=2).reshape(NZ, 2 * MZ)
    weight_z = (jnp.where(jnp.arange(MZ, dtype=jnp.int32) == 0, 1.0, 2.0).astype(jnp.float32) / cell_count)[:, None]
    block_count = NX // CX
    block_ids = jnp.arange(block_count, dtype=jnp.int32)

    def block_of(source, block_id):
        return lax.dynamic_slice_in_dim(source, (block_id * CX).astype(jnp.int32), CX, 1)

    def positions(block_id):
        return (block_id * CX + jnp.arange(CX, dtype=jnp.int32)).astype(jnp.int32)

    def analyze_block(block, places):
        spectra = jnp.dot(block.reshape(-1, NZ), table_z, precision=PRECISE).reshape(C, CX, NY, MZ, 2)
        return forward_x(forward_y(spectra, phases_y), angles(freq_x, places, NX))

    def synthesize_block(spectrum, places):
        rows = inverse_y(inverse_x(spectrum, angles(freq_x, places, NX)), phases_y)
        return jnp.dot(rows.reshape(-1, 2 * MZ), table_z.T, precision=PRECISE).reshape(C, CX, NY, NZ)

    def spectrum_step(running, block_id):
        block = block_of(field, block_id).astype(jnp.float32)
        return (running + analyze_block(block, positions(block_id)), None)
    zero_spec = jnp.zeros((C, width_x, width_y, MZ, 2), jnp.float32)
    spec_u, _ = lax.scan(spectrum_step, zero_spec, block_ids)
    weights = spectral_weight.astype(jnp.float32).reshape(2, C, C, MZ, width_x, width_y).transpose(1, 2, 4, 5, 3, 0)
    mixed_re = jnp.einsum('coijm,cijm->oijm', weights[..., 0], spec_u[..., 0], precision=PRECISE) - jnp.einsum('coijm,cijm->oijm', weights[..., 1], spec_u[..., 1], precision=PRECISE)
    mixed_im = jnp.einsum('coijm,cijm->oijm', weights[..., 0], spec_u[..., 1], precision=PRECISE) + jnp.einsum('coijm,cijm->oijm', weights[..., 1], spec_u[..., 0], precision=PRECISE)
    mixed_modes = jnp.stack([mixed_re, mixed_im], axis=-1) * weight_z

    def local_pre(block_id):
        block = block_of(field, block_id)
        conv = synthesize_block(mixed_modes, positions(block_id))
        pointwise = jnp.dot(pointwise_weight.T, block.reshape(C, -1), preferred_element_type=jnp.float32).reshape(C, CX, NY, NZ)
        preact = pointwise + bias[:, None, None, None] + conv
        activated, pullback = jax.vjp(jax.nn.gelu, preact)
        gradient = pullback(block_of(cotangent, block_id).astype(jnp.float32))[0]
        return (block, activated, gradient)

    def first_step(running, block_id):
        spec_d, sum_w, sum_b = running
        block, activated, gradient = local_pre(block_id)
        spec_d = spec_d + analyze_block(gradient, positions(block_id))
        grad_flat = gradient.reshape(C, -1)
        sum_w = sum_w + jnp.dot(block.astype(jnp.float32).reshape(C, -1), grad_flat.T, precision=PRECISE)
        sum_b = sum_b + lax.optimization_barrier(jnp.sum(grad_flat, axis=1))
        return ((spec_d, sum_w, sum_b), activated.astype(jnp.bfloat16))
    start_state = (zero_spec, jnp.zeros((C, C), jnp.float32), jnp.zeros((C,), jnp.float32))
    (spec_d, sum_w, sum_b), outputs = lax.scan(first_step, start_state, block_ids)
    output = outputs.transpose(1, 0, 2, 3, 4).reshape(C, NX, NY, NZ)
    grad_mix = spec_d * weight_z
    spec_re = jnp.einsum('coijm,oijm->cijm', weights[..., 0], grad_mix[..., 0], precision=PRECISE) + jnp.einsum('coijm,oijm->cijm', weights[..., 1], grad_mix[..., 1], precision=PRECISE)
    spec_im = jnp.einsum('coijm,oijm->cijm', weights[..., 0], grad_mix[..., 1], precision=PRECISE) - jnp.einsum('coijm,oijm->cijm', weights[..., 1], grad_mix[..., 0], precision=PRECISE)
    grad_spec = jnp.stack([spec_re, spec_im], axis=-1)
    weight_re = jnp.einsum('cijm,oijm->coijm', spec_u[..., 0], grad_mix[..., 0], precision=PRECISE) + jnp.einsum('cijm,oijm->coijm', spec_u[..., 1], grad_mix[..., 1], precision=PRECISE)
    weight_im = jnp.einsum('cijm,oijm->coijm', spec_u[..., 0], grad_mix[..., 1], precision=PRECISE) - jnp.einsum('cijm,oijm->coijm', spec_u[..., 1], grad_mix[..., 0], precision=PRECISE)
    grad_spectral = jnp.stack([weight_re, weight_im], axis=-1).transpose(5, 0, 1, 4, 2, 3).reshape(2, C, C, MZ, width_x * width_y)

    def second_step(block_id):
        block, activated, gradient = local_pre(block_id)
        returned = synthesize_block(grad_spec, positions(block_id))
        pointwise = jnp.dot(pointwise_weight.astype(jnp.float32), gradient.reshape(C, -1), precision=PRECISE).reshape(C, CX, NY, NZ)
        return (pointwise + returned).astype(jnp.bfloat16)
    grad_blocks = lax.map(second_step, block_ids)
    grad_field = grad_blocks.transpose(1, 0, 2, 3, 4).reshape(C, NX, NY, NZ)
    shrink = cell_count ** (-0.5)
    return (output, grad_field, grad_spectral, sum_w * shrink, sum_b * shrink)
```

```python
import functools

import jax
import jax.numpy as jnp
import numpy as np
from jax import lax
from jax.experimental import pallas as pl
from jax.experimental.pallas import tpu as pltpu
from jax.sharding import PartitionSpec as P

C = 20
NX, NY, NZ = 256, 128, 256
KX, KY, KZ = 48, 48, 24
GX, GY = 32, 8
CELLS = float(NX * NY * NZ)
F32 = jnp.float32
BF16 = jnp.bfloat16
MESH = pl.DeviceIdType.MESH
NN = (((1,), (0,)), ((), ()))
NT = (((1,), (1,)), ((), ()))
GELU_A = float(np.sqrt(2.0 / np.pi))
GELU_B = 0.044715


def halves(table):
    high = table.astype(BF16)
    low = (table - np.asarray(high, np.float64)).astype(BF16)
    return np.asarray(high), np.asarray(low)


def tables():
    kz, r, d = np.meshgrid(np.arange(3), np.arange(2), np.arange(8), indexing="ij")
    depth = (d * 3 + kz).reshape(-1, 1) * np.arange(NZ)[None, :] % NZ * (2 * np.pi / NZ)
    tz = np.where(r.reshape(-1, 1) == 0, np.cos(depth), -np.sin(depth))
    tz = np.concatenate(halves(tz), axis=0)

    fx = np.where(np.arange(KX) < 24, np.arange(KX), np.arange(KX) - 48 + NX)
    fy = np.where(np.arange(KY) < 24, np.arange(KY), np.arange(KY) - 48 + NY)
    phase = np.arange(NY)[:, None] * fy[None, :] % NY * (2 * np.pi / NY)
    cos, sin = np.cos(phase).reshape(8, 16, KY), np.sin(phase).reshape(8, 16, KY)
    y = np.zeros((8, 2, 16, 128))
    y[:, 0, :, 0:48], y[:, 0, :, 48:96] = cos, -sin
    y[:, 1, :, 0:48], y[:, 1, :, 48:96] = sin, cos
    yh, yl = halves(y.reshape(256, 128))

    g = np.arange(GX)
    first = 3 * (g // 2) + g % 2
    kx = first[:, None] + np.arange(2)[None, :]
    phase = fx[kx][:, :, None] * np.arange(NX)[None, None, :] % NX * (2 * np.pi / NX)
    both = np.stack([np.cos(phase), np.sin(phase)])
    both = both.reshape(2, GX, 2, GX, 8)
    eye = np.eye(2)
    ax = np.einsum("egtsx,mn->egmtsnx", both, eye).reshape(256, 512)
    bx = np.einsum("egtsx,mn->esmxgnt", both, eye).reshape(1024, 128)
    axh, axl = halves(ax)
    bxh, bxl = halves(bx)

    m = np.arange(64)
    kz_m = np.where(m < 48, m // 16, (m - 48) // 4)
    c_m = np.where(m < 48, m % 16, 16 + (m - 48) % 4)
    row = np.arange(120)
    sel_o = (row[None, :] // 6 == c_m[:, None]) & (row[None, :] % 6 // 2 == kz_m[:, None])
    row = np.arange(480)
    sel_c = (row[None, :] // 24 == c_m[:, None]) & (row[None, :] % 6 // 2 == kz_m[:, None])
    live = (m < 60)[:, None]
    sel_o = np.asarray((sel_o & live).astype(BF16))
    sel_c = np.asarray((sel_c & live).astype(BF16))
    return tz, yh, yl, axh, axl, bxh, bxl, sel_o, sel_c


def iota(shape, axis):
    return lax.broadcasted_iota(jnp.int32, shape, axis)


def dot(a, b, dims):
    return lax.dot_general(a, b, dims, preferred_element_type=F32)


def split(x):
    high = x.astype(BF16)
    return high, (x - high.astype(F32)).astype(BF16)


def dot3(a, b, dims):
    return dot(a[0], b[0], dims) + dot(a[0], b[1], dims) + dot(a[1], b[0], dims)


def pick(sel, x):
    high, low = split(x)
    return dot(sel, high, NN) + dot(sel, low, NN)


def kernel(
    field, cot, w, pw, bias, tz, yh, yl, axh, axl, bxh, bxl, sel_o, sel_c,
    out, gf, gs, small,
    fs, cs, gh, gl, pw1, pw2, bb, pws, sy, ry, sx, rx, sp, rp, wf, tmp,
    u1, u2, d1, d2, q1, q2, lw, ls, lr, ms, mr,
    sy_sem, ry_sem, sx_sem, rx_sem, sp_sem, rp_sem, l_sem,
):
    g = lax.axis_index("gx")
    yy = lax.axis_index("gy")
    even = lax.rem(g, 2) == 0

    barrier = pltpu.get_barrier_semaphore()

    def greet_y(k, _):
        pl.semaphore_signal(
            barrier, inc=1, device_id=(g, lax.rem(yy + k, GY)), device_id_type=MESH
        )
        return 0

    def greet_x(k, _):
        pl.semaphore_signal(
            barrier, inc=1, device_id=(lax.rem(g + k, GX), yy), device_id_type=MESH
        )
        return 0

    lax.fori_loop(1, GY, greet_y, 0)
    lax.fori_loop(1, GX, greet_x, 0)

    def send_y(st):
        for k in range(1, GY):
            d = lax.rem(yy + k, GY)
            pltpu.make_async_remote_copy(
                src_ref=sy.at[st, :, pl.ds(d * 32, 32), :],
                dst_ref=ry.at[st, :, pl.ds(yy * 32, 32), :],
                send_sem=sy_sem.at[st],
                recv_sem=ry_sem.at[st],
                device_id=(g, d),
                device_id_type=MESH,
            ).start()
        own = pl.ds(yy * 32, 32)
        pltpu.make_async_copy(
            sy.at[st, :, own, :], ry.at[st, :, own, :], ry_sem.at[st]
        ).start()

    def send_gx(src, dst, ssem, rsem, size):
        def body(k, _):
            d = lax.rem(g + k, GX)
            pltpu.make_async_remote_copy(
                src_ref=src.at[pl.ds(d * size, size)],
                dst_ref=dst.at[pl.ds(g * size, size)],
                send_sem=ssem,
                recv_sem=rsem,
                device_id=(d, yy),
                device_id_type=MESH,
            ).start()
            return 0

        lax.fori_loop(1, GX, body, 0)
        own = pl.ds(g * size, size)
        pltpu.make_async_copy(src.at[own], dst.at[own], rsem).start()

    def send_x(st):
        send_gx(sx.at[st], rx.at[st], sx_sem.at[st], rx_sem.at[st], 16)

    def send_p(st):
        send_gx(sp.at[st], rp.at[st], sp_sem.at[st], rp_sem.at[st], 1)

    def landed(ref, sem):
        pltpu.make_async_copy(ref, ref, sem).wait()

    lane = iota((64, 128), 1)

    def widen(c, _):
        rows = pl.ds(c * 128, 128)
        v = field[c].astype(F32).reshape(128, 256)
        fs[0, rows, :] = v[:, :128]
        fs[1, rows, :] = v[:, 128:]
        return 0

    lax.fori_loop(0, C, widen, 0)

    def rows_of(ref, y):
        rows = pl.ds(y, 160, stride=16)
        return jnp.concatenate([ref[0, rows, :], ref[1, rows, :]], axis=1)

    pad_rows = jnp.zeros((96, 256), BF16)

    def analyze_z(st, y, s):
        for r in range(2):
            rows = pl.ds(r * 16 + y, 8, stride=32)
            tail = None
            for kz in range(3):
                at = (kz * 2 + r) * 8
                sy[st, kz, rows, :] = s[at : at + 8, :128]
                piece = s[at : at + 8, 128:]
                tail = piece if kz == 0 else tail + pltpu.roll(piece, 32 * kz, 1)
            sy[st, 3, rows, :] = tail

    def synthesize_z(st, y):
        main, tail = [], []
        for kz in range(3):
            for r in range(2):
                rows = pl.ds(r * 16 + y, 8, stride=32)
                main.append(ry[st, kz, rows, :])
                piece = ry[st, 3, rows, :]
                tail.append(piece if kz == 0 else pltpu.roll(piece, 128 - 32 * kz, 1))
        data = jnp.concatenate(
            [jnp.concatenate(main, axis=0), jnp.concatenate(tail, axis=0)], axis=1
        )
        data = split(jnp.transpose(data)[:160])
        return dot3(data, (tz[0:48, :], tz[48:96, :]), NN)

    def first_y(y, _):
        f = jnp.concatenate([rows_of(fs, y).astype(BF16), pad_rows], axis=0)
        s = dot(tz[...], f, NT)
        analyze_z(0, y, s[0:48] + s[48:96])
        return 0

    lax.fori_loop(0, 16, first_y, 0)

    pl.semaphore_wait(barrier, GY - 1 + GX - 1)
    send_y(0)

    def widen_more(c, _):
        rows = pl.ds(c * 128, 128)
        v = cot[c].astype(F32).reshape(128, 256)
        cs[0, rows, :] = v[:, :128]
        cs[1, rows, :] = v[:, 128:]
        wf[c, :, 0:72] = w[c].astype(F32).reshape(120, 72)
        return 0

    wf[...] = jnp.zeros_like(wf)
    lax.fori_loop(0, C, widen_more, 0)

    pws[...] = jnp.zeros_like(pws)
    pws[0:20, 0:20] = pw[...].astype(F32)
    pws[32:33, 0:20] = bias[...]
    ones_e = iota((160, 128), 0) // 8 == iota((160, 128), 1)
    ones_e = jnp.where(ones_e, 1.0, 0.0)
    e = ones_e[:, :32].astype(BF16)
    same_x = lax.rem(iota((160, 160), 0), 8) == lax.rem(iota((160, 160), 1), 8)
    m = pws[0:32, 0:32].astype(BF16)
    t = dot(e, m, NT).astype(BF16)
    pw1[...] = jnp.where(same_x, dot(t, e, NT), 0.0).astype(BF16)
    t = dot(e, m, NN).astype(BF16)
    pw2[...] = jnp.where(same_x, dot(t, e, NT), 0.0).astype(BF16)
    column = jnp.sum(ones_e * pws[32:33, :], axis=1, keepdims=True)
    bb[...] = jnp.broadcast_to(column, (160, 128))

    def forward_y(st):
        for t in range(4):
            data = split(jnp.transpose(ry[st, t]))
            sx[st, pl.ds(t * 128, 128), :] = dot3(data, (yh[...], yl[...]), NN)

    def forward_x(st):
        p = dot3((axh[...], axl[...]), split(rx[st]), NN)
        pc, ps = p[:128], p[128:]
        side = iota((128, 128), 1) < 48
        o = pc + jnp.where(side, pltpu.roll(ps, 80, 1), -pltpu.roll(ps, 48, 1))
        sp[st] = o.reshape(32, 4, 128)

    def spectrum(st):
        tmp[...] = rp[st].reshape(128, 128)
        k0 = tmp[pl.ds(0, 64, stride=2), :]
        k1 = tmp[pl.ds(1, 64, stride=2), :]
        roll = lambda v, n: pltpu.roll(v, n, 1)
        re_e = jnp.where(lane < 48, k0, roll(k1, 48))
        im_e = jnp.where(lane < 48, roll(k0, 80), k1)
        re_o = jnp.where(lane < 24, roll(k0, 104), roll(k1, 24))
        im_o = jnp.where(lane < 24, roll(k0, 56), roll(k1, 104))
        live = lane < 72
        re = jnp.where(live, jnp.where(even, re_e, re_o), 0.0)
        im = jnp.where(live, jnp.where(even, im_e, im_o), 0.0)
        return re, im

    def modes(re, im, st):
        roll = lambda v, n: pltpu.roll(v, n, 1)
        within = lambda a, b: (lane >= a) & (lane < b)
        zero = jnp.zeros((64, 128), F32)
        e0 = jnp.where(lane < 48, re, jnp.where(within(48, 96), roll(im, 48), zero))
        e1 = jnp.where(lane < 24, roll(re, 80), jnp.where(within(48, 72), im, zero))
        o0 = jnp.where(
            within(24, 48), roll(re, 24), jnp.where(within(72, 96), roll(im, 72), zero)
        )
        o1 = jnp.where(lane < 48, roll(re, 104), jnp.where(within(48, 96), roll(im, 24), zero))
        tmp[pl.ds(0, 64, stride=2), :] = jnp.where(even, e0, o0)
        tmp[pl.ds(1, 64, stride=2), :] = jnp.where(even, e1, o1)
        sp[st] = tmp[...].reshape(32, 4, 128)

    def inverse_x(st):
        p = dot3((bxh[...], bxl[...]), split(rp[st].reshape(128, 128)), NN)
        pc, ps = p[:512], p[512:]
        side = iota((512, 128), 1) < 48
        sx[st] = pc + jnp.where(side, -pltpu.roll(ps, 80, 1), pltpu.roll(ps, 48, 1))

    def inverse_y(st):
        for t in range(4):
            data = split(rx[st, pl.ds(t * 128, 128), :])
            sy[st, t] = dot3((yh[...], yl[...]), data, NT)

    row64 = iota((64, 128), 0)
    zeroth = (row64 < 16) | ((row64 >= 48) & (row64 < 52))
    weight_z = jnp.where(zeroth & (yy == 0), 1.0 / CELLS, 2.0 / CELLS)

    landed(ry.at[0], ry_sem.at[0])
    forward_y(0)
    send_x(0)
    landed(rx.at[0], rx_sem.at[0])
    forward_x(0)
    send_p(0)
    landed(rp.at[0], rp_sem.at[0])
    re, im = spectrum(0)
    for kz in range(3):
        for o in range(4):
            for r in range(2):
                at = o * 6 + kz * 2 + r
                sign = 1.0 if r == 0 else -1.0
                most = pl.ds(at, 16, stride=24)
                rest = pl.ds(16 * 24 + at, 4, stride=24)
                u1[most, :] = re[kz * 16 : kz * 16 + 16]
                u1[rest, :] = re[48 + kz * 4 : 52 + kz * 4]
                u2[most, :] = sign * im[kz * 16 : kz * 16 + 16]
                u2[rest, :] = sign * im[48 + kz * 4 : 52 + kz * 4]

    real_row = lax.rem(iota((24, 128), 0), 2) == 0

    def mix(c, acc):
        a, b = acc
        rows = pl.ds(c * 24, 24)
        s1, s2 = u1[rows, :], u2[rows, :]
        sa = jnp.concatenate([jnp.where(real_row, s1, s2)] * 5, axis=0)
        sb = jnp.concatenate([jnp.where(real_row, s2, s1)] * 5, axis=0)
        return a + wf[c] * sa, b + wf[c] * sb

    zero = jnp.zeros((120, 128), F32)
    a, b = lax.fori_loop(0, C, mix, (zero, zero))
    modes(pick(sel_o[...], a) * weight_z, pick(sel_o[...], b) * weight_z, 1)
    send_p(1)
    landed(rp.at[1], rp_sem.at[1])
    inverse_x(1)
    send_x(1)
    landed(rx.at[1], rx_sem.at[1])
    inverse_y(1)
    send_y(1)
    landed(ry.at[1], ry_sem.at[1])

    lw[...] = jnp.zeros_like(lw)
    ones_rows = jnp.ones((16, 256), BF16)

    def middle(y, _):
        conv = synthesize_z(1, y)
        f = rows_of(fs, y).astype(BF16)
        v = dot(pw1[...], f, NN) + jnp.concatenate([bb[...], bb[...]], axis=1) + conv
        square = v * v
        t = jnp.tanh(GELU_A * v * (1.0 + GELU_B * square))
        half = 0.5 * (1.0 + t)
        act = v * half
        slope = half + (0.5 * GELU_A) * v * (1.0 - t * t) * (1.0 + (3.0 * GELU_B) * square)
        grad = rows_of(cs, y) * slope
        rows = pl.ds(y, 160, stride=16)
        fs[0, rows, :] = act[:, :128]
        fs[1, rows, :] = act[:, 128:]
        high, low = split(grad)
        gh[y] = high
        gl[y] = low
        f = jnp.concatenate([f, ones_rows], axis=0)
        lw[...] += dot(f, high, NT) + dot(f, low, NT)
        s = dot(tz[...], jnp.concatenate([high, pad_rows], axis=0), NT)
        s = s[0:48] + s[48:96]
        s = s + dot(tz[0:48, :], jnp.concatenate([low, pad_rows], axis=0), NT)
        analyze_z(2, y, s)
        return 0

    lax.fori_loop(0, 16, middle, 0)
    send_y(2)

    row, col = iota((176, 160), 0), iota((176, 160), 1)
    keep = (row >= 160) | (lax.rem(row, 8) == lax.rem(col, 8))
    total = jnp.where(keep, lw[...], 0.0)
    row, col = iota((32, 176), 0), iota((32, 176), 1)
    left = ((col < 160) & (col // 8 == row)) | ((row == 20) & (col == 160))
    left = jnp.where(left, 1.0, 0.0).astype(BF16)
    high, low = split(pick(left, total))
    e128 = ones_e.astype(BF16)
    ls[...] = dot(high, e128, NN) + dot(low, e128, NN)
    for k in range(1, GY):
        d = lax.rem(yy + k, GY)
        pltpu.make_async_remote_copy(
            src_ref=ls,
            dst_ref=lr.at[yy],
            send_sem=l_sem.at[0],
            recv_sem=l_sem.at[1],
            device_id=(g, d),
            device_id_type=MESH,
        ).start()
    pltpu.make_async_copy(ls, lr.at[yy], l_sem.at[1]).start()

    def write_out(c, _):
        rows = pl.ds(c * 128, 128)
        v = jnp.concatenate([fs[0, rows, :], fs[1, rows, :]], axis=1)
        out[c] = v.astype(BF16).reshape(8, 16, 256)
        return 0

    lax.fori_loop(0, C, write_out, 0)

    landed(ry.at[2], ry_sem.at[2])
    forward_y(2)
    send_x(2)

    landed(lr, l_sem.at[1])
    ms[...] = jnp.sum(lr[...], axis=0)

    def share(k, _):
        d = lax.rem(g + k, GX)
        pltpu.make_async_remote_copy(
            src_ref=ms,
            dst_ref=mr.at[g],
            send_sem=l_sem.at[2],
            recv_sem=l_sem.at[3],
            device_id=(d, yy),
            device_id_type=MESH,
        ).start()
        return 0

    lax.fori_loop(1, GX, share, 0)
    pltpu.make_async_copy(ms, mr.at[g], l_sem.at[3]).start()

    landed(rx.at[2], rx_sem.at[2])
    forward_x(2)
    send_p(2)
    landed(rp.at[2], rp_sem.at[2])
    re, im = spectrum(2)
    re, im = re * weight_z, im * weight_z
    for kz in range(3):
        for r in range(2):
            most = pl.ds(kz * 2 + r, 16, stride=6)
            rest = pl.ds(96 + kz * 2 + r, 4, stride=6)
            one, two = (re, im) if r == 0 else (im, re)
            d1[most, :] = one[kz * 16 : kz * 16 + 16]
            d1[rest, :] = one[48 + kz * 4 : 52 + kz * 4]
            d2[most, :] = two[kz * 16 : kz * 16 + 16]
            d2[rest, :] = two[48 + kz * 4 : 52 + kz * 4]

    even_row = lax.rem(iota((120, 128), 0), 2) == 0

    def unmix(c, _):
        rows = pl.ds(c * 24, 24)
        x1 = d1[...]
        x2 = jnp.where(even_row, d2[...], -d2[...])
        wc = wf[c]
        q1[rows, :] = jnp.sum((wc * x1).reshape(5, 24, 128), axis=0)
        q2[rows, :] = jnp.sum((wc * x2).reshape(5, 24, 128), axis=0)
        return 0

    lax.fori_loop(0, C, unmix, 0)
    modes(pick(sel_c[...], q1[...]), pick(sel_c[...], q2[...]), 3)
    send_p(3)

    def outer(c, _):
        rows = pl.ds(c * 24, 24)
        s1 = jnp.concatenate([u1[rows, :]] * 5, axis=0)
        s2 = jnp.concatenate([u2[rows, :]] * 5, axis=0)
        v = s1 * d1[...] + s2 * d2[...]
        gs[c] = v[:, 0:72].reshape(20, 3, 2, 72)
        return 0

    lax.fori_loop(0, C, outer, 0)

    landed(rp.at[3], rp_sem.at[3])
    inverse_x(3)
    send_x(3)
    landed(mr, l_sem.at[3])
    small[...] = jnp.sum(mr[...], axis=0) * (CELLS**-0.5)
    landed(rx.at[3], rx_sem.at[3])
    inverse_y(3)
    send_y(3)
    landed(ry.at[3], ry_sem.at[3])

    def last(y, _):
        back = dot(pw2[...], gh[y], NN) + dot(pw2[...], gl[y], NN) + synthesize_z(3, y)
        rows = pl.ds(y, 160, stride=16)
        cs[0, rows, :] = back[:, :128]
        cs[1, rows, :] = back[:, 128:]
        return 0

    lax.fori_loop(0, 16, last, 0)

    def write_grad(c, _):
        rows = pl.ds(c * 128, 128)
        v = jnp.concatenate([cs[0, rows, :], cs[1, rows, :]], axis=1)
        gf[c] = v.astype(BF16).reshape(8, 16, 256)
        return 0

    lax.fori_loop(0, C, write_grad, 0)

    for st in range(4):
        part = sy.at[st, :, pl.ds(0, 224), :]
        pltpu.make_async_copy(part, part, sy_sem.at[st]).wait()
        part = sx.at[st, pl.ds(0, 31 * 16)]
        pltpu.make_async_copy(part, part, sx_sem.at[st]).wait()
        part = sp.at[st, pl.ds(0, 31)]
        pltpu.make_async_copy(part, part, sp_sem.at[st]).wait()
    part = lr.at[pl.ds(0, 7)]
    pltpu.make_async_copy(part, part, l_sem.at[0]).wait()
    part = mr.at[pl.ds(0, 31)]
    pltpu.make_async_copy(part, part, l_sem.at[2]).wait()


def local(consts, field, cotangent, spectral_weight, pointwise_weight, bias):
    vmem = pl.BlockSpec(memory_space=pltpu.VMEM)
    dma = pltpu.SemaphoreType.DMA
    weights = jnp.transpose(spectral_weight, (1, 2, 3, 0, 4))
    scratch = [
        pltpu.VMEM((2, 2560, 128), F32),
        pltpu.VMEM((2, 2560, 128), F32),
        pltpu.VMEM((16, 160, 256), BF16),
        pltpu.VMEM((16, 160, 256), BF16),
        pltpu.VMEM((160, 160), BF16),
        pltpu.VMEM((160, 160), BF16),
        pltpu.VMEM((160, 128), F32),
        pltpu.VMEM((40, 128), F32),
        pltpu.VMEM((4, 4, 256, 128), F32),
        pltpu.VMEM((4, 4, 256, 128), F32),
        pltpu.VMEM((4, 512, 128), F32),
        pltpu.VMEM((4, 512, 128), F32),
        pltpu.VMEM((4, 32, 4, 128), F32),
        pltpu.VMEM((4, 32, 4, 128), F32),
        pltpu.VMEM((20, 120, 128), F32),
        pltpu.VMEM((128, 128), F32),
        pltpu.VMEM((480, 128), F32),
        pltpu.VMEM((480, 128), F32),
        pltpu.VMEM((120, 128), F32),
        pltpu.VMEM((120, 128), F32),
        pltpu.VMEM((480, 128), F32),
        pltpu.VMEM((480, 128), F32),
        pltpu.VMEM((176, 160), F32),
        pltpu.VMEM((32, 128), F32),
        pltpu.VMEM((8, 32, 128), F32),
        pltpu.VMEM((32, 128), F32),
        pltpu.VMEM((32, 32, 128), F32),
        dma((4,)), dma((4,)), dma((4,)), dma((4,)), dma((4,)), dma((4,)), dma((4,)),
    ]
    out, gf, gs, small = pl.pallas_call(
        kernel,
        out_shape=(
            jax.ShapeDtypeStruct((C, 8, 16, 256), BF16),
            jax.ShapeDtypeStruct((C, 8, 16, 256), BF16),
            jax.ShapeDtypeStruct((C, C, 3, 2, 72), F32),
            jax.ShapeDtypeStruct((32, 128), F32),
        ),
        in_specs=[vmem] * 14,
        out_specs=(vmem,) * 4,
        scratch_shapes=scratch,
        compiler_params=pltpu.CompilerParams(
            collective_id=0, has_side_effects=True, vmem_limit_bytes=58 << 20
        ),
        name="fourier_layer",
    )(field, cotangent, weights, pointwise_weight, bias.reshape(1, C), *consts)
    return (
        out,
        gf,
        jnp.transpose(gs, (3, 0, 1, 2, 4)),
        small[0:C, 0:C],
        small[C, 0:C],
    )


def solution(mesh):
    consts = [jnp.asarray(t) for t in tables()]
    placed = (
        P(None, "gx", "gy", None),
        P(None, "gx", "gy", None),
        P(None, None, None, "gy", "gx"),
        P(),
        P(),
    )
    return jax.shard_map(
        functools.partial(local, consts),
        mesh=mesh,
        in_specs=placed,
        out_specs=placed,
        check_vma=False,
    )
```

```python
import functools

import jax
import jax.numpy as jnp
import numpy as np
from jax import lax
from jax.experimental import pallas as pl
from jax.experimental.pallas import tpu as pltpu
from jax.sharding import PartitionSpec as P

C = 20
NX, NY, NZ = 256, 128, 256
KX, KY, KZ = 48, 48, 24
GX, GY = 32, 8
CELLS = float(NX * NY * NZ)
F32 = jnp.float32
BF16 = jnp.bfloat16
MESH = pl.DeviceIdType.MESH
NN = (((1,), (0,)), ((), ()))
NT = (((1,), (1,)), ((), ()))
GELU_A = float(np.sqrt(2.0 / np.pi))
GELU_B = 0.044715


def halves(table):
    high = table.astype(BF16)
    low = (table - np.asarray(high, np.float64)).astype(BF16)
    return np.asarray(high), np.asarray(low)


def tables():
    kz, r, d = np.meshgrid(np.arange(3), np.arange(2), np.arange(8), indexing="ij")
    depth = (d * 3 + kz).reshape(-1, 1) * np.arange(NZ)[None, :] % NZ * (2 * np.pi / NZ)
    tz = np.where(r.reshape(-1, 1) == 0, np.cos(depth), -np.sin(depth))
    tz = np.concatenate(halves(tz), axis=0)

    fx = np.where(np.arange(KX) < 24, np.arange(KX), np.arange(KX) - 48 + NX)
    fy = np.where(np.arange(KY) < 24, np.arange(KY), np.arange(KY) - 48 + NY)
    phase = np.arange(NY)[:, None] * fy[None, :] % NY * (2 * np.pi / NY)
    cos, sin = np.cos(phase).reshape(8, 16, KY), np.sin(phase).reshape(8, 16, KY)
    y = np.zeros((8, 2, 16, 128))
    y[:, 0, :, 0:48], y[:, 0, :, 48:96] = cos, -sin
    y[:, 1, :, 0:48], y[:, 1, :, 48:96] = sin, cos
    yh, yl = halves(y.reshape(256, 128))

    g = np.arange(GX)
    first = 3 * (g // 2) + g % 2
    kx = first[:, None] + np.arange(2)[None, :]
    phase = fx[kx][:, :, None] * np.arange(NX)[None, None, :] % NX * (2 * np.pi / NX)
    both = np.stack([np.cos(phase), np.sin(phase)])
    both = both.reshape(2, GX, 2, GX, 8)
    eye = np.eye(2)
    ax = np.einsum("egtsx,mn->egmtsnx", both, eye).reshape(256, 512)
    bx = np.einsum("egtsx,mn->esmxgnt", both, eye).reshape(1024, 128)
    axh, axl = halves(ax)
    bxh, bxl = halves(bx)

    m = np.arange(64)
    kz_m = np.where(m < 48, m // 16, (m - 48) // 4)
    c_m = np.where(m < 48, m % 16, 16 + (m - 48) % 4)
    row = np.arange(120)
    sel_o = (row[None, :] // 6 == c_m[:, None]) & (row[None, :] % 6 // 2 == kz_m[:, None])
    row = np.arange(480)
    sel_c = (row[None, :] // 24 == c_m[:, None]) & (row[None, :] % 6 // 2 == kz_m[:, None])
    live = (m < 60)[:, None]
    sel_o = np.asarray((sel_o & live).astype(BF16))
    sel_c = np.asarray((sel_c & live).astype(BF16))
    return tz, yh, yl, axh, axl, bxh, bxl, sel_o, sel_c


def hops(k):
    return min(k // 4, 8 - k // 4) + min(k % 4, 4 - k % 4)


def iota(shape, axis):
    return lax.broadcasted_iota(jnp.int32, shape, axis)


def dot(a, b, dims):
    return lax.dot_general(a, b, dims, preferred_element_type=F32)


def split(x):
    high = x.astype(BF16)
    return high, (x - high.astype(F32)).astype(BF16)


def dot3(a, b, dims):
    return dot(a[0], b[0], dims) + dot(a[0], b[1], dims) + dot(a[1], b[0], dims)


def pick(sel, x):
    high, low = split(x)
    return dot(sel, high, NN) + dot(sel, low, NN)


def kernel(
    field, cot, w, pw, bias, tz, yh, yl, axh, axl, bxh, bxl, sel_o, sel_c,
    out, gf, gs, small,
    fs, cs, gh, gl, pw1, pw2, bb, pws, sy, ry, sx, rx, sp, rp, wf, tmp,
    u1, u2, d1, d2, q1, q2, lw, ls, lr, ms, mr,
    sy_sem, ry_sem, sx_sem, rx_sem, sp_sem, rp_sem, l_sem,
):
    g = lax.axis_index("gx")
    yy = lax.axis_index("gy")
    even = lax.rem(g, 2) == 0

    barrier = pltpu.get_barrier_semaphore()

    def greet_y(k, _):
        pl.semaphore_signal(
            barrier, inc=1, device_id=(g, lax.rem(yy + k, GY)), device_id_type=MESH
        )
        return 0

    def greet_x(k, _):
        pl.semaphore_signal(
            barrier, inc=1, device_id=(lax.rem(g + k, GX), yy), device_id_type=MESH
        )
        return 0

    lax.fori_loop(1, GY, greet_y, 0)
    lax.fori_loop(1, GX, greet_x, 0)

    def send_y(st):
        for k in range(1, GY):
            d = lax.rem(yy + k, GY)
            pltpu.make_async_remote_copy(
                src_ref=sy.at[st, :, pl.ds(d * 32, 32), :],
                dst_ref=ry.at[st, :, pl.ds(yy * 32, 32), :],
                send_sem=sy_sem.at[st],
                recv_sem=ry_sem.at[st],
                device_id=(g, d),
                device_id_type=MESH,
            ).start()
        own = pl.ds(yy * 32, 32)
        pltpu.make_async_copy(
            sy.at[st, :, own, :], ry.at[st, :, own, :], ry_sem.at[st]
        ).start()

    gz, gw = g // 4, lax.rem(g, 4)
    far_first = sorted(range(1, GX), key=hops, reverse=True)

    def send_gx(src, dst, ssem, rsem, size):
        for k in far_first:
            d = lax.rem(gz + k // 4, 8) * 4 + lax.rem(gw + k % 4, 4)
            pltpu.make_async_remote_copy(
                src_ref=src.at[pl.ds(d * size, size)],
                dst_ref=dst.at[pl.ds(g * size, size)],
                send_sem=ssem,
                recv_sem=rsem,
                device_id=(d, yy),
                device_id_type=MESH,
            ).start()
        own = pl.ds(g * size, size)
        pltpu.make_async_copy(src.at[own], dst.at[own], rsem).start()

    def send_x(st):
        send_gx(sx.at[st], rx.at[st], sx_sem.at[st], rx_sem.at[st], 16)

    def send_p(st):
        send_gx(sp.at[st], rp.at[st], sp_sem.at[st], rp_sem.at[st], 1)

    def landed(ref, sem):
        pltpu.make_async_copy(ref, ref, sem).wait()

    lane = iota((64, 128), 1)

    def widen(c, _):
        rows = pl.ds(c * 128, 128)
        v = field[c].astype(F32).reshape(128, 256)
        fs[0, rows, :] = v[:, :128]
        fs[1, rows, :] = v[:, 128:]
        return 0

    lax.fori_loop(0, C, widen, 0, unroll=4)

    def rows_of(ref, y):
        rows = pl.ds(y, 160, stride=16)
        return jnp.concatenate([ref[0, rows, :], ref[1, rows, :]], axis=1)

    pad_rows = jnp.zeros((96, 256), BF16)

    def analyze_z(st, y, s):
        for r in range(2):
            rows = pl.ds(r * 16 + y, 8, stride=32)
            tail = None
            for kz in range(3):
                at = (kz * 2 + r) * 8
                sy[st, kz, rows, :] = s[at : at + 8, :128]
                piece = s[at : at + 8, 128:]
                tail = piece if kz == 0 else tail + pltpu.roll(piece, 32 * kz, 1)
            sy[st, 3, rows, :] = tail

    def synthesize_z(st, y):
        main, tail = [], []
        for kz in range(3):
            for r in range(2):
                rows = pl.ds(r * 16 + y, 8, stride=32)
                main.append(ry[st, kz, rows, :])
                piece = ry[st, 3, rows, :]
                tail.append(piece if kz == 0 else pltpu.roll(piece, 128 - 32 * kz, 1))
        data = jnp.concatenate(
            [jnp.concatenate(main, axis=0), jnp.concatenate(tail, axis=0)], axis=1
        )
        data = split(jnp.transpose(data)[:160])
        return dot3(data, (tz[0:48, :], tz[48:96, :]), NN)

    def first_y(y, _):
        f = jnp.concatenate([rows_of(fs, y).astype(BF16), pad_rows], axis=0)
        s = dot(tz[...], f, NT)
        analyze_z(0, y, s[0:48] + s[48:96])
        return 0

    lax.fori_loop(0, 16, first_y, 0, unroll=4)

    pl.semaphore_wait(barrier, GY - 1 + GX - 1)
    send_y(0)

    def widen_more(c, _):
        rows = pl.ds(c * 128, 128)
        v = cot[c].astype(F32).reshape(128, 256)
        cs[0, rows, :] = v[:, :128]
        cs[1, rows, :] = v[:, 128:]
        wf[c, :, 0:72] = w[c].astype(F32).reshape(120, 72)
        return 0

    wf[...] = jnp.zeros_like(wf)
    lax.fori_loop(0, C, widen_more, 0, unroll=4)

    pws[...] = jnp.zeros_like(pws)
    pws[0:20, 0:20] = pw[...].astype(F32)
    pws[32:33, 0:20] = bias[...]
    ones_e = iota((160, 128), 0) // 8 == iota((160, 128), 1)
    ones_e = jnp.where(ones_e, 1.0, 0.0)
    e = ones_e[:, :32].astype(BF16)
    same_x = lax.rem(iota((160, 160), 0), 8) == lax.rem(iota((160, 160), 1), 8)
    m = pws[0:32, 0:32].astype(BF16)
    t = dot(e, m, NT).astype(BF16)
    pw1[...] = jnp.where(same_x, dot(t, e, NT), 0.0).astype(BF16)
    t = dot(e, m, NN).astype(BF16)
    pw2[...] = jnp.where(same_x, dot(t, e, NT), 0.0).astype(BF16)
    column = jnp.sum(ones_e * pws[32:33, :], axis=1, keepdims=True)
    bb[...] = jnp.broadcast_to(column, (160, 128))

    def forward_y(st):
        for t in range(4):
            data = split(jnp.transpose(ry[st, t]))
            sx[st, pl.ds(t * 128, 128), :] = dot3(data, (yh[...], yl[...]), NN)

    def forward_x(st):
        p = dot3((axh[...], axl[...]), split(rx[st]), NN)
        pc, ps = p[:128], p[128:]
        side = iota((128, 128), 1) < 48
        o = pc + jnp.where(side, pltpu.roll(ps, 80, 1), -pltpu.roll(ps, 48, 1))
        sp[st] = o.reshape(32, 4, 128)

    def spectrum(st):
        tmp[...] = rp[st].reshape(128, 128)
        k0 = tmp[pl.ds(0, 64, stride=2), :]
        k1 = tmp[pl.ds(1, 64, stride=2), :]
        roll = lambda v, n: pltpu.roll(v, n, 1)
        re_e = jnp.where(lane < 48, k0, roll(k1, 48))
        im_e = jnp.where(lane < 48, roll(k0, 80), k1)
        re_o = jnp.where(lane < 24, roll(k0, 104), roll(k1, 24))
        im_o = jnp.where(lane < 24, roll(k0, 56), roll(k1, 104))
        live = lane < 72
        re = jnp.where(live, jnp.where(even, re_e, re_o), 0.0)
        im = jnp.where(live, jnp.where(even, im_e, im_o), 0.0)
        return re, im

    def modes(re, im, st):
        roll = lambda v, n: pltpu.roll(v, n, 1)
        within = lambda a, b: (lane >= a) & (lane < b)
        zero = jnp.zeros((64, 128), F32)
        e0 = jnp.where(lane < 48, re, jnp.where(within(48, 96), roll(im, 48), zero))
        e1 = jnp.where(lane < 24, roll(re, 80), jnp.where(within(48, 72), im, zero))
        o0 = jnp.where(
            within(24, 48), roll(re, 24), jnp.where(within(72, 96), roll(im, 72), zero)
        )
        o1 = jnp.where(lane < 48, roll(re, 104), jnp.where(within(48, 96), roll(im, 24), zero))
        tmp[pl.ds(0, 64, stride=2), :] = jnp.where(even, e0, o0)
        tmp[pl.ds(1, 64, stride=2), :] = jnp.where(even, e1, o1)
        sp[st] = tmp[...].reshape(32, 4, 128)

    def inverse_x(st):
        p = dot3((bxh[...], bxl[...]), split(rp[st].reshape(128, 128)), NN)
        pc, ps = p[:512], p[512:]
        side = iota((512, 128), 1) < 48
        sx[st] = pc + jnp.where(side, -pltpu.roll(ps, 80, 1), pltpu.roll(ps, 48, 1))

    def inverse_y(st):
        for t in range(4):
            data = split(rx[st, pl.ds(t * 128, 128), :])
            sy[st, t] = dot3((yh[...], yl[...]), data, NT)

    row64 = iota((64, 128), 0)
    zeroth = (row64 < 16) | ((row64 >= 48) & (row64 < 52))
    weight_z = jnp.where(zeroth & (yy == 0), 1.0 / CELLS, 2.0 / CELLS)

    landed(ry.at[0], ry_sem.at[0])
    forward_y(0)
    send_x(0)
    landed(rx.at[0], rx_sem.at[0])
    forward_x(0)
    send_p(0)
    landed(rp.at[0], rp_sem.at[0])
    re, im = spectrum(0)
    for kz in range(3):
        for o in range(4):
            for r in range(2):
                at = o * 6 + kz * 2 + r
                sign = 1.0 if r == 0 else -1.0
                most = pl.ds(at, 16, stride=24)
                rest = pl.ds(16 * 24 + at, 4, stride=24)
                u1[most, :] = re[kz * 16 : kz * 16 + 16]
                u1[rest, :] = re[48 + kz * 4 : 52 + kz * 4]
                u2[most, :] = sign * im[kz * 16 : kz * 16 + 16]
                u2[rest, :] = sign * im[48 + kz * 4 : 52 + kz * 4]

    real_row = lax.rem(iota((24, 128), 0), 2) == 0

    def mix(c, acc):
        a, b = acc
        rows = pl.ds(c * 24, 24)
        s1, s2 = u1[rows, :], u2[rows, :]
        sa = jnp.concatenate([jnp.where(real_row, s1, s2)] * 5, axis=0)
        sb = jnp.concatenate([jnp.where(real_row, s2, s1)] * 5, axis=0)
        return a + wf[c] * sa, b + wf[c] * sb

    zero = jnp.zeros((120, 128), F32)
    a, b = lax.fori_loop(0, C, mix, (zero, zero))
    modes(pick(sel_o[...], a) * weight_z, pick(sel_o[...], b) * weight_z, 1)
    send_p(1)
    landed(rp.at[1], rp_sem.at[1])
    inverse_x(1)
    send_x(1)
    landed(rx.at[1], rx_sem.at[1])
    inverse_y(1)
    send_y(1)
    landed(ry.at[1], ry_sem.at[1])

    lw[...] = jnp.zeros_like(lw)
    ones_rows = jnp.ones((16, 256), BF16)

    def middle(y, _):
        conv = synthesize_z(1, y)
        f = rows_of(fs, y).astype(BF16)
        v = dot(pw1[...], f, NN) + jnp.concatenate([bb[...], bb[...]], axis=1) + conv
        square = v * v
        t = jnp.tanh(GELU_A * v * (1.0 + GELU_B * square))
        half = 0.5 * (1.0 + t)
        act = v * half
        slope = half + (0.5 * GELU_A) * v * (1.0 - t * t) * (1.0 + (3.0 * GELU_B) * square)
        grad = rows_of(cs, y) * slope
        rows = pl.ds(y, 160, stride=16)
        fs[0, rows, :] = act[:, :128]
        fs[1, rows, :] = act[:, 128:]
        high, low = split(grad)
        gh[y] = high
        gl[y] = low
        f = jnp.concatenate([f, ones_rows], axis=0)
        lw[...] += dot(f, high, NT) + dot(f, low, NT)
        s = dot(tz[...], jnp.concatenate([high, pad_rows], axis=0), NT)
        s = s[0:48] + s[48:96]
        s = s + dot(tz[0:48, :], jnp.concatenate([low, pad_rows], axis=0), NT)
        analyze_z(2, y, s)
        return 0

    lax.fori_loop(0, 16, middle, 0, unroll=4)
    send_y(2)

    row, col = iota((176, 160), 0), iota((176, 160), 1)
    keep = (row >= 160) | (lax.rem(row, 8) == lax.rem(col, 8))
    total = jnp.where(keep, lw[...], 0.0)
    row, col = iota((32, 176), 0), iota((32, 176), 1)
    left = ((col < 160) & (col // 8 == row)) | ((row == 20) & (col == 160))
    left = jnp.where(left, 1.0, 0.0).astype(BF16)
    high, low = split(pick(left, total))
    e128 = ones_e.astype(BF16)
    ls[...] = dot(high, e128, NN) + dot(low, e128, NN)
    for k in range(1, GY):
        d = lax.rem(yy + k, GY)
        pltpu.make_async_remote_copy(
            src_ref=ls,
            dst_ref=lr.at[yy],
            send_sem=l_sem.at[0],
            recv_sem=l_sem.at[1],
            device_id=(g, d),
            device_id_type=MESH,
        ).start()
    pltpu.make_async_copy(ls, lr.at[yy], l_sem.at[1]).start()

    def write_out(c, _):
        rows = pl.ds(c * 128, 128)
        v = jnp.concatenate([fs[0, rows, :], fs[1, rows, :]], axis=1)
        out[c] = v.astype(BF16).reshape(8, 16, 256)
        return 0

    lax.fori_loop(0, C, write_out, 0, unroll=4)

    landed(ry.at[2], ry_sem.at[2])
    forward_y(2)
    send_x(2)

    landed(lr, l_sem.at[1])
    ms[...] = jnp.sum(lr[...], axis=0)

    def share(k, _):
        d = lax.rem(g + k, GX)
        pltpu.make_async_remote_copy(
            src_ref=ms,
            dst_ref=mr.at[g],
            send_sem=l_sem.at[2],
            recv_sem=l_sem.at[3],
            device_id=(d, yy),
            device_id_type=MESH,
        ).start()
        return 0

    lax.fori_loop(1, GX, share, 0)
    pltpu.make_async_copy(ms, mr.at[g], l_sem.at[3]).start()

    landed(rx.at[2], rx_sem.at[2])
    forward_x(2)
    send_p(2)
    landed(rp.at[2], rp_sem.at[2])
    re, im = spectrum(2)
    re, im = re * weight_z, im * weight_z
    for kz in range(3):
        for r in range(2):
            most = pl.ds(kz * 2 + r, 16, stride=6)
            rest = pl.ds(96 + kz * 2 + r, 4, stride=6)
            one, two = (re, im) if r == 0 else (im, re)
            d1[most, :] = one[kz * 16 : kz * 16 + 16]
            d1[rest, :] = one[48 + kz * 4 : 52 + kz * 4]
            d2[most, :] = two[kz * 16 : kz * 16 + 16]
            d2[rest, :] = two[48 + kz * 4 : 52 + kz * 4]

    even_row = lax.rem(iota((120, 128), 0), 2) == 0

    def unmix(c, _):
        rows = pl.ds(c * 24, 24)
        x1 = d1[...]
        x2 = jnp.where(even_row, d2[...], -d2[...])
        wc = wf[c]
        q1[rows, :] = jnp.sum((wc * x1).reshape(5, 24, 128), axis=0)
        q2[rows, :] = jnp.sum((wc * x2).reshape(5, 24, 128), axis=0)
        return 0

    lax.fori_loop(0, C, unmix, 0, unroll=2)
    modes(pick(sel_c[...], q1[...]), pick(sel_c[...], q2[...]), 3)
    send_p(3)

    def outer(c, _):
        rows = pl.ds(c * 24, 24)
        s1 = jnp.concatenate([u1[rows, :]] * 5, axis=0)
        s2 = jnp.concatenate([u2[rows, :]] * 5, axis=0)
        v = s1 * d1[...] + s2 * d2[...]
        gs[c] = v[:, 0:72].reshape(20, 3, 2, 72)
        return 0

    lax.fori_loop(0, C, outer, 0, unroll=2)

    landed(rp.at[3], rp_sem.at[3])
    inverse_x(3)
    send_x(3)
    landed(mr, l_sem.at[3])
    small[...] = jnp.sum(mr[...], axis=0) * (CELLS**-0.5)
    landed(rx.at[3], rx_sem.at[3])
    inverse_y(3)
    send_y(3)
    landed(ry.at[3], ry_sem.at[3])

    def last(y, _):
        back = dot(pw2[...], gh[y], NN) + dot(pw2[...], gl[y], NN) + synthesize_z(3, y)
        rows = pl.ds(y, 160, stride=16)
        cs[0, rows, :] = back[:, :128]
        cs[1, rows, :] = back[:, 128:]
        return 0

    lax.fori_loop(0, 16, last, 0, unroll=4)

    def write_grad(c, _):
        rows = pl.ds(c * 128, 128)
        v = jnp.concatenate([cs[0, rows, :], cs[1, rows, :]], axis=1)
        gf[c] = v.astype(BF16).reshape(8, 16, 256)
        return 0

    lax.fori_loop(0, C, write_grad, 0, unroll=4)

    for st in range(4):
        part = sy.at[st, :, pl.ds(0, 224), :]
        pltpu.make_async_copy(part, part, sy_sem.at[st]).wait()
        part = sx.at[st, pl.ds(0, 31 * 16)]
        pltpu.make_async_copy(part, part, sx_sem.at[st]).wait()
        part = sp.at[st, pl.ds(0, 31)]
        pltpu.make_async_copy(part, part, sp_sem.at[st]).wait()
    part = lr.at[pl.ds(0, 7)]
    pltpu.make_async_copy(part, part, l_sem.at[0]).wait()
    part = mr.at[pl.ds(0, 31)]
    pltpu.make_async_copy(part, part, l_sem.at[2]).wait()


def local(consts, field, cotangent, spectral_weight, pointwise_weight, bias):
    vmem = pl.BlockSpec(memory_space=pltpu.VMEM)
    dma = pltpu.SemaphoreType.DMA
    weights = jnp.transpose(spectral_weight, (1, 2, 3, 0, 4))
    scratch = [
        pltpu.VMEM((2, 2560, 128), F32),
        pltpu.VMEM((2, 2560, 128), F32),
        pltpu.VMEM((16, 160, 256), BF16),
        pltpu.VMEM((16, 160, 256), BF16),
        pltpu.VMEM((160, 160), BF16),
        pltpu.VMEM((160, 160), BF16),
        pltpu.VMEM((160, 128), F32),
        pltpu.VMEM((40, 128), F32),
        pltpu.VMEM((4, 4, 256, 128), F32),
        pltpu.VMEM((4, 4, 256, 128), F32),
        pltpu.VMEM((4, 512, 128), F32),
        pltpu.VMEM((4, 512, 128), F32),
        pltpu.VMEM((4, 32, 4, 128), F32),
        pltpu.VMEM((4, 32, 4, 128), F32),
        pltpu.VMEM((20, 120, 128), F32),
        pltpu.VMEM((128, 128), F32),
        pltpu.VMEM((480, 128), F32),
        pltpu.VMEM((480, 128), F32),
        pltpu.VMEM((120, 128), F32),
        pltpu.VMEM((120, 128), F32),
        pltpu.VMEM((480, 128), F32),
        pltpu.VMEM((480, 128), F32),
        pltpu.VMEM((176, 160), F32),
        pltpu.VMEM((32, 128), F32),
        pltpu.VMEM((8, 32, 128), F32),
        pltpu.VMEM((32, 128), F32),
        pltpu.VMEM((32, 32, 128), F32),
        dma((4,)), dma((4,)), dma((4,)), dma((4,)), dma((4,)), dma((4,)), dma((4,)),
    ]
    out, gf, gs, small = pl.pallas_call(
        kernel,
        out_shape=(
            jax.ShapeDtypeStruct((C, 8, 16, 256), BF16),
            jax.ShapeDtypeStruct((C, 8, 16, 256), BF16),
            jax.ShapeDtypeStruct((C, C, 3, 2, 72), F32),
            jax.ShapeDtypeStruct((32, 128), F32),
        ),
        in_specs=[vmem] * 14,
        out_specs=(vmem,) * 4,
        scratch_shapes=scratch,
        compiler_params=pltpu.CompilerParams(
            collective_id=0, has_side_effects=True, vmem_limit_bytes=58 << 20
        ),
        name="fourier_layer",
    )(field, cotangent, weights, pointwise_weight, bias.reshape(1, C), *consts)
    return (
        out,
        gf,
        jnp.transpose(gs, (3, 0, 1, 2, 4)),
        small[0:C, 0:C],
        small[C, 0:C],
    )


def solution(mesh):
    consts = [jnp.asarray(t) for t in tables()]
    placed = (
        P(None, "gx", "gy", None),
        P(None, "gx", "gy", None),
        P(None, None, None, "gy", "gx"),
        P(),
        P(),
    )
    return jax.shard_map(
        functools.partial(local, consts),
        mesh=mesh,
        in_specs=placed,
        out_specs=placed,
        check_vma=False,
    )
```

```python
import functools

import jax
import jax.numpy as jnp
import numpy as np
from jax import lax
from jax.experimental import pallas as pl
from jax.experimental.pallas import tpu as pltpu
from jax.sharding import PartitionSpec as P

C = 20
NX, NY, NZ = 256, 128, 256
KX, KY, KZ = 48, 48, 24
GX, GY = 32, 8
CELLS = float(NX * NY * NZ)
F32 = jnp.float32
BF16 = jnp.bfloat16
MESH = pl.DeviceIdType.MESH
NN = (((1,), (0,)), ((), ()))
NT = (((1,), (1,)), ((), ()))
GELU_A = float(np.sqrt(2.0 / np.pi))
GELU_B = 0.044715


def halves(table):
    high = table.astype(BF16)
    low = (table - np.asarray(high, np.float64)).astype(BF16)
    return np.asarray(high), np.asarray(low)


def tables():
    kz, r, d = np.meshgrid(np.arange(3), np.arange(2), np.arange(8), indexing="ij")
    depth = (d * 3 + kz).reshape(-1, 1) * np.arange(NZ)[None, :] % NZ * (2 * np.pi / NZ)
    tz = np.where(r.reshape(-1, 1) == 0, np.cos(depth), -np.sin(depth))
    tz = np.concatenate(halves(tz), axis=0)

    fx = np.where(np.arange(KX) < 24, np.arange(KX), np.arange(KX) - 48 + NX)
    fy = np.where(np.arange(KY) < 24, np.arange(KY), np.arange(KY) - 48 + NY)
    phase = np.arange(NY)[:, None] * fy[None, :] % NY * (2 * np.pi / NY)
    cos, sin = np.cos(phase).reshape(8, 16, KY), np.sin(phase).reshape(8, 16, KY)
    y = np.zeros((8, 2, 16, 128))
    y[:, 0, :, 0:48], y[:, 0, :, 48:96] = cos, -sin
    y[:, 1, :, 0:48], y[:, 1, :, 48:96] = sin, cos
    y = y.reshape(8, 2, 2, 8, 128).transpose(0, 2, 1, 3, 4)
    yh, yl = halves(y.reshape(256, 128))

    g = np.arange(GX)
    first = 3 * (g // 2) + g % 2
    kx = first[:, None] + np.arange(2)[None, :]
    phase = fx[kx][:, :, None] * np.arange(NX)[None, None, :] % NX * (2 * np.pi / NX)
    both = np.stack([np.cos(phase), np.sin(phase)])
    both = both.reshape(2, GX, 2, GX, 8)
    eye = np.eye(2)
    ax = np.einsum("egtsx,mn->egmtsnx", both, eye).reshape(256, 512)
    bx = np.einsum("egtsx,mn->esmxgnt", both, eye).reshape(1024, 128)
    axh, axl = halves(ax)
    bxh, bxl = halves(bx)

    m = np.arange(64)
    kz_m = np.where(m < 48, m // 16, (m - 48) // 4)
    c_m = np.where(m < 48, m % 16, 16 + (m - 48) % 4)
    row = np.arange(120)
    sel_o = (row[None, :] // 6 == c_m[:, None]) & (row[None, :] % 6 // 2 == kz_m[:, None])
    row = np.arange(480)
    sel_c = (row[None, :] // 24 == c_m[:, None]) & (row[None, :] % 6 // 2 == kz_m[:, None])
    live = (m < 60)[:, None]
    sel_o = np.asarray((sel_o & live).astype(BF16))
    sel_c = np.asarray((sel_c & live).astype(BF16))
    return tz, yh, yl, axh, axl, bxh, bxl, sel_o, sel_c


def hops(k):
    return min(k // 4, 8 - k // 4) + min(k % 4, 4 - k % 4)


def iota(shape, axis):
    return lax.broadcasted_iota(jnp.int32, shape, axis)


def dot(a, b, dims):
    return lax.dot_general(a, b, dims, preferred_element_type=F32)


def split(x):
    high = x.astype(BF16)
    return high, (x - high.astype(F32)).astype(BF16)


def dot3(a, b, dims):
    return dot(a[0], b[0], dims) + dot(a[0], b[1], dims) + dot(a[1], b[0], dims)


def pick(sel, x):
    high, low = split(x)
    return dot(sel, high, NN) + dot(sel, low, NN)


def kernel(
    field, cot, w, pw, bias, tz, yh, yl, axh, axl, bxh, bxl, sel_o, sel_c,
    out, gf, gs, small,
    fs, cs, gh, gl, pw1, pw2, bb, pws, sy, ry, sx, rx, sp, rp, wf, tmp,
    u1, u2, d1, d2, q1, q2, lw, ls, lr, ms, mr, out_v, gf_v, gs_v,
    sy_sem, ry_sem, sx_sem, rx_sem, sp_sem, rp_sem, l_sem, o_sem,
):
    g = lax.axis_index("gx")
    yy = lax.axis_index("gy")
    even = lax.rem(g, 2) == 0

    barrier = pltpu.get_barrier_semaphore()

    def greet_y(k, _):
        pl.semaphore_signal(
            barrier, inc=1, device_id=(g, lax.rem(yy + k, GY)), device_id_type=MESH
        )
        return 0

    def greet_x(k, _):
        pl.semaphore_signal(
            barrier, inc=1, device_id=(lax.rem(g + k, GX), yy), device_id_type=MESH
        )
        return 0

    lax.fori_loop(1, GY, greet_y, 0)
    lax.fori_loop(1, GX, greet_x, 0)

    chip, core = yy // 2, lax.rem(yy, 2)
    others_y = [
        lax.rem(chip + n, 4) * 2 + (core if same else 1 - core)
        for n, same in ((2, 1), (2, 0), (1, 1), (3, 1), (1, 0), (3, 0), (0, 0))
    ]

    def send_y(st, h):
        sem_s, sem_r = sy_sem.at[2 * st + h], ry_sem.at[2 * st + h]
        own = pl.ds(yy * 32 + h * 16, 16)
        for d in others_y:
            pltpu.make_async_remote_copy(
                src_ref=sy.at[st, :, pl.ds(d * 32 + h * 16, 16), :],
                dst_ref=ry.at[st, :, own, :],
                send_sem=sem_s,
                recv_sem=sem_r,
                device_id=(g, d),
                device_id_type=MESH,
            ).start()
        pltpu.make_async_copy(sy.at[st, :, own, :], ry.at[st, :, own, :], sem_r).start()

    def landed_y(st, h):
        landed(ry.at[st, :, pl.ds(0, 128), :], ry_sem.at[2 * st + h])

    gz, gw = g // 4, lax.rem(g, 4)
    far_first = sorted(range(1, GX), key=hops, reverse=True)

    def send_gx(src, dst, ssem, rsem, size):
        for k in far_first:
            d = lax.rem(gz + k // 4, 8) * 4 + lax.rem(gw + k % 4, 4)
            pltpu.make_async_remote_copy(
                src_ref=src.at[pl.ds(d * size, size)],
                dst_ref=dst.at[pl.ds(g * size, size)],
                send_sem=ssem,
                recv_sem=rsem,
                device_id=(d, yy),
                device_id_type=MESH,
            ).start()
        own = pl.ds(g * size, size)
        pltpu.make_async_copy(src.at[own], dst.at[own], rsem).start()

    def send_x(st):
        send_gx(sx.at[st], rx.at[st], sx_sem.at[st], rx_sem.at[st], 16)

    def send_p(st):
        send_gx(sp.at[st], rp.at[st], sp_sem.at[st], rp_sem.at[st], 1)

    def landed(ref, sem):
        pltpu.make_async_copy(ref, ref, sem).wait()

    lane = iota((64, 128), 1)

    def widen(c, _):
        rows = pl.ds(c * 128, 128)
        v = field[c].astype(F32).reshape(128, 256)
        fs[0, rows, :] = v[:, :128]
        fs[1, rows, :] = v[:, 128:]
        return 0

    lax.fori_loop(0, C, widen, 0, unroll=4)

    def rows_of(ref, y):
        rows = pl.ds(y, 160, stride=16)
        return jnp.concatenate([ref[0, rows, :], ref[1, rows, :]], axis=1)

    pad_rows = jnp.zeros((96, 256), BF16)

    def analyze_z(st, h, y, s):
        for r in range(2):
            rows = pl.ds(h * 16 + r * 8 + y, 8, stride=32)
            tail = None
            for kz in range(3):
                at = (kz * 2 + r) * 8
                sy[st, kz, rows, :] = s[at : at + 8, :128]
                piece = s[at : at + 8, 128:]
                tail = piece if kz == 0 else tail + pltpu.roll(piece, 32 * kz, 1)
            sy[st, 3, rows, :] = tail

    def synthesize_z(st, h, y):
        main, tail = [], []
        for kz in range(3):
            for r in range(2):
                rows = pl.ds(h * 16 + r * 8 + y, 8, stride=32)
                main.append(ry[st, kz, rows, :])
                piece = ry[st, 3, rows, :]
                tail.append(piece if kz == 0 else pltpu.roll(piece, 128 - 32 * kz, 1))
        data = jnp.concatenate(
            [jnp.concatenate(main, axis=0), jnp.concatenate(tail, axis=0)], axis=1
        )
        data = split(jnp.transpose(data)[:160])
        return dot3(data, (tz[0:48, :], tz[48:96, :]), NN)

    def first_y(h, y, _):
        f = jnp.concatenate([rows_of(fs, h * 8 + y).astype(BF16), pad_rows], axis=0)
        s = dot(tz[...], f, NT)
        analyze_z(0, h, y, s[0:48] + s[48:96])
        return 0

    for h in range(2):
        lax.fori_loop(0, 8, functools.partial(first_y, h), 0, unroll=4)

    pl.semaphore_wait(barrier, GY - 1 + GX - 1)
    send_y(0, 0)
    send_y(0, 1)

    def widen_more(c, _):
        rows = pl.ds(c * 128, 128)
        v = cot[c].astype(F32).reshape(128, 256)
        cs[0, rows, :] = v[:, :128]
        cs[1, rows, :] = v[:, 128:]
        wf[c, :, 0:72] = w[c].astype(F32).reshape(120, 72)
        return 0

    wf[...] = jnp.zeros_like(wf)
    lax.fori_loop(0, C, widen_more, 0, unroll=4)

    pws[...] = jnp.zeros_like(pws)
    pws[0:20, 0:20] = pw[...].astype(F32)
    pws[32:33, 0:20] = bias[...]
    ones_e = iota((160, 128), 0) // 8 == iota((160, 128), 1)
    ones_e = jnp.where(ones_e, 1.0, 0.0)
    e = ones_e[:, :32].astype(BF16)
    same_x = lax.rem(iota((160, 160), 0), 8) == lax.rem(iota((160, 160), 1), 8)
    m = pws[0:32, 0:32].astype(BF16)
    t = dot(e, m, NT).astype(BF16)
    pw1[...] = jnp.where(same_x, dot(t, e, NT), 0.0).astype(BF16)
    t = dot(e, m, NN).astype(BF16)
    pw2[...] = jnp.where(same_x, dot(t, e, NT), 0.0).astype(BF16)
    column = jnp.sum(ones_e * pws[32:33, :], axis=1, keepdims=True)
    bb[...] = jnp.broadcast_to(column, (160, 128))

    def forward_y(st):
        for t in range(4):
            data = split(jnp.transpose(ry[st, t]))
            sx[st, pl.ds(t * 128, 128), :] = dot3(data, (yh[...], yl[...]), NN)

    def forward_x(st):
        p = dot3((axh[...], axl[...]), split(rx[st]), NN)
        pc, ps = p[:128], p[128:]
        side = iota((128, 128), 1) < 48
        o = pc + jnp.where(side, pltpu.roll(ps, 80, 1), -pltpu.roll(ps, 48, 1))
        sp[st] = o.reshape(32, 4, 128)

    def spectrum(st):
        tmp[...] = rp[st].reshape(128, 128)
        k0 = tmp[pl.ds(0, 64, stride=2), :]
        k1 = tmp[pl.ds(1, 64, stride=2), :]
        roll = lambda v, n: pltpu.roll(v, n, 1)
        re_e = jnp.where(lane < 48, k0, roll(k1, 48))
        im_e = jnp.where(lane < 48, roll(k0, 80), k1)
        re_o = jnp.where(lane < 24, roll(k0, 104), roll(k1, 24))
        im_o = jnp.where(lane < 24, roll(k0, 56), roll(k1, 104))
        live = lane < 72
        re = jnp.where(live, jnp.where(even, re_e, re_o), 0.0)
        im = jnp.where(live, jnp.where(even, im_e, im_o), 0.0)
        return re, im

    def modes(re, im, st):
        roll = lambda v, n: pltpu.roll(v, n, 1)
        within = lambda a, b: (lane >= a) & (lane < b)
        zero = jnp.zeros((64, 128), F32)
        e0 = jnp.where(lane < 48, re, jnp.where(within(48, 96), roll(im, 48), zero))
        e1 = jnp.where(lane < 24, roll(re, 80), jnp.where(within(48, 72), im, zero))
        o0 = jnp.where(
            within(24, 48), roll(re, 24), jnp.where(within(72, 96), roll(im, 72), zero)
        )
        o1 = jnp.where(lane < 48, roll(re, 104), jnp.where(within(48, 96), roll(im, 24), zero))
        tmp[pl.ds(0, 64, stride=2), :] = jnp.where(even, e0, o0)
        tmp[pl.ds(1, 64, stride=2), :] = jnp.where(even, e1, o1)
        sp[st] = tmp[...].reshape(32, 4, 128)

    def inverse_x(st):
        p = dot3((bxh[...], bxl[...]), split(rp[st].reshape(128, 128)), NN)
        pc, ps = p[:512], p[512:]
        side = iota((512, 128), 1) < 48
        sx[st] = pc + jnp.where(side, -pltpu.roll(ps, 80, 1), pltpu.roll(ps, 48, 1))

    def inverse_y(st):
        for t in range(4):
            data = split(rx[st, pl.ds(t * 128, 128), :])
            sy[st, t] = dot3((yh[...], yl[...]), data, NT)

    row64 = iota((64, 128), 0)
    zeroth = (row64 < 16) | ((row64 >= 48) & (row64 < 52))
    weight_z = jnp.where(zeroth & (yy == 0), 1.0 / CELLS, 2.0 / CELLS)

    landed_y(0, 0)
    landed_y(0, 1)
    forward_y(0)
    send_x(0)
    landed(rx.at[0], rx_sem.at[0])
    forward_x(0)
    send_p(0)
    landed(rp.at[0], rp_sem.at[0])
    re, im = spectrum(0)
    for kz in range(3):
        for o in range(4):
            for r in range(2):
                at = o * 6 + kz * 2 + r
                sign = 1.0 if r == 0 else -1.0
                most = pl.ds(at, 16, stride=24)
                rest = pl.ds(16 * 24 + at, 4, stride=24)
                u1[most, :] = re[kz * 16 : kz * 16 + 16]
                u1[rest, :] = re[48 + kz * 4 : 52 + kz * 4]
                u2[most, :] = sign * im[kz * 16 : kz * 16 + 16]
                u2[rest, :] = sign * im[48 + kz * 4 : 52 + kz * 4]

    real_row = lax.rem(iota((24, 128), 0), 2) == 0

    def mix(c, acc):
        a, b = acc
        rows = pl.ds(c * 24, 24)
        s1, s2 = u1[rows, :], u2[rows, :]
        sa = jnp.concatenate([jnp.where(real_row, s1, s2)] * 5, axis=0)
        sb = jnp.concatenate([jnp.where(real_row, s2, s1)] * 5, axis=0)
        return a + wf[c] * sa, b + wf[c] * sb

    zero = jnp.zeros((120, 128), F32)
    a, b = lax.fori_loop(0, C, mix, (zero, zero))
    modes(pick(sel_o[...], a) * weight_z, pick(sel_o[...], b) * weight_z, 1)
    send_p(1)
    landed(rp.at[1], rp_sem.at[1])
    inverse_x(1)
    send_x(1)
    landed(rx.at[1], rx_sem.at[1])
    inverse_y(1)
    send_y(1, 0)
    send_y(1, 1)

    lw[...] = jnp.zeros_like(lw)
    ones_rows = jnp.ones((16, 256), BF16)

    def middle(h, y8, _):
        conv = synthesize_z(1, h, y8)
        y = h * 8 + y8
        f = rows_of(fs, y).astype(BF16)
        v = dot(pw1[...], f, NN) + jnp.concatenate([bb[...], bb[...]], axis=1) + conv
        square = v * v
        t = jnp.tanh(GELU_A * v * (1.0 + GELU_B * square))
        half = 0.5 * (1.0 + t)
        act = v * half
        slope = half + (0.5 * GELU_A) * v * (1.0 - t * t) * (1.0 + (3.0 * GELU_B) * square)
        grad = rows_of(cs, y) * slope
        rows = pl.ds(y, 160, stride=16)
        fs[0, rows, :] = act[:, :128]
        fs[1, rows, :] = act[:, 128:]
        high, low = split(grad)
        gh[y] = high
        gl[y] = low
        f = jnp.concatenate([f, ones_rows], axis=0)
        lw[...] += dot(f, high, NT) + dot(f, low, NT)
        s = dot(tz[...], jnp.concatenate([high, pad_rows], axis=0), NT)
        s = s[0:48] + s[48:96]
        s = s + dot(tz[0:48, :], jnp.concatenate([low, pad_rows], axis=0), NT)
        analyze_z(2, h, y8, s)
        return 0

    for h in range(2):
        landed_y(1, h)
        lax.fori_loop(0, 8, functools.partial(middle, h), 0, unroll=4)
        send_y(2, h)

    row, col = iota((176, 160), 0), iota((176, 160), 1)
    keep = (row >= 160) | (lax.rem(row, 8) == lax.rem(col, 8))
    total = jnp.where(keep, lw[...], 0.0)
    row, col = iota((32, 176), 0), iota((32, 176), 1)
    left = ((col < 160) & (col // 8 == row)) | ((row == 20) & (col == 160))
    left = jnp.where(left, 1.0, 0.0).astype(BF16)
    high, low = split(pick(left, total))
    e128 = ones_e.astype(BF16)
    ls[...] = dot(high, e128, NN) + dot(low, e128, NN)
    for k in range(1, GY):
        d = lax.rem(yy + k, GY)
        pltpu.make_async_remote_copy(
            src_ref=ls,
            dst_ref=lr.at[yy],
            send_sem=l_sem.at[0],
            recv_sem=l_sem.at[1],
            device_id=(g, d),
            device_id_type=MESH,
        ).start()
    pltpu.make_async_copy(ls, lr.at[yy], l_sem.at[1]).start()

    def write_out(c, _):
        rows = pl.ds(c * 128, 128)
        v = jnp.concatenate([fs[0, rows, :], fs[1, rows, :]], axis=1)
        out_v[c] = v.astype(BF16).reshape(8, 16, 256)
        return 0

    lax.fori_loop(0, C, write_out, 0, unroll=4)
    pltpu.make_async_copy(out_v, out, o_sem.at[0]).start()

    landed_y(2, 0)
    landed_y(2, 1)
    forward_y(2)
    send_x(2)

    landed(lr, l_sem.at[1])
    ms[...] = jnp.sum(lr[...], axis=0)

    def share(k, _):
        d = lax.rem(g + k, GX)
        pltpu.make_async_remote_copy(
            src_ref=ms,
            dst_ref=mr.at[g],
            send_sem=l_sem.at[2],
            recv_sem=l_sem.at[3],
            device_id=(d, yy),
            device_id_type=MESH,
        ).start()
        return 0

    lax.fori_loop(1, GX, share, 0)
    pltpu.make_async_copy(ms, mr.at[g], l_sem.at[3]).start()

    landed(rx.at[2], rx_sem.at[2])
    forward_x(2)
    send_p(2)
    landed(rp.at[2], rp_sem.at[2])
    re, im = spectrum(2)
    re, im = re * weight_z, im * weight_z
    for kz in range(3):
        for r in range(2):
            most = pl.ds(kz * 2 + r, 16, stride=6)
            rest = pl.ds(96 + kz * 2 + r, 4, stride=6)
            one, two = (re, im) if r == 0 else (im, re)
            d1[most, :] = one[kz * 16 : kz * 16 + 16]
            d1[rest, :] = one[48 + kz * 4 : 52 + kz * 4]
            d2[most, :] = two[kz * 16 : kz * 16 + 16]
            d2[rest, :] = two[48 + kz * 4 : 52 + kz * 4]

    even_row = lax.rem(iota((120, 128), 0), 2) == 0

    def unmix(c, _):
        rows = pl.ds(c * 24, 24)
        x1 = d1[...]
        x2 = jnp.where(even_row, d2[...], -d2[...])
        wc = wf[c]
        q1[rows, :] = jnp.sum((wc * x1).reshape(5, 24, 128), axis=0)
        q2[rows, :] = jnp.sum((wc * x2).reshape(5, 24, 128), axis=0)
        return 0

    lax.fori_loop(0, C, unmix, 0, unroll=2)
    modes(pick(sel_c[...], q1[...]), pick(sel_c[...], q2[...]), 3)
    send_p(3)

    def outer(c, _):
        rows = pl.ds(c * 24, 24)
        s1 = jnp.concatenate([u1[rows, :]] * 5, axis=0)
        s2 = jnp.concatenate([u2[rows, :]] * 5, axis=0)
        v = s1 * d1[...] + s2 * d2[...]
        gs_v[c] = v[:, 0:72].reshape(20, 3, 2, 72)
        return 0

    lax.fori_loop(0, C, outer, 0, unroll=2)
    pltpu.make_async_copy(gs_v, gs, o_sem.at[1]).start()

    landed(rp.at[3], rp_sem.at[3])
    inverse_x(3)
    send_x(3)
    landed(mr, l_sem.at[3])
    small[...] = jnp.sum(mr[...], axis=0) * (CELLS**-0.5)
    landed(rx.at[3], rx_sem.at[3])
    inverse_y(3)
    send_y(3, 0)
    send_y(3, 1)

    def last(h, y8, _):
        y = h * 8 + y8
        back = dot(pw2[...], gh[y], NN) + dot(pw2[...], gl[y], NN)
        back = back + synthesize_z(3, h, y8)
        rows = pl.ds(y, 160, stride=16)
        cs[0, rows, :] = back[:, :128]
        cs[1, rows, :] = back[:, 128:]
        return 0

    for h in range(2):
        landed_y(3, h)
        lax.fori_loop(0, 8, functools.partial(last, h), 0, unroll=4)

    def write_grad(c, _):
        rows = pl.ds(c * 128, 128)
        v = jnp.concatenate([cs[0, rows, :], cs[1, rows, :]], axis=1)
        gf_v[c] = v.astype(BF16).reshape(8, 16, 256)
        return 0

    for n in range(4):
        lax.fori_loop(n * 5, n * 5 + 5, write_grad, 0, unroll=5)
        part = pl.ds(n * 5, 5)
        pltpu.make_async_copy(gf_v.at[part], gf.at[part], o_sem.at[2 + n]).start()

    for st in range(4):
        part = sy.at[st, :, pl.ds(0, 112), :]
        for h in range(2):
            pltpu.make_async_copy(part, part, sy_sem.at[2 * st + h]).wait()
        part = sx.at[st, pl.ds(0, 31 * 16)]
        pltpu.make_async_copy(part, part, sx_sem.at[st]).wait()
        part = sp.at[st, pl.ds(0, 31)]
        pltpu.make_async_copy(part, part, sp_sem.at[st]).wait()
    part = lr.at[pl.ds(0, 7)]
    pltpu.make_async_copy(part, part, l_sem.at[0]).wait()
    part = mr.at[pl.ds(0, 31)]
    pltpu.make_async_copy(part, part, l_sem.at[2]).wait()
    pltpu.make_async_copy(out_v, out, o_sem.at[0]).wait()
    pltpu.make_async_copy(gs_v, gs, o_sem.at[1]).wait()
    for n in range(4):
        part = pl.ds(n * 5, 5)
        pltpu.make_async_copy(gf_v.at[part], gf.at[part], o_sem.at[2 + n]).wait()


def deliver(out_a, gf_a, gs_a, small, out, gf, gs, gp, gb, out_v, gf_v, gs_v, sems):
    there, back = [], []
    for n in range(4):
        part = pl.ds(n * 5, 5)
        for i, (a, v, b) in enumerate(
            ((out_a, out_v, out), (gf_a, gf_v, gf), (gs_a, gs_v, gs))
        ):
            sem = n * 3 + i
            there.append(pltpu.make_async_copy(a.at[part], v.at[part], sems.at[sem]))
            back.append(pltpu.make_async_copy(v.at[part], b.at[part], sems.at[12 + sem]))
    for copy in there:
        copy.start()
    gp[...] = small[0:C, 0:C]
    gb[...] = small[C : C + 1, 0:C]
    for one, other in zip(there, back):
        one.wait()
        other.start()
    for copy in back:
        copy.wait()


def local(consts, field, cotangent, spectral_weight, pointwise_weight, bias):
    vmem = pl.BlockSpec(memory_space=pltpu.VMEM)
    anywhere = pl.BlockSpec(memory_space=pl.ANY)
    dma = pltpu.SemaphoreType.DMA
    weights = jnp.transpose(spectral_weight, (1, 2, 3, 0, 4))
    scratch = [
        pltpu.VMEM((2, 2560, 128), F32),
        pltpu.VMEM((2, 2560, 128), F32),
        pltpu.VMEM((16, 160, 256), BF16),
        pltpu.VMEM((16, 160, 256), BF16),
        pltpu.VMEM((160, 160), BF16),
        pltpu.VMEM((160, 160), BF16),
        pltpu.VMEM((160, 128), F32),
        pltpu.VMEM((40, 128), F32),
        pltpu.VMEM((4, 4, 256, 128), F32),
        pltpu.VMEM((4, 4, 256, 128), F32),
        pltpu.VMEM((4, 512, 128), F32),
        pltpu.VMEM((4, 512, 128), F32),
        pltpu.VMEM((4, 32, 4, 128), F32),
        pltpu.VMEM((4, 32, 4, 128), F32),
        pltpu.VMEM((20, 120, 128), F32),
        pltpu.VMEM((128, 128), F32),
        pltpu.VMEM((480, 128), F32),
        pltpu.VMEM((480, 128), F32),
        pltpu.VMEM((120, 128), F32),
        pltpu.VMEM((120, 128), F32),
        pltpu.VMEM((480, 128), F32),
        pltpu.VMEM((480, 128), F32),
        pltpu.VMEM((176, 160), F32),
        pltpu.VMEM((32, 128), F32),
        pltpu.VMEM((8, 32, 128), F32),
        pltpu.VMEM((32, 128), F32),
        pltpu.VMEM((32, 32, 128), F32),
        pltpu.VMEM((C, 8, 16, 256), BF16),
        pltpu.VMEM((C, 8, 16, 256), BF16),
        pltpu.VMEM((C, C, 3, 2, 72), F32),
        dma((8,)), dma((8,)), dma((4,)), dma((4,)), dma((4,)), dma((4,)), dma((4,)), dma((6,)),
    ]
    out, gf, gs, small = pl.pallas_call(
        kernel,
        out_shape=(
            jax.ShapeDtypeStruct((C, 8, 16, 256), BF16),
            jax.ShapeDtypeStruct((C, 8, 16, 256), BF16),
            jax.ShapeDtypeStruct((C, C, 3, 2, 72), F32),
            jax.ShapeDtypeStruct((32, 128), F32),
        ),
        in_specs=[vmem] * 14,
        out_specs=(anywhere,) * 3 + (vmem,),
        scratch_shapes=scratch,
        compiler_params=pltpu.CompilerParams(
            collective_id=0, has_side_effects=True, vmem_limit_bytes=58 << 20
        ),
        name="fourier_layer",
    )(field, cotangent, weights, pointwise_weight, bias.reshape(1, C), *consts)
    out, gf, gs, gp, gb = pl.pallas_call(
        deliver,
        out_shape=(
            jax.ShapeDtypeStruct((C, 8, 16, 256), BF16),
            jax.ShapeDtypeStruct((C, 8, 16, 256), BF16),
            jax.ShapeDtypeStruct((C, C, 3, 2, 72), F32),
            jax.ShapeDtypeStruct((C, C), F32),
            jax.ShapeDtypeStruct((1, C), F32),
        ),
        in_specs=[anywhere] * 3 + [vmem],
        out_specs=(anywhere,) * 3 + (vmem,) * 2,
        scratch_shapes=[
            pltpu.VMEM((C, 8, 16, 256), BF16),
            pltpu.VMEM((C, 8, 16, 256), BF16),
            pltpu.VMEM((C, C, 3, 2, 72), F32),
            dma((24,)),
        ],
        compiler_params=pltpu.CompilerParams(vmem_limit_bytes=58 << 20),
        name="deliver",
    )(out, gf, gs, small)
    return out, gf, jnp.transpose(gs, (3, 0, 1, 2, 4)), gp, gb.reshape(C)


def solution(mesh):
    consts = [jnp.asarray(t) for t in tables()]
    placed = (
        P(None, "gx", "gy", None),
        P(None, "gx", "gy", None),
        P(None, None, None, "gy", "gx"),
        P(),
        P(),
    )
    return jax.shard_map(
        functools.partial(local, consts),
        mesh=mesh,
        in_specs=placed,
        out_specs=placed,
        check_vma=False,
    )
```

```python
import functools

import jax
import jax.numpy as jnp
import numpy as np
from jax import lax
from jax.experimental import pallas as pl
from jax.experimental.pallas import tpu as pltpu
from jax.sharding import PartitionSpec as P

C = 20
NX, NY, NZ = 256, 128, 256
KX, KY, KZ = 48, 48, 24
GX, GY = 32, 8
CELLS = float(NX * NY * NZ)
F32 = jnp.float32
BF16 = jnp.bfloat16
MESH = pl.DeviceIdType.MESH
NN = (((1,), (0,)), ((), ()))
NT = (((1,), (1,)), ((), ()))
GELU_A = float(np.sqrt(2.0 / np.pi))
GELU_B = 0.044715


def halves(table):
    high = table.astype(BF16)
    low = (table - np.asarray(high, np.float64)).astype(BF16)
    return np.asarray(high), np.asarray(low)


def tables():
    kz, r, d = np.meshgrid(np.arange(3), np.arange(2), np.arange(8), indexing="ij")
    depth = (d * 3 + kz).reshape(-1, 1) * np.arange(NZ)[None, :] % NZ * (2 * np.pi / NZ)
    tz = np.where(r.reshape(-1, 1) == 0, np.cos(depth), -np.sin(depth))
    tz = np.concatenate(halves(tz), axis=0)

    fx = np.where(np.arange(KX) < 24, np.arange(KX), np.arange(KX) - 48 + NX)
    fy = np.where(np.arange(KY) < 24, np.arange(KY), np.arange(KY) - 48 + NY)
    phase = np.arange(NY)[:, None] * fy[None, :] % NY * (2 * np.pi / NY)
    cos, sin = np.cos(phase).reshape(8, 16, KY), np.sin(phase).reshape(8, 16, KY)
    y = np.zeros((8, 2, 16, 128))
    y[:, 0, :, 0:48], y[:, 0, :, 48:96] = cos, -sin
    y[:, 1, :, 0:48], y[:, 1, :, 48:96] = sin, cos
    y = y.reshape(8, 2, 2, 8, 128).transpose(0, 2, 1, 3, 4)
    yh, yl = halves(y.reshape(256, 128))

    g = np.arange(GX)
    first = 3 * (g // 2) + g % 2
    kx = first[:, None] + np.arange(2)[None, :]
    phase = fx[kx][:, :, None] * np.arange(NX)[None, None, :] % NX * (2 * np.pi / NX)
    both = np.stack([np.cos(phase), np.sin(phase)])
    both = both.reshape(2, GX, 2, GX, 8)
    eye = np.eye(2)
    ax = np.einsum("egtsx,mn->egmtsnx", both, eye).reshape(256, 512)
    bx = np.einsum("egtsx,mn->esmxgnt", both, eye).reshape(1024, 128)
    axh, axl = halves(ax)
    bxh, bxl = halves(bx)

    m = np.arange(64)
    kz_m = np.where(m < 48, m // 16, (m - 48) // 4)
    c_m = np.where(m < 48, m % 16, 16 + (m - 48) % 4)
    row = np.arange(120)
    sel_o = (row[None, :] // 6 == c_m[:, None]) & (row[None, :] % 6 // 2 == kz_m[:, None])
    row = np.arange(480)
    sel_c = (row[None, :] // 24 == c_m[:, None]) & (row[None, :] % 6 // 2 == kz_m[:, None])
    live = (m < 60)[:, None]
    sel_o = np.asarray((sel_o & live).astype(BF16))
    sel_c = np.asarray((sel_c & live).astype(BF16))
    return tz, yh, yl, axh, axl, bxh, bxl, sel_o, sel_c


def hops(k):
    return min(k // 4, 8 - k // 4) + min(k % 4, 4 - k % 4)


def iota(shape, axis):
    return lax.broadcasted_iota(jnp.int32, shape, axis)


def dot(a, b, dims):
    return lax.dot_general(a, b, dims, preferred_element_type=F32)


def split(x):
    high = x.astype(BF16)
    return high, (x - high.astype(F32)).astype(BF16)


def dot3(a, b, dims):
    return dot(a[0], b[0], dims) + dot(a[0], b[1], dims) + dot(a[1], b[0], dims)


def pick(sel, x):
    high, low = split(x)
    return dot(sel, high, NN) + dot(sel, low, NN)


def kernel(
    field, cot, w, pw, bias, tz, yh, yl, axh, axl, bxh, bxl, sel_o, sel_c,
    out, gf, gs, small,
    fs, cs, gh, gl, pw1, pw2, bb, pws, sy, ry, sx, rx, sp, rp, wf, tmp,
    u1, u2, d1, d2, q1, q2, lw, ls, lr, ms, mr, out_v, gf_v, gs_v,
    sy_sem, ry_sem, sx_sem, rx_sem, sp_sem, rp_sem, l_sem, o_sem,
):
    g = lax.axis_index("gx")
    yy = lax.axis_index("gy")
    even = lax.rem(g, 2) == 0

    barrier = pltpu.get_barrier_semaphore()

    def greet_y(k, _):
        pl.semaphore_signal(
            barrier, inc=1, device_id=(g, lax.rem(yy + k, GY)), device_id_type=MESH
        )
        return 0

    def greet_x(k, _):
        pl.semaphore_signal(
            barrier, inc=1, device_id=(lax.rem(g + k, GX), yy), device_id_type=MESH
        )
        return 0

    lax.fori_loop(1, GY, greet_y, 0)
    lax.fori_loop(1, GX, greet_x, 0)

    chip, core = yy // 2, lax.rem(yy, 2)
    others_y = [
        lax.rem(chip + n, 4) * 2 + (core if same else 1 - core)
        for n, same in ((2, 1), (2, 0), (1, 1), (3, 1), (1, 0), (3, 0), (0, 0))
    ]

    def send_y(st, h):
        sem_s, sem_r = sy_sem.at[2 * st + h], ry_sem.at[2 * st + h]
        own = pl.ds(yy * 32 + h * 16, 16)
        for d in others_y:
            pltpu.make_async_remote_copy(
                src_ref=sy.at[st, :, pl.ds(d * 32 + h * 16, 16), :],
                dst_ref=ry.at[st, :, own, :],
                send_sem=sem_s,
                recv_sem=sem_r,
                device_id=(g, d),
                device_id_type=MESH,
            ).start()
        pltpu.make_async_copy(sy.at[st, :, own, :], ry.at[st, :, own, :], sem_r).start()

    def send_y_tiles(st):
        own = pl.ds(yy * 32 + 16, 16)
        for t in range(4):
            sem = 8 + st * 2 + t
            for d in others_y:
                pltpu.make_async_remote_copy(
                    src_ref=sy.at[st, t, pl.ds(d * 32 + 16, 16), :],
                    dst_ref=ry.at[st, t, own, :],
                    send_sem=sy_sem.at[sem],
                    recv_sem=ry_sem.at[sem],
                    device_id=(g, d),
                    device_id_type=MESH,
                ).start()
            pltpu.make_async_copy(
                sy.at[st, t, own, :], ry.at[st, t, own, :], ry_sem.at[sem]
            ).start()

    def landed_y(st, h):
        landed(ry.at[st, :, pl.ds(0, 128), :], ry_sem.at[2 * st + h])

    gz, gw = g // 4, lax.rem(g, 4)
    far_first = sorted(range(1, GX), key=hops, reverse=True)

    def place(z, w):
        return w * 8 + z

    def send_gx(src, dst, ssem, rsem, size, to_owner):
        mine = place(gz, gw)
        to = g if to_owner else mine
        for k in far_first:
            z, w = lax.rem(gz + k // 4, 8), lax.rem(gw + k % 4, 4)
            at = place(z, w) if to_owner else z * 4 + w
            pltpu.make_async_remote_copy(
                src_ref=src.at[pl.ds(at * size, size)],
                dst_ref=dst.at[pl.ds(to * size, size)],
                send_sem=ssem,
                recv_sem=rsem,
                device_id=(z * 4 + w, yy),
                device_id_type=MESH,
            ).start()
        own = mine if to_owner else g
        pltpu.make_async_copy(
            src.at[pl.ds(own * size, size)], dst.at[pl.ds(to * size, size)], rsem
        ).start()

    def send_x(st):
        send_gx(sx.at[st], rx.at[st], sx_sem.at[st], rx_sem.at[st], 16, False)

    def send_p(st):
        send_gx(sp.at[st], rp.at[st], sp_sem.at[st], rp_sem.at[st], 1, st % 2 == 1)

    def send_x_tile(st, t):
        own = pl.ds(g * 16, 16)

        def remote(z, at):
            pltpu.make_async_remote_copy(
                src_ref=sx.at[st, at],
                dst_ref=rx.at[st, own],
                send_sem=sx_sem.at[st],
                recv_sem=rx_sem.at[st],
                device_id=(z * 4 + t, yy),
                device_id_type=MESH,
            ).start()

        for n in (4, 3, 5, 2, 6, 1, 7):
            z = lax.rem(gz + n, 8)
            remote(z, pl.ds(place(z, t) * 16, 16))
        at = pl.ds(place(gz, t) * 16, 16)

        @pl.when(gw != t)
        def _():
            remote(gz, at)

        @pl.when(gw == t)
        def _():
            pltpu.make_async_copy(sx.at[st, at], rx.at[st, own], rx_sem.at[st]).start()

    def landed(ref, sem):
        pltpu.make_async_copy(ref, ref, sem).wait()

    lane = iota((64, 128), 1)

    def widen(c, _):
        rows = pl.ds(c * 128, 128)
        v = field[c].astype(F32).reshape(128, 256)
        fs[0, rows, :] = v[:, :128]
        fs[1, rows, :] = v[:, 128:]
        return 0

    lax.fori_loop(0, C, widen, 0, unroll=4)

    def rows_of(ref, y):
        rows = pl.ds(y, 160, stride=16)
        return jnp.concatenate([ref[0, rows, :], ref[1, rows, :]], axis=1)

    pad_rows = jnp.zeros((96, 256), BF16)

    def analyze_z(st, h, y, s):
        for r in range(2):
            rows = pl.ds(h * 16 + r * 8 + y, 8, stride=32)
            tail = None
            for kz in range(3):
                at = (kz * 2 + r) * 8
                sy[st, kz, rows, :] = s[at : at + 8, :128]
                piece = s[at : at + 8, 128:]
                tail = piece if kz == 0 else tail + pltpu.roll(piece, 32 * kz, 1)
            sy[st, 3, rows, :] = tail

    def synthesize_z(st, h, y):
        main, tail = [], []
        for kz in range(3):
            for r in range(2):
                rows = pl.ds(h * 16 + r * 8 + y, 8, stride=32)
                main.append(ry[st, kz, rows, :])
                piece = ry[st, 3, rows, :]
                tail.append(piece if kz == 0 else pltpu.roll(piece, 128 - 32 * kz, 1))
        data = jnp.concatenate(
            [jnp.concatenate(main, axis=0), jnp.concatenate(tail, axis=0)], axis=1
        )
        data = split(jnp.transpose(data)[:160])
        return dot3(data, (tz[0:48, :], tz[48:96, :]), NN)

    def first_y(h, y, _):
        f = jnp.concatenate([rows_of(fs, h * 8 + y).astype(BF16), pad_rows], axis=0)
        s = dot(tz[...], f, NT)
        analyze_z(0, h, y, s[0:48] + s[48:96])
        return 0

    for h in range(2):
        lax.fori_loop(0, 8, functools.partial(first_y, h), 0, unroll=8)

    pl.semaphore_wait(barrier, GY - 1 + GX - 1)
    send_y(0, 0)
    send_y_tiles(0)

    def widen_more(c, _):
        rows = pl.ds(c * 128, 128)
        v = cot[c].astype(F32).reshape(128, 256)
        cs[0, rows, :] = v[:, :128]
        cs[1, rows, :] = v[:, 128:]
        wf[c, :, 0:72] = w[c].astype(F32).reshape(120, 72)
        return 0

    wf[...] = jnp.zeros_like(wf)
    lax.fori_loop(0, C, widen_more, 0, unroll=4)

    pws[...] = jnp.zeros_like(pws)
    pws[0:20, 0:20] = pw[...].astype(F32)
    pws[32:33, 0:20] = bias[...]
    ones_e = iota((160, 128), 0) // 8 == iota((160, 128), 1)
    ones_e = jnp.where(ones_e, 1.0, 0.0)
    e = ones_e[:, :32].astype(BF16)
    same_x = lax.rem(iota((160, 160), 0), 8) == lax.rem(iota((160, 160), 1), 8)
    m = pws[0:32, 0:32].astype(BF16)
    t = dot(e, m, NT).astype(BF16)
    pw1[...] = jnp.where(same_x, dot(t, e, NT), 0.0).astype(BF16)
    t = dot(e, m, NN).astype(BF16)
    pw2[...] = jnp.where(same_x, dot(t, e, NT), 0.0).astype(BF16)
    column = jnp.sum(ones_e * pws[32:33, :], axis=1, keepdims=True)
    bb[...] = jnp.broadcast_to(column, (160, 128))

    def forward_y(st):
        landed_y(st, 0)
        for t in range(4):
            landed(ry.at[st, t, pl.ds(0, 128), :], ry_sem.at[8 + st * 2 + t])
            data = split(jnp.transpose(ry[st, t]))
            sx[st, pl.ds(t * 128, 128), :] = dot3(data, (yh[...], yl[...]), NN)
            send_x_tile(st, t)

    def forward_x(st):
        p = dot3((axh[...], axl[...]), split(rx[st]), NN)
        pc, ps = p[:128], p[128:]
        side = iota((128, 128), 1) < 48
        o = pc + jnp.where(side, pltpu.roll(ps, 80, 1), -pltpu.roll(ps, 48, 1))
        sp[st] = o.reshape(32, 4, 128)

    def spectrum(st):
        tmp[...] = rp[st].reshape(128, 128)
        k0 = tmp[pl.ds(0, 64, stride=2), :]
        k1 = tmp[pl.ds(1, 64, stride=2), :]
        roll = lambda v, n: pltpu.roll(v, n, 1)
        re_e = jnp.where(lane < 48, k0, roll(k1, 48))
        im_e = jnp.where(lane < 48, roll(k0, 80), k1)
        re_o = jnp.where(lane < 24, roll(k0, 104), roll(k1, 24))
        im_o = jnp.where(lane < 24, roll(k0, 56), roll(k1, 104))
        live = lane < 72
        re = jnp.where(live, jnp.where(even, re_e, re_o), 0.0)
        im = jnp.where(live, jnp.where(even, im_e, im_o), 0.0)
        return re, im

    def modes(re, im, st):
        roll = lambda v, n: pltpu.roll(v, n, 1)
        within = lambda a, b: (lane >= a) & (lane < b)
        zero = jnp.zeros((64, 128), F32)
        e0 = jnp.where(lane < 48, re, jnp.where(within(48, 96), roll(im, 48), zero))
        e1 = jnp.where(lane < 24, roll(re, 80), jnp.where(within(48, 72), im, zero))
        o0 = jnp.where(
            within(24, 48), roll(re, 24), jnp.where(within(72, 96), roll(im, 72), zero)
        )
        o1 = jnp.where(lane < 48, roll(re, 104), jnp.where(within(48, 96), roll(im, 24), zero))
        tmp[pl.ds(0, 64, stride=2), :] = jnp.where(even, e0, o0)
        tmp[pl.ds(1, 64, stride=2), :] = jnp.where(even, e1, o1)
        sp[st] = tmp[...].reshape(32, 4, 128)

    def inverse_x(st):
        p = dot3((bxh[...], bxl[...]), split(rp[st].reshape(128, 128)), NN)
        pc, ps = p[:512], p[512:]
        side = iota((512, 128), 1) < 48
        sx[st] = pc + jnp.where(side, -pltpu.roll(ps, 80, 1), pltpu.roll(ps, 48, 1))

    def inverse_y(st):
        for t in range(4):
            data = split(rx[st, pl.ds(t * 128, 128), :])
            sy[st, t] = dot3((yh[...], yl[...]), data, NT)

    row64 = iota((64, 128), 0)
    zeroth = (row64 < 16) | ((row64 >= 48) & (row64 < 52))
    weight_z = jnp.where(zeroth & (yy == 0), 1.0 / CELLS, 2.0 / CELLS)

    forward_y(0)
    landed(rx.at[0], rx_sem.at[0])
    forward_x(0)
    send_p(0)
    landed(rp.at[0], rp_sem.at[0])
    re, im = spectrum(0)
    for kz in range(3):
        for o in range(4):
            for r in range(2):
                at = o * 6 + kz * 2 + r
                sign = 1.0 if r == 0 else -1.0
                most = pl.ds(at, 16, stride=24)
                rest = pl.ds(16 * 24 + at, 4, stride=24)
                u1[most, :] = re[kz * 16 : kz * 16 + 16]
                u1[rest, :] = re[48 + kz * 4 : 52 + kz * 4]
                u2[most, :] = sign * im[kz * 16 : kz * 16 + 16]
                u2[rest, :] = sign * im[48 + kz * 4 : 52 + kz * 4]

    real_row = lax.rem(iota((24, 128), 0), 2) == 0

    def mix(c, acc):
        a, b = acc
        rows = pl.ds(c * 24, 24)
        s1, s2 = u1[rows, :], u2[rows, :]
        sa = jnp.concatenate([jnp.where(real_row, s1, s2)] * 5, axis=0)
        sb = jnp.concatenate([jnp.where(real_row, s2, s1)] * 5, axis=0)
        return a + wf[c] * sa, b + wf[c] * sb

    zero = jnp.zeros((120, 128), F32)
    a, b = lax.fori_loop(0, C, mix, (zero, zero), unroll=4)
    modes(pick(sel_o[...], a) * weight_z, pick(sel_o[...], b) * weight_z, 1)
    send_p(1)
    landed(rp.at[1], rp_sem.at[1])
    inverse_x(1)
    send_x(1)
    landed(rx.at[1], rx_sem.at[1])
    inverse_y(1)
    send_y(1, 0)
    send_y(1, 1)

    lw[...] = jnp.zeros_like(lw)
    ones_rows = jnp.ones((16, 256), BF16)

    def middle(h, y8, _):
        conv = synthesize_z(1, h, y8)
        y = h * 8 + y8
        f = rows_of(fs, y).astype(BF16)
        v = dot(pw1[...], f, NN) + jnp.concatenate([bb[...], bb[...]], axis=1) + conv
        square = v * v
        t = jnp.tanh(GELU_A * v * (1.0 + GELU_B * square))
        half = 0.5 * (1.0 + t)
        act = v * half
        slope = half + (0.5 * GELU_A) * v * (1.0 - t * t) * (1.0 + (3.0 * GELU_B) * square)
        grad = rows_of(cs, y) * slope
        rows = pl.ds(y, 160, stride=16)
        fs[0, rows, :] = act[:, :128]
        fs[1, rows, :] = act[:, 128:]
        high, low = split(grad)
        gh[y] = high
        gl[y] = low
        f = jnp.concatenate([tz[...], f, ones_rows], axis=0)
        p = dot(f, jnp.concatenate([high, pad_rows], axis=0), NT)
        f = jnp.concatenate([f[0:48], f[96:]], axis=0)
        n = dot(f, jnp.concatenate([low, pad_rows], axis=0), NT)
        lw[...] += p[96:] + n[48:]
        analyze_z(2, h, y8, p[0:48] + p[48:96] + n[0:48])
        return 0

    for h in range(2):
        landed_y(1, h)
        lax.fori_loop(0, 8, functools.partial(middle, h), 0, unroll=8)
        if h == 0:
            send_y(2, 0)
        else:
            send_y_tiles(2)

    row, col = iota((176, 160), 0), iota((176, 160), 1)
    keep = (row >= 160) | (lax.rem(row, 8) == lax.rem(col, 8))
    total = jnp.where(keep, lw[:, 0:160], 0.0)
    row, col = iota((32, 176), 0), iota((32, 176), 1)
    left = ((col < 160) & (col // 8 == row)) | ((row == 20) & (col == 160))
    left = jnp.where(left, 1.0, 0.0).astype(BF16)
    high, low = split(pick(left, total))
    e128 = ones_e.astype(BF16)
    ls[...] = dot(high, e128, NN) + dot(low, e128, NN)
    for k in range(1, GY):
        d = lax.rem(yy + k, GY)
        pltpu.make_async_remote_copy(
            src_ref=ls,
            dst_ref=lr.at[yy],
            send_sem=l_sem.at[0],
            recv_sem=l_sem.at[1],
            device_id=(g, d),
            device_id_type=MESH,
        ).start()
    pltpu.make_async_copy(ls, lr.at[yy], l_sem.at[1]).start()

    def write_out(c, _):
        rows = pl.ds(c * 128, 128)
        v = jnp.concatenate([fs[0, rows, :], fs[1, rows, :]], axis=1)
        out_v[c] = v.astype(BF16).reshape(8, 16, 256)
        return 0

    lax.fori_loop(0, C, write_out, 0, unroll=4)
    pltpu.make_async_copy(out_v, out, o_sem.at[0]).start()

    forward_y(2)

    landed(lr, l_sem.at[1])
    ms[...] = jnp.sum(lr[...], axis=0)

    def share(k, _):
        d = lax.rem(g + k, GX)
        pltpu.make_async_remote_copy(
            src_ref=ms,
            dst_ref=mr.at[g],
            send_sem=l_sem.at[2],
            recv_sem=l_sem.at[3],
            device_id=(d, yy),
            device_id_type=MESH,
        ).start()
        return 0

    lax.fori_loop(1, GX, share, 0)
    pltpu.make_async_copy(ms, mr.at[g], l_sem.at[3]).start()

    landed(rx.at[2], rx_sem.at[2])
    forward_x(2)
    send_p(2)
    landed(rp.at[2], rp_sem.at[2])
    re, im = spectrum(2)
    re, im = re * weight_z, im * weight_z
    for kz in range(3):
        for r in range(2):
            most = pl.ds(kz * 2 + r, 16, stride=6)
            rest = pl.ds(96 + kz * 2 + r, 4, stride=6)
            one, two = (re, im) if r == 0 else (im, re)
            d1[most, :] = one[kz * 16 : kz * 16 + 16]
            d1[rest, :] = one[48 + kz * 4 : 52 + kz * 4]
            d2[most, :] = two[kz * 16 : kz * 16 + 16]
            d2[rest, :] = two[48 + kz * 4 : 52 + kz * 4]

    even_row = lax.rem(iota((120, 128), 0), 2) == 0

    def unmix(c, _):
        rows = pl.ds(c * 24, 24)
        x1 = d1[...]
        x2 = jnp.where(even_row, d2[...], -d2[...])
        wc = wf[c]
        q1[rows, :] = jnp.sum((wc * x1).reshape(5, 24, 128), axis=0)
        q2[rows, :] = jnp.sum((wc * x2).reshape(5, 24, 128), axis=0)
        return 0

    lax.fori_loop(0, C, unmix, 0, unroll=4)
    modes(pick(sel_c[...], q1[...]), pick(sel_c[...], q2[...]), 3)
    send_p(3)

    def outer(c, _):
        rows = pl.ds(c * 24, 24)
        s1 = jnp.concatenate([u1[rows, :]] * 5, axis=0)
        s2 = jnp.concatenate([u2[rows, :]] * 5, axis=0)
        v = s1 * d1[...] + s2 * d2[...]
        gs_v[c] = v[:, 0:72].reshape(20, 3, 2, 72)
        return 0

    lax.fori_loop(0, C, outer, 0, unroll=2)
    pltpu.make_async_copy(gs_v, gs, o_sem.at[1]).start()

    landed(rp.at[3], rp_sem.at[3])
    inverse_x(3)
    send_x(3)
    landed(mr, l_sem.at[3])
    small[...] = jnp.sum(mr[...], axis=0) * (CELLS**-0.5)
    landed(rx.at[3], rx_sem.at[3])
    inverse_y(3)
    send_y(3, 0)
    send_y(3, 1)

    def last(h, y8, _):
        y = h * 8 + y8
        back = dot(pw2[...], gh[y], NN) + dot(pw2[...], gl[y], NN)
        back = back + synthesize_z(3, h, y8)
        rows = pl.ds(y, 160, stride=16)
        cs[0, rows, :] = back[:, :128]
        cs[1, rows, :] = back[:, 128:]
        return 0

    for h in range(2):
        landed_y(3, h)
        lax.fori_loop(0, 8, functools.partial(last, h), 0, unroll=8)

    def write_grad(c, _):
        rows = pl.ds(c * 128, 128)
        v = jnp.concatenate([cs[0, rows, :], cs[1, rows, :]], axis=1)
        gf_v[c] = v.astype(BF16).reshape(8, 16, 256)
        return 0

    for n in range(4):
        lax.fori_loop(n * 5, n * 5 + 5, write_grad, 0, unroll=5)
        part = pl.ds(n * 5, 5)
        pltpu.make_async_copy(gf_v.at[part], gf.at[part], o_sem.at[2 + n]).start()

    for st in range(4):
        part = sy.at[st, :, pl.ds(0, 112), :]
        for h in range(2 if st % 2 == 1 else 1):
            pltpu.make_async_copy(part, part, sy_sem.at[2 * st + h]).wait()
        if st % 2 == 0:
            for t in range(4):
                part = sy.at[st, t, pl.ds(0, 112), :]
                pltpu.make_async_copy(part, part, sy_sem.at[8 + st * 2 + t]).wait()
        part = sx.at[st, pl.ds(0, 31 * 16)]
        pltpu.make_async_copy(part, part, sx_sem.at[st]).wait()
        part = sp.at[st, pl.ds(0, 31)]
        pltpu.make_async_copy(part, part, sp_sem.at[st]).wait()
    part = lr.at[pl.ds(0, 7)]
    pltpu.make_async_copy(part, part, l_sem.at[0]).wait()
    part = mr.at[pl.ds(0, 31)]
    pltpu.make_async_copy(part, part, l_sem.at[2]).wait()
    pltpu.make_async_copy(out_v, out, o_sem.at[0]).wait()
    pltpu.make_async_copy(gs_v, gs, o_sem.at[1]).wait()
    for n in range(4):
        part = pl.ds(n * 5, 5)
        pltpu.make_async_copy(gf_v.at[part], gf.at[part], o_sem.at[2 + n]).wait()


def deliver(out_a, gf_a, gs_a, small, out, gf, gs, gp, gb, out_v, gf_v, gs_v, sems):
    there, back = [], []
    for n in range(4):
        part = pl.ds(n * 5, 5)
        for i, (a, v, b) in enumerate(
            ((out_a, out_v, out), (gf_a, gf_v, gf), (gs_a, gs_v, gs))
        ):
            sem = n * 3 + i
            there.append(pltpu.make_async_copy(a.at[part], v.at[part], sems.at[sem]))
            back.append(pltpu.make_async_copy(v.at[part], b.at[part], sems.at[12 + sem]))
    for copy in there:
        copy.start()
    gp[...] = small[0:C, 0:C]
    gb[...] = small[C : C + 1, 0:C]
    for one, other in zip(there, back):
        one.wait()
        other.start()
    for copy in back:
        copy.wait()


def local(consts, field, cotangent, spectral_weight, pointwise_weight, bias):
    vmem = pl.BlockSpec(memory_space=pltpu.VMEM)
    anywhere = pl.BlockSpec(memory_space=pl.ANY)
    dma = pltpu.SemaphoreType.DMA
    weights = jnp.transpose(spectral_weight, (1, 2, 3, 0, 4))
    scratch = [
        pltpu.VMEM((2, 2560, 128), F32),
        pltpu.VMEM((2, 2560, 128), F32),
        pltpu.VMEM((16, 160, 256), BF16),
        pltpu.VMEM((16, 160, 256), BF16),
        pltpu.VMEM((160, 160), BF16),
        pltpu.VMEM((160, 160), BF16),
        pltpu.VMEM((160, 128), F32),
        pltpu.VMEM((40, 128), F32),
        pltpu.VMEM((4, 4, 256, 128), F32),
        pltpu.VMEM((4, 4, 256, 128), F32),
        pltpu.VMEM((4, 512, 128), F32),
        pltpu.VMEM((4, 512, 128), F32),
        pltpu.VMEM((4, 32, 4, 128), F32),
        pltpu.VMEM((4, 32, 4, 128), F32),
        pltpu.VMEM((20, 120, 128), F32),
        pltpu.VMEM((128, 128), F32),
        pltpu.VMEM((480, 128), F32),
        pltpu.VMEM((480, 128), F32),
        pltpu.VMEM((120, 128), F32),
        pltpu.VMEM((120, 128), F32),
        pltpu.VMEM((480, 128), F32),
        pltpu.VMEM((480, 128), F32),
        pltpu.VMEM((176, 256), F32),
        pltpu.VMEM((32, 128), F32),
        pltpu.VMEM((8, 32, 128), F32),
        pltpu.VMEM((32, 128), F32),
        pltpu.VMEM((32, 32, 128), F32),
        pltpu.VMEM((C, 8, 16, 256), BF16),
        pltpu.VMEM((C, 8, 16, 256), BF16),
        pltpu.VMEM((C, C, 3, 2, 72), F32),
        dma((16,)), dma((16,)), dma((4,)), dma((4,)), dma((4,)), dma((4,)), dma((4,)), dma((6,)),
    ]
    out, gf, gs, small = pl.pallas_call(
        kernel,
        out_shape=(
            jax.ShapeDtypeStruct((C, 8, 16, 256), BF16),
            jax.ShapeDtypeStruct((C, 8, 16, 256), BF16),
            jax.ShapeDtypeStruct((C, C, 3, 2, 72), F32),
            jax.ShapeDtypeStruct((32, 128), F32),
        ),
        in_specs=[vmem] * 14,
        out_specs=(anywhere,) * 3 + (vmem,),
        scratch_shapes=scratch,
        compiler_params=pltpu.CompilerParams(
            collective_id=0, has_side_effects=True, vmem_limit_bytes=58 << 20
        ),
        name="fourier_layer",
    )(field, cotangent, weights, pointwise_weight, bias.reshape(1, C), *consts)
    out, gf, gs, gp, gb = pl.pallas_call(
        deliver,
        out_shape=(
            jax.ShapeDtypeStruct((C, 8, 16, 256), BF16),
            jax.ShapeDtypeStruct((C, 8, 16, 256), BF16),
            jax.ShapeDtypeStruct((C, C, 3, 2, 72), F32),
            jax.ShapeDtypeStruct((C, C), F32),
            jax.ShapeDtypeStruct((1, C), F32),
        ),
        in_specs=[anywhere] * 3 + [vmem],
        out_specs=(anywhere,) * 3 + (vmem,) * 2,
        scratch_shapes=[
            pltpu.VMEM((C, 8, 16, 256), BF16),
            pltpu.VMEM((C, 8, 16, 256), BF16),
            pltpu.VMEM((C, C, 3, 2, 72), F32),
            dma((24,)),
        ],
        compiler_params=pltpu.CompilerParams(vmem_limit_bytes=58 << 20),
        name="deliver",
    )(out, gf, gs, small)
    return out, gf, jnp.transpose(gs, (3, 0, 1, 2, 4)), gp, gb.reshape(C)


def solution(mesh):
    consts = [jnp.asarray(t) for t in tables()]
    placed = (
        P(None, "gx", "gy", None),
        P(None, "gx", "gy", None),
        P(None, None, None, "gy", "gx"),
        P(),
        P(),
    )
    return jax.shard_map(
        functools.partial(local, consts),
        mesh=mesh,
        in_specs=placed,
        out_specs=placed,
        check_vma=False,
    )
```

```python
import functools

import jax
import jax.numpy as jnp
import numpy as np
from jax import lax
from jax.experimental import pallas as pl
from jax.experimental.pallas import tpu as pltpu
from jax.sharding import PartitionSpec as P

C = 20
NX, NY, NZ = 256, 128, 256
KX, KY, KZ = 48, 48, 24
GX, GY = 32, 8
CELLS = float(NX * NY * NZ)
F32 = jnp.float32
BF16 = jnp.bfloat16
MESH = pl.DeviceIdType.MESH
NN = (((1,), (0,)), ((), ()))
NT = (((1,), (1,)), ((), ()))
TN = (((0,), (0,)), ((), ()))
GELU_A = float(np.sqrt(2.0 / np.pi))
GELU_B = 0.044715


def halves(table):
    high = table.astype(BF16)
    low = (table - np.asarray(high, np.float64)).astype(BF16)
    return np.asarray(high), np.asarray(low)


def tables():
    kz, r, d = np.meshgrid(np.arange(3), np.arange(2), np.arange(8), indexing="ij")
    depth = (d * 3 + kz).reshape(-1, 1) * np.arange(NZ)[None, :] % NZ * (2 * np.pi / NZ)
    tz = np.where(r.reshape(-1, 1) == 0, np.cos(depth), -np.sin(depth))
    tz = np.concatenate(halves(tz), axis=0)

    fx = np.where(np.arange(KX) < 24, np.arange(KX), np.arange(KX) - 48 + NX)
    fy = np.where(np.arange(KY) < 24, np.arange(KY), np.arange(KY) - 48 + NY)
    phase = np.arange(NY)[:, None] * fy[None, :] % NY * (2 * np.pi / NY)
    cos, sin = np.cos(phase).reshape(8, 16, KY), np.sin(phase).reshape(8, 16, KY)
    y = np.zeros((8, 2, 16, 128))
    y[:, 0, :, 0:48], y[:, 0, :, 48:96] = cos, -sin
    y[:, 1, :, 0:48], y[:, 1, :, 48:96] = sin, cos
    y = y.reshape(8, 2, 2, 8, 128).transpose(0, 2, 1, 3, 4)
    yh, yl = halves(y.reshape(256, 128))

    g = np.arange(GX)
    first = 3 * (g // 2) + g % 2
    kx = first[:, None] + np.arange(2)[None, :]
    phase = fx[kx][:, :, None] * np.arange(NX)[None, None, :] % NX * (2 * np.pi / NX)
    both = np.stack([np.cos(phase), np.sin(phase)])
    both = both.reshape(2, GX, 2, GX, 8)
    eye = np.eye(2)
    ax = np.einsum("egtsx,mn->egmtsnx", both, eye).reshape(256, 512)
    bx = np.einsum("egtsx,mn->esmxgnt", both, eye).reshape(1024, 128)
    axh, axl = halves(ax)
    bxh, bxl = halves(bx)

    m = np.arange(64)
    kz_m = np.where(m < 48, m // 16, (m - 48) // 4)
    c_m = np.where(m < 48, m % 16, 16 + (m - 48) % 4)
    row = np.arange(120)
    sel_o = (row[None, :] // 6 == c_m[:, None]) & (row[None, :] % 6 // 2 == kz_m[:, None])
    row = np.arange(480)
    sel_c = (row[None, :] // 24 == c_m[:, None]) & (row[None, :] % 6 // 2 == kz_m[:, None])
    live = (m < 60)[:, None]
    sel_o = np.asarray((sel_o & live).astype(BF16))
    sel_c = np.asarray((sel_c & live).astype(BF16))
    return tz, yh, yl, axh, axl, bxh, bxl, sel_o, sel_c


def hops(k):
    return min(k // 4, 8 - k // 4) + min(k % 4, 4 - k % 4)


def iota(shape, axis):
    return lax.broadcasted_iota(jnp.int32, shape, axis)


def dot(a, b, dims):
    return lax.dot_general(a, b, dims, preferred_element_type=F32)


def split(x):
    high = x.astype(BF16)
    return high, (x - high.astype(F32)).astype(BF16)


def dot3(a, b, dims):
    return dot(a[0], b[0], dims) + dot(a[0], b[1], dims) + dot(a[1], b[0], dims)


def pick(sel, x):
    high, low = split(x)
    return dot(sel, high, NN) + dot(sel, low, NN)


def kernel(
    field, cot, w, pw, bias, tz, yh, yl, axh, axl, bxh, bxl, sel_o, sel_c,
    out, gf, gs, small,
    fs, cs, gh, gl, pw1, pw2, bb, pws, sy, ry, sx, rx, sp, rp, wf, tmp,
    u1, u2, d1, d2, q1, q2, lw, ls, lr, ms, mr, out_v, gf_v, gs_v, pv, fb, tz3,
    sy_sem, ry_sem, sx_sem, rx_sem, sp_sem, rp_sem, l_sem, o_sem,
):
    g = lax.axis_index("gx")
    yy = lax.axis_index("gy")
    even = lax.rem(g, 2) == 0

    barrier = pltpu.get_barrier_semaphore()

    def greet_y(k, _):
        pl.semaphore_signal(
            barrier, inc=1, device_id=(g, lax.rem(yy + k, GY)), device_id_type=MESH
        )
        return 0

    def greet_x(k, _):
        pl.semaphore_signal(
            barrier, inc=1, device_id=(lax.rem(g + k, GX), yy), device_id_type=MESH
        )
        return 0

    lax.fori_loop(1, GY, greet_y, 0)
    lax.fori_loop(1, GX, greet_x, 0)

    chip, core = yy // 2, lax.rem(yy, 2)
    others_y = [
        lax.rem(chip + n, 4) * 2 + (core if same else 1 - core)
        for n, same in ((2, 1), (2, 0), (1, 1), (3, 1), (1, 0), (3, 0), (0, 0))
    ]

    def send_y(st, h):
        sem_s, sem_r = sy_sem.at[2 * st + h], ry_sem.at[2 * st + h]
        own = pl.ds(yy * 32 + h * 16, 16)
        for d in others_y:
            pltpu.make_async_remote_copy(
                src_ref=sy.at[st, :, pl.ds(d * 32 + h * 16, 16), :],
                dst_ref=ry.at[st, :, own, :],
                send_sem=sem_s,
                recv_sem=sem_r,
                device_id=(g, d),
                device_id_type=MESH,
            ).start()
        pltpu.make_async_copy(sy.at[st, :, own, :], ry.at[st, :, own, :], sem_r).start()

    def send_y_tiles(st):
        own = pl.ds(yy * 32 + 16, 16)
        for t in range(4):
            sem = 8 + st * 2 + t
            for d in others_y:
                pltpu.make_async_remote_copy(
                    src_ref=sy.at[st, t, pl.ds(d * 32 + 16, 16), :],
                    dst_ref=ry.at[st, t, own, :],
                    send_sem=sy_sem.at[sem],
                    recv_sem=ry_sem.at[sem],
                    device_id=(g, d),
                    device_id_type=MESH,
                ).start()
            pltpu.make_async_copy(
                sy.at[st, t, own, :], ry.at[st, t, own, :], ry_sem.at[sem]
            ).start()

    def landed_y(st, h):
        landed(ry.at[st, :, pl.ds(0, 128), :], ry_sem.at[2 * st + h])

    gz, gw = g // 4, lax.rem(g, 4)
    far_first = sorted(range(1, GX), key=hops, reverse=True)

    def place(z, w):
        return w * 8 + z

    def send_gx(src, dst, ssem, rsem, size, to_owner):
        mine = place(gz, gw)
        to = g if to_owner else mine
        for k in far_first:
            z, w = lax.rem(gz + k // 4, 8), lax.rem(gw + k % 4, 4)
            at = place(z, w) if to_owner else z * 4 + w
            pltpu.make_async_remote_copy(
                src_ref=src.at[pl.ds(at * size, size)],
                dst_ref=dst.at[pl.ds(to * size, size)],
                send_sem=ssem,
                recv_sem=rsem,
                device_id=(z * 4 + w, yy),
                device_id_type=MESH,
            ).start()
        own = mine if to_owner else g
        pltpu.make_async_copy(
            src.at[pl.ds(own * size, size)], dst.at[pl.ds(to * size, size)], rsem
        ).start()

    def send_x(st):
        send_gx(sx.at[st], rx.at[st], sx_sem.at[st], rx_sem.at[st], 16, False)

    def send_p(st):
        send_gx(sp.at[st], rp.at[st], sp_sem.at[st], rp_sem.at[st], 1, st % 2 == 1)

    def send_x_tile(st, t):
        own = pl.ds(g * 16, 16)

        def remote(z, at):
            pltpu.make_async_remote_copy(
                src_ref=sx.at[st, at],
                dst_ref=rx.at[st, own],
                send_sem=sx_sem.at[st],
                recv_sem=rx_sem.at[st],
                device_id=(z * 4 + t, yy),
                device_id_type=MESH,
            ).start()

        for n in (4, 3, 5, 2, 6, 1, 7):
            z = lax.rem(gz + n, 8)
            remote(z, pl.ds(place(z, t) * 16, 16))
        at = pl.ds(place(gz, t) * 16, 16)

        @pl.when(gw != t)
        def _():
            remote(gz, at)

        @pl.when(gw == t)
        def _():
            pltpu.make_async_copy(sx.at[st, at], rx.at[st, own], rx_sem.at[st]).start()

    def landed(ref, sem):
        pltpu.make_async_copy(ref, ref, sem).wait()

    lane = iota((64, 128), 1)

    def widen(c, _):
        rows = pl.ds(c * 128, 128)
        v = field[c].astype(F32).reshape(128, 256)
        fs[0, rows, :] = v[:, :128]
        fs[1, rows, :] = v[:, 128:]
        return 0

    lax.fori_loop(0, C, widen, 0, unroll=4)

    def rows_of(ref, y):
        rows = pl.ds(y, 160, stride=16)
        return jnp.concatenate([ref[0, rows, :], ref[1, rows, :]], axis=1)

    pad_rows = jnp.zeros((96, 256), BF16)

    def analyze_z(st, h, y, s):
        for r in range(2):
            rows = pl.ds(h * 16 + r * 8 + y, 8, stride=32)
            tail = None
            for kz in range(3):
                at = (kz * 2 + r) * 8
                sy[st, kz, rows, :] = s[at : at + 8, :128]
                piece = s[at : at + 8, 128:]
                tail = piece if kz == 0 else tail + pltpu.roll(piece, 32 * kz, 1)
            sy[st, 3, rows, :] = tail

    def synthesize_z(st, h, y):
        main, tail = [], []
        for kz in range(3):
            for r in range(2):
                rows = pl.ds(h * 16 + r * 8 + y, 8, stride=32)
                main.append(ry[st, kz, rows, :])
                piece = ry[st, 3, rows, :]
                tail.append(piece if kz == 0 else pltpu.roll(piece, 128 - 32 * kz, 1))
        data = jnp.concatenate(
            [jnp.concatenate(main, axis=0), jnp.concatenate(tail, axis=0)], axis=1
        )
        high, low = split(data)
        data = jnp.concatenate([high, low, high], axis=0)
        return dot(data[:, 0:160], tz3[...], TN)

    tz3[0:48, :] = tz[0:48, :]
    tz3[48:96, :] = tz[0:48, :]
    tz3[96:144, :] = tz[48:96, :]

    def first_y(h, y, _):
        f = jnp.concatenate([rows_of(fs, h * 8 + y).astype(BF16), pad_rows], axis=0)
        s = dot(tz[...], f, NT)
        analyze_z(0, h, y, s[0:48] + s[48:96])
        return 0

    for h in range(2):
        lax.fori_loop(0, 8, functools.partial(first_y, h), 0, unroll=8)

    pl.semaphore_wait(barrier, GY - 1 + GX - 1)
    send_y(0, 0)
    send_y_tiles(0)

    def widen_more(c, _):
        rows = pl.ds(c * 128, 128)
        v = cot[c].astype(F32).reshape(128, 256)
        cs[0, rows, :] = v[:, :128]
        cs[1, rows, :] = v[:, 128:]
        wf[c, :, 0:72] = w[c].astype(F32).reshape(120, 72)
        return 0

    wf[...] = jnp.zeros_like(wf)
    lax.fori_loop(0, C, widen_more, 0, unroll=4)

    pws[...] = jnp.zeros_like(pws)
    pws[0:20, 0:20] = pw[...].astype(F32)
    pws[32:33, 0:20] = bias[...]
    ones_e = iota((160, 128), 0) // 8 == iota((160, 128), 1)
    ones_e = jnp.where(ones_e, 1.0, 0.0)
    e = ones_e[:, :32].astype(BF16)
    same_x = lax.rem(iota((160, 160), 0), 8) == lax.rem(iota((160, 160), 1), 8)
    m = pws[0:32, 0:32].astype(BF16)
    t = dot(e, m, NT).astype(BF16)
    pw1[...] = jnp.where(same_x, dot(t, e, NT), 0.0).astype(BF16)
    t = dot(e, m, NN).astype(BF16)
    pw2[...] = jnp.where(same_x, dot(t, e, NT), 0.0).astype(BF16)
    column = jnp.sum(ones_e * pws[32:33, :], axis=1, keepdims=True)
    bb[...] = jnp.broadcast_to(column, (160, 128))

    def forward_y(st):
        landed_y(st, 0)
        for t in range(4):
            landed(ry.at[st, t, pl.ds(0, 128), :], ry_sem.at[8 + st * 2 + t])
            data = split(jnp.transpose(ry[st, t]))
            sx[st, pl.ds(t * 128, 128), :] = dot3(data, (yh[...], yl[...]), NN)
            send_x_tile(st, t)

    def forward_x(st):
        p = dot3((axh[...], axl[...]), split(rx[st]), NN)
        pc, ps = p[:128], p[128:]
        side = iota((128, 128), 1) < 48
        o = pc + jnp.where(side, pltpu.roll(ps, 80, 1), -pltpu.roll(ps, 48, 1))
        sp[st] = o.reshape(32, 4, 128)

    def spectrum(st):
        tmp[...] = rp[st].reshape(128, 128)
        k0 = tmp[pl.ds(0, 64, stride=2), :]
        k1 = tmp[pl.ds(1, 64, stride=2), :]
        roll = lambda v, n: pltpu.roll(v, n, 1)
        re_e = jnp.where(lane < 48, k0, roll(k1, 48))
        im_e = jnp.where(lane < 48, roll(k0, 80), k1)
        re_o = jnp.where(lane < 24, roll(k0, 104), roll(k1, 24))
        im_o = jnp.where(lane < 24, roll(k0, 56), roll(k1, 104))
        live = lane < 72
        re = jnp.where(live, jnp.where(even, re_e, re_o), 0.0)
        im = jnp.where(live, jnp.where(even, im_e, im_o), 0.0)
        return re, im

    def modes(re, im, st):
        roll = lambda v, n: pltpu.roll(v, n, 1)
        within = lambda a, b: (lane >= a) & (lane < b)
        zero = jnp.zeros((64, 128), F32)
        e0 = jnp.where(lane < 48, re, jnp.where(within(48, 96), roll(im, 48), zero))
        e1 = jnp.where(lane < 24, roll(re, 80), jnp.where(within(48, 72), im, zero))
        o0 = jnp.where(
            within(24, 48), roll(re, 24), jnp.where(within(72, 96), roll(im, 72), zero)
        )
        o1 = jnp.where(lane < 48, roll(re, 104), jnp.where(within(48, 96), roll(im, 24), zero))
        tmp[pl.ds(0, 64, stride=2), :] = jnp.where(even, e0, o0)
        tmp[pl.ds(1, 64, stride=2), :] = jnp.where(even, e1, o1)
        sp[st] = tmp[...].reshape(32, 4, 128)

    def inverse_x(st):
        p = dot3((bxh[...], bxl[...]), split(rp[st].reshape(128, 128)), NN)
        pc, ps = p[:512], p[512:]
        side = iota((512, 128), 1) < 48
        sx[st] = pc + jnp.where(side, -pltpu.roll(ps, 80, 1), pltpu.roll(ps, 48, 1))

    def inverse_y(st):
        for t in range(4):
            data = split(rx[st, pl.ds(t * 128, 128), :])
            sy[st, t] = dot3((yh[...], yl[...]), data, NT)

    row64 = iota((64, 128), 0)
    zeroth = (row64 < 16) | ((row64 >= 48) & (row64 < 52))
    weight_z = jnp.where(zeroth & (yy == 0), 1.0 / CELLS, 2.0 / CELLS)

    forward_y(0)

    def ahead(y, _):
        f = rows_of(fs, y).astype(BF16)
        fb[y] = f
        pv[y] = dot(pw1[...], f, NN) + jnp.concatenate([bb[...], bb[...]], axis=1)
        return 0

    lax.fori_loop(0, 16, ahead, 0, unroll=2)
    landed(rx.at[0], rx_sem.at[0])
    forward_x(0)
    send_p(0)
    landed(rp.at[0], rp_sem.at[0])
    re, im = spectrum(0)
    for kz in range(3):
        for o in range(4):
            for r in range(2):
                at = o * 6 + kz * 2 + r
                sign = 1.0 if r == 0 else -1.0
                most = pl.ds(at, 16, stride=24)
                rest = pl.ds(16 * 24 + at, 4, stride=24)
                u1[most, :] = re[kz * 16 : kz * 16 + 16]
                u1[rest, :] = re[48 + kz * 4 : 52 + kz * 4]
                u2[most, :] = sign * im[kz * 16 : kz * 16 + 16]
                u2[rest, :] = sign * im[48 + kz * 4 : 52 + kz * 4]

    real_row = lax.rem(iota((24, 128), 0), 2) == 0

    def mix(c, acc):
        a, b = acc
        rows = pl.ds(c * 24, 24)
        s1, s2 = u1[rows, :], u2[rows, :]
        sa = jnp.concatenate([jnp.where(real_row, s1, s2)] * 5, axis=0)
        sb = jnp.concatenate([jnp.where(real_row, s2, s1)] * 5, axis=0)
        return a + wf[c] * sa, b + wf[c] * sb

    zero = jnp.zeros((120, 128), F32)
    a, b = lax.fori_loop(0, C, mix, (zero, zero), unroll=4)
    modes(pick(sel_o[...], a) * weight_z, pick(sel_o[...], b) * weight_z, 1)
    send_p(1)
    landed(rp.at[1], rp_sem.at[1])
    inverse_x(1)
    send_x(1)
    landed(rx.at[1], rx_sem.at[1])
    inverse_y(1)
    send_y(1, 0)
    send_y(1, 1)

    lw[...] = jnp.zeros_like(lw)
    ones_rows = jnp.ones((16, 256), BF16)

    def middle(h, y8, _):
        conv = synthesize_z(1, h, y8)
        y = h * 8 + y8
        f = fb[y]
        v = pv[y] + conv
        square = v * v
        t = jnp.tanh(v * (GELU_A + (GELU_A * GELU_B) * square))
        half = 0.5 + 0.5 * t
        act = v * half
        slope = half + act * (1.0 - half) * (2.0 * GELU_A + (6.0 * GELU_A * GELU_B) * square)
        grad = rows_of(cs, y) * slope
        rows = pl.ds(y, 160, stride=16)
        fs[0, rows, :] = act[:, :128]
        fs[1, rows, :] = act[:, 128:]
        high, low = split(grad)
        gh[y] = high
        gl[y] = low
        f = jnp.concatenate([tz[...], f, ones_rows], axis=0)
        p = dot(f, jnp.concatenate([high, pad_rows], axis=0), NT)
        f = jnp.concatenate([f[0:48], f[96:]], axis=0)
        n = dot(f, jnp.concatenate([low, pad_rows], axis=0), NT)
        lw[...] += p[96:] + n[48:]
        analyze_z(2, h, y8, p[0:48] + p[48:96] + n[0:48])
        return 0

    for h in range(2):
        landed_y(1, h)
        lax.fori_loop(0, 8, functools.partial(middle, h), 0, unroll=8)
        if h == 0:
            send_y(2, 0)
        else:
            send_y_tiles(2)

    row, col = iota((176, 160), 0), iota((176, 160), 1)
    keep = (row >= 160) | (lax.rem(row, 8) == lax.rem(col, 8))
    total = jnp.where(keep, lw[:, 0:160], 0.0)
    row, col = iota((32, 176), 0), iota((32, 176), 1)
    left = ((col < 160) & (col // 8 == row)) | ((row == 20) & (col == 160))
    left = jnp.where(left, 1.0, 0.0).astype(BF16)
    high, low = split(pick(left, total))
    e128 = ones_e.astype(BF16)
    ls[...] = dot(high, e128, NN) + dot(low, e128, NN)
    for k in range(1, GY):
        d = lax.rem(yy + k, GY)
        pltpu.make_async_remote_copy(
            src_ref=ls,
            dst_ref=lr.at[yy],
            send_sem=l_sem.at[0],
            recv_sem=l_sem.at[1],
            device_id=(g, d),
            device_id_type=MESH,
        ).start()
    pltpu.make_async_copy(ls, lr.at[yy], l_sem.at[1]).start()

    def write_out(c, _):
        rows = pl.ds(c * 128, 128)
        v = jnp.concatenate([fs[0, rows, :], fs[1, rows, :]], axis=1)
        out_v[c] = v.astype(BF16).reshape(8, 16, 256)
        return 0

    lax.fori_loop(0, C, write_out, 0, unroll=4)
    pltpu.make_async_copy(out_v, out, o_sem.at[0]).start()

    forward_y(2)

    landed(lr, l_sem.at[1])
    ms[...] = jnp.sum(lr[...], axis=0)

    def share(k, _):
        d = lax.rem(g + k, GX)
        pltpu.make_async_remote_copy(
            src_ref=ms,
            dst_ref=mr.at[g],
            send_sem=l_sem.at[2],
            recv_sem=l_sem.at[3],
            device_id=(d, yy),
            device_id_type=MESH,
        ).start()
        return 0

    lax.fori_loop(1, GX, share, 0)
    pltpu.make_async_copy(ms, mr.at[g], l_sem.at[3]).start()

    landed(rx.at[2], rx_sem.at[2])
    forward_x(2)
    send_p(2)
    landed(rp.at[2], rp_sem.at[2])
    re, im = spectrum(2)
    re, im = re * weight_z, im * weight_z
    for kz in range(3):
        for r in range(2):
            most = pl.ds(kz * 2 + r, 16, stride=6)
            rest = pl.ds(96 + kz * 2 + r, 4, stride=6)
            one, two = (re, im) if r == 0 else (im, re)
            d1[most, :] = one[kz * 16 : kz * 16 + 16]
            d1[rest, :] = one[48 + kz * 4 : 52 + kz * 4]
            d2[most, :] = two[kz * 16 : kz * 16 + 16]
            d2[rest, :] = two[48 + kz * 4 : 52 + kz * 4]

    even_row = lax.rem(iota((120, 128), 0), 2) == 0

    def unmix(c, _):
        rows = pl.ds(c * 24, 24)
        x1 = d1[...]
        x2 = jnp.where(even_row, d2[...], -d2[...])
        wc = wf[c]
        q1[rows, :] = jnp.sum((wc * x1).reshape(5, 24, 128), axis=0)
        q2[rows, :] = jnp.sum((wc * x2).reshape(5, 24, 128), axis=0)
        return 0

    lax.fori_loop(0, C, unmix, 0, unroll=4)
    modes(pick(sel_c[...], q1[...]), pick(sel_c[...], q2[...]), 3)
    send_p(3)

    def outer(c, _):
        rows = pl.ds(c * 24, 24)
        s1 = jnp.concatenate([u1[rows, :]] * 5, axis=0)
        s2 = jnp.concatenate([u2[rows, :]] * 5, axis=0)
        v = s1 * d1[...] + s2 * d2[...]
        gs_v[c] = v[:, 0:72].reshape(20, 3, 2, 72)
        return 0

    lax.fori_loop(0, C, outer, 0, unroll=2)
    pltpu.make_async_copy(gs_v, gs, o_sem.at[1]).start()

    landed(rp.at[3], rp_sem.at[3])
    inverse_x(3)
    send_x(3)

    def back_ahead(y, _):
        pv[y] = dot(pw2[...], gh[y], NN) + dot(pw2[...], gl[y], NN)
        return 0

    lax.fori_loop(0, 16, back_ahead, 0, unroll=2)
    landed(mr, l_sem.at[3])
    small[...] = jnp.sum(mr[...], axis=0) * (CELLS**-0.5)
    landed(rx.at[3], rx_sem.at[3])
    inverse_y(3)
    send_y(3, 0)
    send_y(3, 1)

    def last(h, y8, _):
        y = h * 8 + y8
        back = pv[y] + synthesize_z(3, h, y8)
        rows = pl.ds(y, 160, stride=16)
        cs[0, rows, :] = back[:, :128]
        cs[1, rows, :] = back[:, 128:]
        return 0

    for h in range(2):
        landed_y(3, h)
        lax.fori_loop(0, 8, functools.partial(last, h), 0, unroll=8)

    def write_grad(c, _):
        rows = pl.ds(c * 128, 128)
        v = jnp.concatenate([cs[0, rows, :], cs[1, rows, :]], axis=1)
        gf_v[c] = v.astype(BF16).reshape(8, 16, 256)
        return 0

    for n in range(4):
        lax.fori_loop(n * 5, n * 5 + 5, write_grad, 0, unroll=5)
        part = pl.ds(n * 5, 5)
        pltpu.make_async_copy(gf_v.at[part], gf.at[part], o_sem.at[2 + n]).start()

    for st in range(4):
        part = sy.at[st, :, pl.ds(0, 112), :]
        for h in range(2 if st % 2 == 1 else 1):
            pltpu.make_async_copy(part, part, sy_sem.at[2 * st + h]).wait()
        if st % 2 == 0:
            for t in range(4):
                part = sy.at[st, t, pl.ds(0, 112), :]
                pltpu.make_async_copy(part, part, sy_sem.at[8 + st * 2 + t]).wait()
        part = sx.at[st, pl.ds(0, 31 * 16)]
        pltpu.make_async_copy(part, part, sx_sem.at[st]).wait()
        part = sp.at[st, pl.ds(0, 31)]
        pltpu.make_async_copy(part, part, sp_sem.at[st]).wait()
    part = lr.at[pl.ds(0, 7)]
    pltpu.make_async_copy(part, part, l_sem.at[0]).wait()
    part = mr.at[pl.ds(0, 31)]
    pltpu.make_async_copy(part, part, l_sem.at[2]).wait()
    pltpu.make_async_copy(out_v, out, o_sem.at[0]).wait()
    pltpu.make_async_copy(gs_v, gs, o_sem.at[1]).wait()
    for n in range(4):
        part = pl.ds(n * 5, 5)
        pltpu.make_async_copy(gf_v.at[part], gf.at[part], o_sem.at[2 + n]).wait()


def deliver(out_a, gf_a, gs_a, small, out, gf, gs, gp, gb, out_v, gf_v, gs_v, sems):
    there, back = [], []
    for n in range(4):
        part = pl.ds(n * 5, 5)
        for i, (a, v, b) in enumerate(
            ((out_a, out_v, out), (gf_a, gf_v, gf), (gs_a, gs_v, gs))
        ):
            sem = n * 3 + i
            there.append(pltpu.make_async_copy(a.at[part], v.at[part], sems.at[sem]))
            back.append(pltpu.make_async_copy(v.at[part], b.at[part], sems.at[12 + sem]))
    for copy in there:
        copy.start()
    gp[...] = small[0:C, 0:C]
    gb[...] = small[C : C + 1, 0:C]
    for one, other in zip(there, back):
        one.wait()
        other.start()
    for copy in back:
        copy.wait()


def local(consts, field, cotangent, spectral_weight, pointwise_weight, bias):
    vmem = pl.BlockSpec(memory_space=pltpu.VMEM)
    anywhere = pl.BlockSpec(memory_space=pl.ANY)
    dma = pltpu.SemaphoreType.DMA
    weights = jnp.transpose(spectral_weight, (1, 2, 3, 0, 4))
    scratch = [
        pltpu.VMEM((2, 2560, 128), F32),
        pltpu.VMEM((2, 2560, 128), F32),
        pltpu.VMEM((16, 160, 256), BF16),
        pltpu.VMEM((16, 160, 256), BF16),
        pltpu.VMEM((160, 160), BF16),
        pltpu.VMEM((160, 160), BF16),
        pltpu.VMEM((160, 128), F32),
        pltpu.VMEM((40, 128), F32),
        pltpu.VMEM((4, 4, 256, 128), F32),
        pltpu.VMEM((4, 4, 256, 128), F32),
        pltpu.VMEM((4, 512, 128), F32),
        pltpu.VMEM((4, 512, 128), F32),
        pltpu.VMEM((4, 32, 4, 128), F32),
        pltpu.VMEM((4, 32, 4, 128), F32),
        pltpu.VMEM((20, 120, 128), F32),
        pltpu.VMEM((128, 128), F32),
        pltpu.VMEM((480, 128), F32),
        pltpu.VMEM((480, 128), F32),
        pltpu.VMEM((120, 128), F32),
        pltpu.VMEM((120, 128), F32),
        pltpu.VMEM((480, 128), F32),
        pltpu.VMEM((480, 128), F32),
        pltpu.VMEM((176, 256), F32),
        pltpu.VMEM((32, 128), F32),
        pltpu.VMEM((8, 32, 128), F32),
        pltpu.VMEM((32, 128), F32),
        pltpu.VMEM((32, 32, 128), F32),
        pltpu.VMEM((C, 8, 16, 256), BF16),
        pltpu.VMEM((C, 8, 16, 256), BF16),
        pltpu.VMEM((C, C, 3, 2, 72), F32),
        pltpu.VMEM((16, 160, 256), F32),
        pltpu.VMEM((16, 160, 256), BF16),
        pltpu.VMEM((144, 256), BF16),
        dma((16,)), dma((16,)), dma((4,)), dma((4,)), dma((4,)), dma((4,)), dma((4,)), dma((6,)),
    ]
    out, gf, gs, small = pl.pallas_call(
        kernel,
        out_shape=(
            jax.ShapeDtypeStruct((C, 8, 16, 256), BF16),
            jax.ShapeDtypeStruct((C, 8, 16, 256), BF16),
            jax.ShapeDtypeStruct((C, C, 3, 2, 72), F32),
            jax.ShapeDtypeStruct((32, 128), F32),
        ),
        in_specs=[vmem] * 14,
        out_specs=(anywhere,) * 3 + (vmem,),
        scratch_shapes=scratch,
        compiler_params=pltpu.CompilerParams(
            collective_id=0, has_side_effects=True, vmem_limit_bytes=58 << 20
        ),
        name="fourier_layer",
    )(field, cotangent, weights, pointwise_weight, bias.reshape(1, C), *consts)
    out, gf, gs, gp, gb = pl.pallas_call(
        deliver,
        out_shape=(
            jax.ShapeDtypeStruct((C, 8, 16, 256), BF16),
            jax.ShapeDtypeStruct((C, 8, 16, 256), BF16),
            jax.ShapeDtypeStruct((C, C, 3, 2, 72), F32),
            jax.ShapeDtypeStruct((C, C), F32),
            jax.ShapeDtypeStruct((1, C), F32),
        ),
        in_specs=[anywhere] * 3 + [vmem],
        out_specs=(anywhere,) * 3 + (vmem,) * 2,
        scratch_shapes=[
            pltpu.VMEM((C, 8, 16, 256), BF16),
            pltpu.VMEM((C, 8, 16, 256), BF16),
            pltpu.VMEM((C, C, 3, 2, 72), F32),
            dma((24,)),
        ],
        compiler_params=pltpu.CompilerParams(vmem_limit_bytes=58 << 20),
        name="deliver",
    )(out, gf, gs, small)
    return out, gf, jnp.transpose(gs, (3, 0, 1, 2, 4)), gp, gb.reshape(C)


def solution(mesh):
    consts = [jnp.asarray(t) for t in tables()]
    placed = (
        P(None, "gx", "gy", None),
        P(None, "gx", "gy", None),
        P(None, None, None, "gy", "gx"),
        P(),
        P(),
    )
    return jax.shard_map(
        functools.partial(local, consts),
        mesh=mesh,
        in_specs=placed,
        out_specs=placed,
        check_vma=False,
    )
```

```python
import functools

import jax
import jax.numpy as jnp
import numpy as np
from jax import lax
from jax.experimental import pallas as pl
from jax.experimental.pallas import tpu as pltpu
from jax.sharding import PartitionSpec as P

C = 20
NX, NY, NZ = 256, 128, 256
KX, KY, KZ = 48, 48, 24
GX, GY = 32, 8
CELLS = float(NX * NY * NZ)
F32 = jnp.float32
BF16 = jnp.bfloat16
MESH = pl.DeviceIdType.MESH
NN = (((1,), (0,)), ((), ()))
NT = (((1,), (1,)), ((), ()))
TN = (((0,), (0,)), ((), ()))
GELU_A = float(np.sqrt(2.0 / np.pi))
GELU_B = 0.044715


def halves(table):
    high = table.astype(BF16)
    low = (table - np.asarray(high, np.float64)).astype(BF16)
    return np.asarray(high), np.asarray(low)


def tables():
    kz, r, d = np.meshgrid(np.arange(3), np.arange(2), np.arange(8), indexing="ij")
    depth = (d * 3 + kz).reshape(-1, 1) * np.arange(NZ)[None, :] % NZ * (2 * np.pi / NZ)
    tz = np.where(r.reshape(-1, 1) == 0, np.cos(depth), -np.sin(depth))
    tz = np.concatenate(halves(tz), axis=0)

    fx = np.where(np.arange(KX) < 24, np.arange(KX), np.arange(KX) - 48 + NX)
    fy = np.where(np.arange(KY) < 24, np.arange(KY), np.arange(KY) - 48 + NY)
    phase = np.arange(NY)[:, None] * fy[None, :] % NY * (2 * np.pi / NY)
    cos, sin = np.cos(phase).reshape(8, 16, KY), np.sin(phase).reshape(8, 16, KY)
    y = np.zeros((8, 2, 16, 128))
    y[:, 0, :, 0:48], y[:, 0, :, 48:96] = cos, -sin
    y[:, 1, :, 0:48], y[:, 1, :, 48:96] = sin, cos
    y = y.reshape(8, 2, 2, 8, 128).transpose(0, 2, 1, 3, 4)
    yh, yl = halves(y.reshape(256, 128))

    g = np.arange(GX)
    first = 3 * (g // 2) + g % 2
    kx = first[:, None] + np.arange(2)[None, :]
    phase = fx[kx][:, :, None] * np.arange(NX)[None, None, :] % NX * (2 * np.pi / NX)
    both = np.stack([np.cos(phase), np.sin(phase)])
    both = both.reshape(2, GX, 2, GX, 8)
    eye = np.eye(2)
    ax = np.einsum("egtsx,mn->egmtsnx", both, eye).reshape(256, 512)
    bx = np.einsum("egtsx,mn->esmxgnt", both, eye).reshape(1024, 128)
    axh, axl = halves(ax)
    bxh, bxl = halves(bx)

    m = np.arange(64)
    kz_m = np.where(m < 48, m // 16, (m - 48) // 4)
    c_m = np.where(m < 48, m % 16, 16 + (m - 48) % 4)
    row = np.arange(120)
    sel_o = (row[None, :] // 6 == c_m[:, None]) & (row[None, :] % 6 // 2 == kz_m[:, None])
    row = np.arange(480)
    sel_c = (row[None, :] // 24 == c_m[:, None]) & (row[None, :] % 6 // 2 == kz_m[:, None])
    live = (m < 60)[:, None]
    sel_o = np.asarray((sel_o & live).astype(BF16))
    sel_c = np.asarray((sel_c & live).astype(BF16))
    return tz, yh, yl, axh, axl, bxh, bxl, sel_o, sel_c


def hops(k):
    return min(k // 4, 8 - k // 4) + min(k % 4, 4 - k % 4)


def iota(shape, axis):
    return lax.broadcasted_iota(jnp.int32, shape, axis)


def dot(a, b, dims):
    return lax.dot_general(a, b, dims, preferred_element_type=F32)


def split(x):
    high = x.astype(BF16)
    return high, (x - high.astype(F32)).astype(BF16)


def dot3(a, b, dims):
    return dot(a[0], b[0], dims) + dot(a[0], b[1], dims) + dot(a[1], b[0], dims)


def pick(sel, x):
    high, low = split(x)
    return dot(sel, high, NN) + dot(sel, low, NN)


def kernel(
    field, cot, w, pw, bias, tz, yh, yl, axh, axl, bxh, bxl, sel_o, sel_c,
    out, gf, gs, small,
    fs, cs, gh, gl, pw1, pw2, bb, pws, sy, ry, sx, rx, sp, rp, wf, tmp,
    u1, u2, d1, d2, q1, q2, lw, ls, lr, ms, mr, out_v, gf_v, gs_v, pv, fb, tz3,
    sy_sem, ry_sem, sx_sem, rx_sem, sp_sem, rp_sem, l_sem, o_sem,
):
    g = lax.axis_index("gx")
    yy = lax.axis_index("gy")
    even = lax.rem(g, 2) == 0

    barrier = pltpu.get_barrier_semaphore()

    def greet_y(k, _):
        pl.semaphore_signal(
            barrier, inc=1, device_id=(g, lax.rem(yy + k, GY)), device_id_type=MESH
        )
        return 0

    def greet_x(k, _):
        pl.semaphore_signal(
            barrier, inc=1, device_id=(lax.rem(g + k, GX), yy), device_id_type=MESH
        )
        return 0

    lax.fori_loop(1, GY, greet_y, 0)
    lax.fori_loop(1, GX, greet_x, 0)

    chip, core = yy // 2, lax.rem(yy, 2)
    others_y = [
        lax.rem(chip + n, 4) * 2 + (core if same else 1 - core)
        for n, same in ((2, 1), (2, 0), (1, 1), (3, 1), (1, 0), (3, 0), (0, 0))
    ]

    def send_y(st, h):
        sem_s, sem_r = sy_sem.at[2 * st + h], ry_sem.at[2 * st + h]
        own = pl.ds(yy * 32 + h * 16, 16)
        for d in others_y:
            pltpu.make_async_remote_copy(
                src_ref=sy.at[st, :, pl.ds(d * 32 + h * 16, 16), :],
                dst_ref=ry.at[st, :, own, :],
                send_sem=sem_s,
                recv_sem=sem_r,
                device_id=(g, d),
                device_id_type=MESH,
            ).start()
        pltpu.make_async_copy(sy.at[st, :, own, :], ry.at[st, :, own, :], sem_r).start()

    def send_y_tiles(st):
        own = pl.ds(yy * 32 + 16, 16)
        for t in range(4):
            sem = 8 + st * 2 + t
            for d in others_y:
                pltpu.make_async_remote_copy(
                    src_ref=sy.at[st, t, pl.ds(d * 32 + 16, 16), :],
                    dst_ref=ry.at[st, t, own, :],
                    send_sem=sy_sem.at[sem],
                    recv_sem=ry_sem.at[sem],
                    device_id=(g, d),
                    device_id_type=MESH,
                ).start()
            pltpu.make_async_copy(
                sy.at[st, t, own, :], ry.at[st, t, own, :], ry_sem.at[sem]
            ).start()

    def landed_y(st, h):
        landed(ry.at[st, :, pl.ds(0, 128), :], ry_sem.at[2 * st + h])

    gz, gw = g // 4, lax.rem(g, 4)
    far_first = sorted(range(1, GX), key=hops, reverse=True)

    def place(z, w):
        return w * 8 + z

    def send_gx(src, dst, ssem, rsem, size, to_owner):
        mine = place(gz, gw)
        to = g if to_owner else mine
        for k in far_first:
            z, w = lax.rem(gz + k // 4, 8), lax.rem(gw + k % 4, 4)
            at = place(z, w) if to_owner else z * 4 + w
            pltpu.make_async_remote_copy(
                src_ref=src.at[pl.ds(at * size, size)],
                dst_ref=dst.at[pl.ds(to * size, size)],
                send_sem=ssem,
                recv_sem=rsem,
                device_id=(z * 4 + w, yy),
                device_id_type=MESH,
            ).start()
        own = mine if to_owner else g
        pltpu.make_async_copy(
            src.at[pl.ds(own * size, size)], dst.at[pl.ds(to * size, size)], rsem
        ).start()

    def send_x(st):
        send_gx(sx.at[st], rx.at[st], sx_sem.at[st], rx_sem.at[st], 16, False)

    def send_p(st):
        send_gx(sp.at[st], rp.at[st], sp_sem.at[st], rp_sem.at[st], 1, st % 2 == 1)

    def send_x_tile(st, t):
        own = pl.ds(g * 16, 16)

        def remote(z, at):
            pltpu.make_async_remote_copy(
                src_ref=sx.at[st, at],
                dst_ref=rx.at[st, own],
                send_sem=sx_sem.at[st],
                recv_sem=rx_sem.at[st],
                device_id=(z * 4 + t, yy),
                device_id_type=MESH,
            ).start()

        for n in (4, 3, 5, 2, 6, 1, 7):
            z = lax.rem(gz + n, 8)
            remote(z, pl.ds(place(z, t) * 16, 16))
        at = pl.ds(place(gz, t) * 16, 16)

        @pl.when(gw != t)
        def _():
            remote(gz, at)

        @pl.when(gw == t)
        def _():
            pltpu.make_async_copy(sx.at[st, at], rx.at[st, own], rx_sem.at[st]).start()

    def landed(ref, sem):
        pltpu.make_async_copy(ref, ref, sem).wait()

    lane = iota((64, 128), 1)

    def widen(c, _):
        rows = pl.ds(c * 128, 128)
        v = field[c].astype(F32).reshape(128, 256)
        fs[0, rows, :] = v[:, :128]
        fs[1, rows, :] = v[:, 128:]
        return 0

    lax.fori_loop(0, C, widen, 0, unroll=4)

    def rows_of(ref, y):
        rows = pl.ds(y, 160, stride=16)
        return jnp.concatenate([ref[0, rows, :], ref[1, rows, :]], axis=1)

    pad_rows = jnp.zeros((96, 256), BF16)

    def analyze_z(st, h, y, s):
        for r in range(2):
            rows = pl.ds(h * 16 + r * 8 + y, 8, stride=32)
            tail = None
            for kz in range(3):
                at = (kz * 2 + r) * 8
                sy[st, kz, rows, :] = s[at : at + 8, :128]
                piece = s[at : at + 8, 128:]
                tail = piece if kz == 0 else tail + pltpu.roll(piece, 32 * kz, 1)
            sy[st, 3, rows, :] = tail

    def synthesize_z(st, h, y):
        main, tail = [], []
        for kz in range(3):
            for r in range(2):
                rows = pl.ds(h * 16 + r * 8 + y, 8, stride=32)
                main.append(ry[st, kz, rows, :])
                piece = ry[st, 3, rows, :]
                tail.append(piece if kz == 0 else pltpu.roll(piece, 128 - 32 * kz, 1))
        data = jnp.concatenate(
            [jnp.concatenate(main, axis=0), jnp.concatenate(tail, axis=0)], axis=1
        )
        high, low = split(data)
        data = jnp.concatenate([high, low, high], axis=0)
        return dot(data[:, 0:160], tz3[...], TN)

    tz3[0:48, :] = tz[0:48, :]
    tz3[48:96, :] = tz[0:48, :]
    tz3[96:144, :] = tz[48:96, :]

    def first_y(h, y, _):
        f = jnp.concatenate([rows_of(fs, h * 8 + y).astype(BF16), pad_rows], axis=0)
        s = dot(tz[...], f, NT)
        analyze_z(0, h, y, s[0:48] + s[48:96])
        return 0

    for h in range(2):
        lax.fori_loop(0, 8, functools.partial(first_y, h), 0, unroll=8)

    pl.semaphore_wait(barrier, GY - 1 + GX - 1)
    send_y(0, 0)
    send_y_tiles(0)

    def widen_more(c, _):
        rows = pl.ds(c * 128, 128)
        v = cot[c].astype(F32).reshape(128, 256)
        cs[0, rows, :] = v[:, :128]
        cs[1, rows, :] = v[:, 128:]
        wf[c, :, 0:72] = w[c].astype(F32).reshape(120, 72)
        return 0

    wf[...] = jnp.zeros_like(wf)
    lax.fori_loop(0, C, widen_more, 0, unroll=4)

    pws[...] = jnp.zeros_like(pws)
    pws[0:20, 0:20] = pw[...].astype(F32)
    pws[32:33, 0:20] = bias[...]
    ones_e = iota((160, 128), 0) // 8 == iota((160, 128), 1)
    ones_e = jnp.where(ones_e, 1.0, 0.0)
    e = ones_e[:, :32].astype(BF16)
    same_x = lax.rem(iota((160, 160), 0), 8) == lax.rem(iota((160, 160), 1), 8)
    m = pws[0:32, 0:32].astype(BF16)
    t = dot(e, m, NT).astype(BF16)
    pw1[...] = jnp.where(same_x, dot(t, e, NT), 0.0).astype(BF16)
    t = dot(e, m, NN).astype(BF16)
    pw2[...] = jnp.where(same_x, dot(t, e, NT), 0.0).astype(BF16)
    column = jnp.sum(ones_e * pws[32:33, :], axis=1, keepdims=True)
    bb[...] = jnp.broadcast_to(column, (160, 128))

    def forward_y(st):
        landed_y(st, 0)
        for t in range(4):
            landed(ry.at[st, t, pl.ds(0, 128), :], ry_sem.at[8 + st * 2 + t])
            data = split(jnp.transpose(ry[st, t]))
            sx[st, pl.ds(t * 128, 128), :] = dot3(data, (yh[...], yl[...]), NN)
            send_x_tile(st, t)

    def forward_x(st):
        p = dot3((axh[...], axl[...]), split(rx[st]), NN)
        pc, ps = p[:128], p[128:]
        side = iota((128, 128), 1) < 48
        o = pc + jnp.where(side, pltpu.roll(ps, 80, 1), -pltpu.roll(ps, 48, 1))
        sp[st] = o.reshape(32, 4, 128)

    def spectrum(st):
        tmp[...] = rp[st].reshape(128, 128)
        k0 = tmp[pl.ds(0, 64, stride=2), :]
        k1 = tmp[pl.ds(1, 64, stride=2), :]
        roll = lambda v, n: pltpu.roll(v, n, 1)
        re_e = jnp.where(lane < 48, k0, roll(k1, 48))
        im_e = jnp.where(lane < 48, roll(k0, 80), k1)
        re_o = jnp.where(lane < 24, roll(k0, 104), roll(k1, 24))
        im_o = jnp.where(lane < 24, roll(k0, 56), roll(k1, 104))
        live = lane < 72
        re = jnp.where(live, jnp.where(even, re_e, re_o), 0.0)
        im = jnp.where(live, jnp.where(even, im_e, im_o), 0.0)
        return re, im

    def modes(re, im, st):
        roll = lambda v, n: pltpu.roll(v, n, 1)
        within = lambda a, b: (lane >= a) & (lane < b)
        zero = jnp.zeros((64, 128), F32)
        e0 = jnp.where(lane < 48, re, jnp.where(within(48, 96), roll(im, 48), zero))
        e1 = jnp.where(lane < 24, roll(re, 80), jnp.where(within(48, 72), im, zero))
        o0 = jnp.where(
            within(24, 48), roll(re, 24), jnp.where(within(72, 96), roll(im, 72), zero)
        )
        o1 = jnp.where(lane < 48, roll(re, 104), jnp.where(within(48, 96), roll(im, 24), zero))
        tmp[pl.ds(0, 64, stride=2), :] = jnp.where(even, e0, o0)
        tmp[pl.ds(1, 64, stride=2), :] = jnp.where(even, e1, o1)
        sp[st] = tmp[...].reshape(32, 4, 128)

    def inverse_x(st):
        p = dot3((bxh[...], bxl[...]), split(rp[st].reshape(128, 128)), NN)
        pc, ps = p[:512], p[512:]
        side = iota((512, 128), 1) < 48
        sx[st] = pc + jnp.where(side, -pltpu.roll(ps, 80, 1), pltpu.roll(ps, 48, 1))

    def inverse_y(st):
        for t in range(4):
            data = split(rx[st, pl.ds(t * 128, 128), :])
            sy[st, t] = dot3((yh[...], yl[...]), data, NT)

    row64 = iota((64, 128), 0)
    zeroth = (row64 < 16) | ((row64 >= 48) & (row64 < 52))
    weight_z = jnp.where(zeroth & (yy == 0), 1.0 / CELLS, 2.0 / CELLS)

    forward_y(0)

    def ahead(y, _):
        f = rows_of(fs, y).astype(BF16)
        fb[y] = f
        pv[y] = dot(pw1[...], f, NN) + jnp.concatenate([bb[...], bb[...]], axis=1)
        return 0

    lax.fori_loop(0, 16, ahead, 0, unroll=2)
    landed(rx.at[0], rx_sem.at[0])
    forward_x(0)
    send_p(0)
    landed(rp.at[0], rp_sem.at[0])
    re, im = spectrum(0)
    for kz in range(3):
        for o in range(4):
            for r in range(2):
                at = o * 6 + kz * 2 + r
                sign = 1.0 if r == 0 else -1.0
                most = pl.ds(at, 16, stride=24)
                rest = pl.ds(16 * 24 + at, 4, stride=24)
                u1[most, :] = re[kz * 16 : kz * 16 + 16]
                u1[rest, :] = re[48 + kz * 4 : 52 + kz * 4]
                u2[most, :] = sign * im[kz * 16 : kz * 16 + 16]
                u2[rest, :] = sign * im[48 + kz * 4 : 52 + kz * 4]

    real_row = lax.rem(iota((24, 128), 0), 2) == 0

    def mix(c, acc):
        a, b = acc
        rows = pl.ds(c * 24, 24)
        s1, s2 = u1[rows, :], u2[rows, :]
        sa = jnp.concatenate([jnp.where(real_row, s1, s2)] * 5, axis=0)
        sb = jnp.concatenate([jnp.where(real_row, s2, s1)] * 5, axis=0)
        return a + wf[c] * sa, b + wf[c] * sb

    zero = jnp.zeros((120, 128), F32)
    a, b = lax.fori_loop(0, C, mix, (zero, zero), unroll=4)
    modes(pick(sel_o[...], a) * weight_z, pick(sel_o[...], b) * weight_z, 1)
    send_p(1)
    landed(rp.at[1], rp_sem.at[1])
    inverse_x(1)
    send_x(1)
    landed(rx.at[1], rx_sem.at[1])
    inverse_y(1)
    send_y(1, 0)
    send_y(1, 1)

    lw[...] = jnp.zeros_like(lw)
    ones_rows = jnp.ones((16, 256), BF16)

    def middle(h, y8, _):
        conv = synthesize_z(1, h, y8)
        y = h * 8 + y8
        f = fb[y]
        v = pv[y] + conv
        square = v * v
        t = jnp.tanh(v * (GELU_A + (GELU_A * GELU_B) * square))
        half = 0.5 + 0.5 * t
        act = v * half
        slope = half + act * (1.0 - half) * (2.0 * GELU_A + (6.0 * GELU_A * GELU_B) * square)
        grad = rows_of(cs, y) * slope
        rows = pl.ds(y, 160, stride=16)
        fs[0, rows, :] = act[:, :128]
        fs[1, rows, :] = act[:, 128:]
        high, low = split(grad)
        gh[y] = high
        gl[y] = low
        f = jnp.concatenate([tz[...], f, ones_rows], axis=0)
        p = dot(f, jnp.concatenate([high, pad_rows], axis=0), NT)
        f = jnp.concatenate([f[0:48], f[96:]], axis=0)
        n = dot(f, jnp.concatenate([low, pad_rows], axis=0), NT)
        lw[...] += p[96:] + n[48:]
        analyze_z(2, h, y8, p[0:48] + p[48:96] + n[0:48])
        return 0

    for h in range(2):
        landed_y(1, h)
        lax.fori_loop(0, 8, functools.partial(middle, h), 0, unroll=8)
        if h == 0:
            send_y(2, 0)
        else:
            send_y_tiles(2)

    row, col = iota((176, 160), 0), iota((176, 160), 1)
    keep = (row >= 160) | (lax.rem(row, 8) == lax.rem(col, 8))
    total = jnp.where(keep, lw[:, 0:160], 0.0)
    row, col = iota((32, 176), 0), iota((32, 176), 1)
    left = ((col < 160) & (col // 8 == row)) | ((row == 20) & (col == 160))
    left = jnp.where(left, 1.0, 0.0).astype(BF16)
    high, low = split(pick(left, total))
    e128 = ones_e.astype(BF16)
    packed = dot(high, e128, NN) + dot(low, e128, NN)
    ls[...] = packed[0:8] + pltpu.roll(packed[8:16], 32, 1) + pltpu.roll(packed[16:24], 64, 1)
    for k in range(1, GY):
        d = lax.rem(yy + k, GY)
        pltpu.make_async_remote_copy(
            src_ref=ls,
            dst_ref=lr.at[yy],
            send_sem=l_sem.at[0],
            recv_sem=l_sem.at[1],
            device_id=(g, d),
            device_id_type=MESH,
        ).start()
    pltpu.make_async_copy(ls, lr.at[yy], l_sem.at[1]).start()

    forward_y(2)

    def write_out(c, _):
        rows = pl.ds(c * 128, 128)
        v = jnp.concatenate([fs[0, rows, :], fs[1, rows, :]], axis=1)
        out_v[c] = v.astype(BF16).reshape(8, 16, 256)
        return 0

    lax.fori_loop(0, C, write_out, 0, unroll=4)
    pltpu.make_async_copy(out_v, out, o_sem.at[0]).start()

    landed(rx.at[2], rx_sem.at[2])
    forward_x(2)
    send_p(2)
    landed(rp.at[2], rp_sem.at[2])
    re, im = spectrum(2)
    re, im = re * weight_z, im * weight_z
    for kz in range(3):
        for r in range(2):
            most = pl.ds(kz * 2 + r, 16, stride=6)
            rest = pl.ds(96 + kz * 2 + r, 4, stride=6)
            one, two = (re, im) if r == 0 else (im, re)
            d1[most, :] = one[kz * 16 : kz * 16 + 16]
            d1[rest, :] = one[48 + kz * 4 : 52 + kz * 4]
            d2[most, :] = two[kz * 16 : kz * 16 + 16]
            d2[rest, :] = two[48 + kz * 4 : 52 + kz * 4]

    even_row = lax.rem(iota((120, 128), 0), 2) == 0

    def unmix(c, _):
        rows = pl.ds(c * 24, 24)
        x1 = d1[...]
        x2 = jnp.where(even_row, d2[...], -d2[...])
        wc = wf[c]
        q1[rows, :] = jnp.sum((wc * x1).reshape(5, 24, 128), axis=0)
        q2[rows, :] = jnp.sum((wc * x2).reshape(5, 24, 128), axis=0)
        return 0

    lax.fori_loop(0, C, unmix, 0, unroll=4)
    modes(pick(sel_c[...], q1[...]), pick(sel_c[...], q2[...]), 3)
    send_p(3)

    def outer(c, _):
        rows = pl.ds(c * 24, 24)
        s1 = jnp.concatenate([u1[rows, :]] * 5, axis=0)
        s2 = jnp.concatenate([u2[rows, :]] * 5, axis=0)
        v = s1 * d1[...] + s2 * d2[...]
        gs_v[c] = v[:, 0:72].reshape(20, 3, 2, 72)
        return 0

    lax.fori_loop(0, C, outer, 0, unroll=2)
    pltpu.make_async_copy(gs_v, gs, o_sem.at[1]).start()

    landed(rp.at[3], rp_sem.at[3])
    inverse_x(3)
    send_x(3)

    def back_ahead(y, _):
        pv[y] = dot(pw2[...], gh[y], NN) + dot(pw2[...], gl[y], NN)
        return 0

    lax.fori_loop(0, 16, back_ahead, 0, unroll=2)
    landed(rx.at[3], rx_sem.at[3])
    inverse_y(3)
    send_y(3, 0)
    send_y(3, 1)

    landed(lr, l_sem.at[1])
    ms[...] = jnp.sum(lr[...], axis=0)

    def share(k, _):
        d = lax.rem(g + k, GX)
        pltpu.make_async_remote_copy(
            src_ref=ms,
            dst_ref=mr.at[g],
            send_sem=l_sem.at[2],
            recv_sem=l_sem.at[3],
            device_id=(d, yy),
            device_id_type=MESH,
        ).start()
        return 0

    lax.fori_loop(1, GX, share, 0)
    pltpu.make_async_copy(ms, mr.at[g], l_sem.at[3]).start()


    def last(h, y8, _):
        y = h * 8 + y8
        back = pv[y] + synthesize_z(3, h, y8)
        rows = pl.ds(y, 160, stride=16)
        cs[0, rows, :] = back[:, :128]
        cs[1, rows, :] = back[:, 128:]
        return 0

    for h in range(2):
        landed_y(3, h)
        lax.fori_loop(0, 8, functools.partial(last, h), 0, unroll=8)

    def write_grad(c, _):
        rows = pl.ds(c * 128, 128)
        v = jnp.concatenate([cs[0, rows, :], cs[1, rows, :]], axis=1)
        gf_v[c] = v.astype(BF16).reshape(8, 16, 256)
        return 0

    landed(mr, l_sem.at[3])
    sums = jnp.sum(mr[...], axis=0) * (CELLS**-0.5)
    small[0:8, :] = sums
    small[8:16, :] = pltpu.roll(sums, 96, 1)
    small[16:24, :] = pltpu.roll(sums, 64, 1)

    for n in range(4):
        lax.fori_loop(n * 5, n * 5 + 5, write_grad, 0, unroll=5)
        part = pl.ds(n * 5, 5)
        pltpu.make_async_copy(gf_v.at[part], gf.at[part], o_sem.at[2 + n]).start()

    for st in range(4):
        part = sy.at[st, :, pl.ds(0, 112), :]
        for h in range(2 if st % 2 == 1 else 1):
            pltpu.make_async_copy(part, part, sy_sem.at[2 * st + h]).wait()
        if st % 2 == 0:
            for t in range(4):
                part = sy.at[st, t, pl.ds(0, 112), :]
                pltpu.make_async_copy(part, part, sy_sem.at[8 + st * 2 + t]).wait()
        part = sx.at[st, pl.ds(0, 31 * 16)]
        pltpu.make_async_copy(part, part, sx_sem.at[st]).wait()
        part = sp.at[st, pl.ds(0, 31)]
        pltpu.make_async_copy(part, part, sp_sem.at[st]).wait()
    part = lr.at[pl.ds(0, 7)]
    pltpu.make_async_copy(part, part, l_sem.at[0]).wait()
    part = mr.at[pl.ds(0, 31)]
    pltpu.make_async_copy(part, part, l_sem.at[2]).wait()
    pltpu.make_async_copy(out_v, out, o_sem.at[0]).wait()
    pltpu.make_async_copy(gs_v, gs, o_sem.at[1]).wait()
    for n in range(4):
        part = pl.ds(n * 5, 5)
        pltpu.make_async_copy(gf_v.at[part], gf.at[part], o_sem.at[2 + n]).wait()


def deliver(out_a, gf_a, gs_a, small, out, gf, gs, gp, gb, out_v, gf_v, gs_v, sems):
    there, back = [], []
    for n in range(4):
        part = pl.ds(n * 5, 5)
        for i, (a, v, b) in enumerate(
            ((out_a, out_v, out), (gf_a, gf_v, gf), (gs_a, gs_v, gs))
        ):
            sem = n * 3 + i
            there.append(pltpu.make_async_copy(a.at[part], v.at[part], sems.at[sem]))
            back.append(pltpu.make_async_copy(v.at[part], b.at[part], sems.at[12 + sem]))
    for copy in there:
        copy.start()
    gp[...] = small[0:C, 0:C]
    gb[...] = small[C : C + 1, 0:C]
    for one, other in zip(there, back):
        one.wait()
        other.start()
    for copy in back:
        copy.wait()


def local(consts, field, cotangent, spectral_weight, pointwise_weight, bias):
    vmem = pl.BlockSpec(memory_space=pltpu.VMEM)
    anywhere = pl.BlockSpec(memory_space=pl.ANY)
    dma = pltpu.SemaphoreType.DMA
    weights = jnp.transpose(spectral_weight, (1, 2, 3, 0, 4))
    scratch = [
        pltpu.VMEM((2, 2560, 128), F32),
        pltpu.VMEM((2, 2560, 128), F32),
        pltpu.VMEM((16, 160, 256), BF16),
        pltpu.VMEM((16, 160, 256), BF16),
        pltpu.VMEM((160, 160), BF16),
        pltpu.VMEM((160, 160), BF16),
        pltpu.VMEM((160, 128), F32),
        pltpu.VMEM((40, 128), F32),
        pltpu.VMEM((4, 4, 256, 128), F32),
        pltpu.VMEM((4, 4, 256, 128), F32),
        pltpu.VMEM((4, 512, 128), F32),
        pltpu.VMEM((4, 512, 128), F32),
        pltpu.VMEM((4, 32, 4, 128), F32),
        pltpu.VMEM((4, 32, 4, 128), F32),
        pltpu.VMEM((20, 120, 128), F32),
        pltpu.VMEM((128, 128), F32),
        pltpu.VMEM((480, 128), F32),
        pltpu.VMEM((480, 128), F32),
        pltpu.VMEM((120, 128), F32),
        pltpu.VMEM((120, 128), F32),
        pltpu.VMEM((480, 128), F32),
        pltpu.VMEM((480, 128), F32),
        pltpu.VMEM((176, 256), F32),
        pltpu.VMEM((8, 128), F32),
        pltpu.VMEM((8, 8, 128), F32),
        pltpu.VMEM((8, 128), F32),
        pltpu.VMEM((32, 8, 128), F32),
        pltpu.VMEM((C, 8, 16, 256), BF16),
        pltpu.VMEM((C, 8, 16, 256), BF16),
        pltpu.VMEM((C, C, 3, 2, 72), F32),
        pltpu.VMEM((16, 160, 256), F32),
        pltpu.VMEM((16, 160, 256), BF16),
        pltpu.VMEM((144, 256), BF16),
        dma((16,)), dma((16,)), dma((4,)), dma((4,)), dma((4,)), dma((4,)), dma((4,)), dma((6,)),
    ]
    out, gf, gs, small = pl.pallas_call(
        kernel,
        out_shape=(
            jax.ShapeDtypeStruct((C, 8, 16, 256), BF16),
            jax.ShapeDtypeStruct((C, 8, 16, 256), BF16),
            jax.ShapeDtypeStruct((C, C, 3, 2, 72), F32),
            jax.ShapeDtypeStruct((24, 128), F32),
        ),
        in_specs=[vmem] * 14,
        out_specs=(anywhere,) * 3 + (vmem,),
        scratch_shapes=scratch,
        compiler_params=pltpu.CompilerParams(
            collective_id=0, has_side_effects=True, vmem_limit_bytes=58 << 20
        ),
        name="fourier_layer",
    )(field, cotangent, weights, pointwise_weight, bias.reshape(1, C), *consts)
    out, gf, gs, gp, gb = pl.pallas_call(
        deliver,
        out_shape=(
            jax.ShapeDtypeStruct((C, 8, 16, 256), BF16),
            jax.ShapeDtypeStruct((C, 8, 16, 256), BF16),
            jax.ShapeDtypeStruct((C, C, 3, 2, 72), F32),
            jax.ShapeDtypeStruct((C, C), F32),
            jax.ShapeDtypeStruct((1, C), F32),
        ),
        in_specs=[anywhere] * 3 + [vmem],
        out_specs=(anywhere,) * 3 + (vmem,) * 2,
        scratch_shapes=[
            pltpu.VMEM((C, 8, 16, 256), BF16),
            pltpu.VMEM((C, 8, 16, 256), BF16),
            pltpu.VMEM((C, C, 3, 2, 72), F32),
            dma((24,)),
        ],
        compiler_params=pltpu.CompilerParams(vmem_limit_bytes=58 << 20),
        name="deliver",
    )(out, gf, gs, small)
    return out, gf, jnp.transpose(gs, (3, 0, 1, 2, 4)), gp, gb.reshape(C)


def solution(mesh):
    consts = [jnp.asarray(t) for t in tables()]
    placed = (
        P(None, "gx", "gy", None),
        P(None, "gx", "gy", None),
        P(None, None, None, "gy", "gx"),
        P(),
        P(),
    )
    return jax.shard_map(
        functools.partial(local, consts),
        mesh=mesh,
        in_specs=placed,
        out_specs=placed,
        check_vma=False,
    )
```

```python
import functools

import jax
import jax.numpy as jnp
import numpy as np
from jax import lax
from jax.experimental import pallas as pl
from jax.experimental.pallas import tpu as pltpu
from jax.sharding import PartitionSpec as P

C = 20
NX, NY, NZ = 256, 128, 256
KX, KY, KZ = 48, 48, 24
GX, GY = 32, 8
CELLS = float(NX * NY * NZ)
F32 = jnp.float32
BF16 = jnp.bfloat16
MESH = pl.DeviceIdType.MESH
NN = (((1,), (0,)), ((), ()))
NT = (((1,), (1,)), ((), ()))
TN = (((0,), (0,)), ((), ()))
GELU_A = float(np.sqrt(2.0 / np.pi))
GELU_B = 0.044715


def halves(table):
    high = table.astype(BF16)
    low = (table - np.asarray(high, np.float64)).astype(BF16)
    return np.asarray(high), np.asarray(low)


def tables():
    kz, r, d = np.meshgrid(np.arange(3), np.arange(2), np.arange(8), indexing="ij")
    depth = (d * 3 + kz).reshape(-1, 1) * np.arange(NZ)[None, :] % NZ * (2 * np.pi / NZ)
    tz = np.where(r.reshape(-1, 1) == 0, np.cos(depth), -np.sin(depth))
    tz = np.concatenate(halves(tz), axis=0)

    fx = np.where(np.arange(KX) < 24, np.arange(KX), np.arange(KX) - 48 + NX)
    fy = np.where(np.arange(KY) < 24, np.arange(KY), np.arange(KY) - 48 + NY)
    phase = np.arange(NY)[:, None] * fy[None, :] % NY * (2 * np.pi / NY)
    cos, sin = np.cos(phase).reshape(8, 16, KY), np.sin(phase).reshape(8, 16, KY)
    y = np.zeros((8, 2, 16, 128))
    y[:, 0, :, 0:48], y[:, 0, :, 48:96] = cos, -sin
    y[:, 1, :, 0:48], y[:, 1, :, 48:96] = sin, cos
    y = y.reshape(8, 2, 2, 8, 128).transpose(0, 2, 1, 3, 4)
    yh, yl = halves(y.reshape(256, 128))

    g = np.arange(GX)
    first = 3 * (g // 2) + g % 2
    kx = first[:, None] + np.arange(2)[None, :]
    phase = fx[kx][:, :, None] * np.arange(NX)[None, None, :] % NX * (2 * np.pi / NX)
    both = np.stack([np.cos(phase), np.sin(phase)])
    both = both.reshape(2, GX, 2, GX, 8)
    eye = np.eye(2)
    ax = np.einsum("egtsx,mn->egmtsnx", both, eye).reshape(256, 512)
    bx = np.einsum("egtsx,mn->esmxgnt", both, eye).reshape(1024, 128)
    axh, axl = halves(ax)
    bxh, bxl = halves(bx)

    m = np.arange(64)
    kz_m = np.where(m < 48, m // 16, (m - 48) // 4)
    c_m = np.where(m < 48, m % 16, 16 + (m - 48) % 4)
    row = np.arange(120)
    sel_o = (row[None, :] // 6 == c_m[:, None]) & (row[None, :] % 6 // 2 == kz_m[:, None])
    row = np.arange(480)
    sel_c = (row[None, :] // 24 == c_m[:, None]) & (row[None, :] % 6 // 2 == kz_m[:, None])
    live = (m < 60)[:, None]
    sel_o = np.asarray((sel_o & live).astype(BF16))
    sel_c = np.asarray((sel_c & live).astype(BF16))
    return tz, yh, yl, axh, axl, bxh, bxl, sel_o, sel_c


def hops(k):
    return min(k // 4, 8 - k // 4) + min(k % 4, 4 - k % 4)


def iota(shape, axis):
    return lax.broadcasted_iota(jnp.int32, shape, axis)


def dot(a, b, dims):
    return lax.dot_general(a, b, dims, preferred_element_type=F32)


def split(x):
    high = x.astype(BF16)
    return high, (x - high.astype(F32)).astype(BF16)


def dot3(a, b, dims):
    return dot(a[0], b[0], dims) + dot(a[0], b[1], dims) + dot(a[1], b[0], dims)


def pick(sel, x):
    high, low = split(x)
    return dot(sel, high, NN) + dot(sel, low, NN)


def kernel(
    field, cot, w, pw, bias, tz, yh, yl, axh, axl, bxh, bxl, sel_o, sel_c,
    out, gf, gs, small,
    fs, cs, gh, gl, pw1, pw2, bb, pws, sy, ry, sx, rx, sp, rp, wf, tmp,
    u1, u2, d1, d2, q1, q2, lw, ls, lr, ms, mr, out_v, gf_v, gs_v, pv, fb, tz3,
    sy_sem, ry_sem, sx_sem, rx_sem, sp_sem, rp_sem, l_sem, o_sem,
):
    g = lax.axis_index("gx")
    yy = lax.axis_index("gy")
    even = lax.rem(g, 2) == 0

    barrier = pltpu.get_barrier_semaphore()

    def greet_y(k, _):
        pl.semaphore_signal(
            barrier, inc=1, device_id=(g, lax.rem(yy + k, GY)), device_id_type=MESH
        )
        return 0

    def greet_x(k, _):
        pl.semaphore_signal(
            barrier, inc=1, device_id=(lax.rem(g + k, GX), yy), device_id_type=MESH
        )
        return 0

    lax.fori_loop(1, GY, greet_y, 0)
    lax.fori_loop(1, GX, greet_x, 0)

    chip, core = yy // 2, lax.rem(yy, 2)
    others_y = [
        lax.rem(chip + n, 4) * 2 + (core if same else 1 - core)
        for n, same in ((2, 1), (2, 0), (1, 1), (3, 1), (1, 0), (3, 0), (0, 0))
    ]

    def send_y(st, h):
        sem_s, sem_r = sy_sem.at[2 * st + h], ry_sem.at[2 * st + h]
        own = pl.ds(yy * 32 + h * 16, 16)
        for d in others_y:
            pltpu.make_async_remote_copy(
                src_ref=sy.at[st, :, pl.ds(d * 32 + h * 16, 16), :],
                dst_ref=ry.at[st, :, own, :],
                send_sem=sem_s,
                recv_sem=sem_r,
                device_id=(g, d),
                device_id_type=MESH,
            ).start()
        pltpu.make_async_copy(sy.at[st, :, own, :], ry.at[st, :, own, :], sem_r).start()

    def send_y_tiles(st):
        own = pl.ds(yy * 32 + 16, 16)
        for t in range(4):
            sem = 8 + st * 2 + t
            for d in others_y:
                pltpu.make_async_remote_copy(
                    src_ref=sy.at[st, t, pl.ds(d * 32 + 16, 16), :],
                    dst_ref=ry.at[st, t, own, :],
                    send_sem=sy_sem.at[sem],
                    recv_sem=ry_sem.at[sem],
                    device_id=(g, d),
                    device_id_type=MESH,
                ).start()
            pltpu.make_async_copy(
                sy.at[st, t, own, :], ry.at[st, t, own, :], ry_sem.at[sem]
            ).start()

    def landed_y(st, h):
        landed(ry.at[st, :, pl.ds(0, 128), :], ry_sem.at[2 * st + h])

    gz, gw = g // 4, lax.rem(g, 4)
    far_first = sorted(range(1, GX), key=hops, reverse=True)

    def place(z, w):
        return w * 8 + z

    def send_gx(src, dst, ssem, rsem, size, to_owner):
        mine = place(gz, gw)
        to = g if to_owner else mine
        for k in far_first:
            z, w = lax.rem(gz + k // 4, 8), lax.rem(gw + k % 4, 4)
            at = place(z, w) if to_owner else z * 4 + w
            pltpu.make_async_remote_copy(
                src_ref=src.at[pl.ds(at * size, size)],
                dst_ref=dst.at[pl.ds(to * size, size)],
                send_sem=ssem,
                recv_sem=rsem,
                device_id=(z * 4 + w, yy),
                device_id_type=MESH,
            ).start()
        own = mine if to_owner else g
        pltpu.make_async_copy(
            src.at[pl.ds(own * size, size)], dst.at[pl.ds(to * size, size)], rsem
        ).start()

    def send_x(st):
        send_gx(sx.at[st], rx.at[st], sx_sem.at[st], rx_sem.at[st], 16, False)

    def send_p(st):
        send_gx(sp.at[st], rp.at[st], sp_sem.at[st], rp_sem.at[st], 1, st % 2 == 1)

    def send_x_tile(st, t):
        own = pl.ds(g * 16, 16)

        def remote(z, at):
            pltpu.make_async_remote_copy(
                src_ref=sx.at[st, at],
                dst_ref=rx.at[st, own],
                send_sem=sx_sem.at[st],
                recv_sem=rx_sem.at[st],
                device_id=(z * 4 + t, yy),
                device_id_type=MESH,
            ).start()

        for n in (4, 3, 5, 2, 6, 1, 7):
            z = lax.rem(gz + n, 8)
            remote(z, pl.ds(place(z, t) * 16, 16))
        at = pl.ds(place(gz, t) * 16, 16)

        @pl.when(gw != t)
        def _():
            remote(gz, at)

        @pl.when(gw == t)
        def _():
            pltpu.make_async_copy(sx.at[st, at], rx.at[st, own], rx_sem.at[st]).start()

    def landed(ref, sem):
        pltpu.make_async_copy(ref, ref, sem).wait()

    lane = iota((64, 128), 1)

    def widen(c, _):
        rows = pl.ds(c * 128, 128)
        v = field[c].astype(F32).reshape(128, 256)
        fs[0, rows, :] = v[:, :128]
        fs[1, rows, :] = v[:, 128:]
        return 0

    lax.fori_loop(0, C, widen, 0, unroll=4)

    def rows_of(ref, y):
        rows = pl.ds(y, 160, stride=16)
        return jnp.concatenate([ref[0, rows, :], ref[1, rows, :]], axis=1)

    pad_rows = jnp.zeros((96, 256), BF16)

    def analyze_z(st, h, y, s):
        for r in range(2):
            rows = pl.ds(h * 16 + r * 8 + y, 8, stride=32)
            tail = None
            for kz in range(3):
                at = (kz * 2 + r) * 8
                sy[st, kz, rows, :] = s[at : at + 8, :128]
                piece = s[at : at + 8, 128:]
                tail = piece if kz == 0 else tail + pltpu.roll(piece, 32 * kz, 1)
            sy[st, 3, rows, :] = tail

    def synthesize_z(st, h, y):
        main, tail = [], []
        for kz in range(3):
            for r in range(2):
                rows = pl.ds(h * 16 + r * 8 + y, 8, stride=32)
                main.append(ry[st, kz, rows, :])
                piece = ry[st, 3, rows, :]
                tail.append(piece if kz == 0 else pltpu.roll(piece, 128 - 32 * kz, 1))
        data = jnp.concatenate(
            [jnp.concatenate(main, axis=0), jnp.concatenate(tail, axis=0)], axis=1
        )
        high, low = split(data)
        data = jnp.concatenate([high, low, high], axis=0)
        return dot(data[:, 0:160], tz3[...], TN)


    def first_y(h, y, _):
        f = jnp.concatenate([rows_of(fs, h * 8 + y).astype(BF16), pad_rows], axis=0)
        s = dot(tz[...], f, NT)
        analyze_z(0, h, y, s[0:48] + s[48:96])
        return 0

    for h in range(2):
        lax.fori_loop(0, 8, functools.partial(first_y, h), 0, unroll=8)

    pl.semaphore_wait(barrier, GY - 1 + GX - 1)
    send_y(0, 0)
    send_y_tiles(0)

    def forward_y(st):
        landed_y(st, 0)
        for t in range(4):
            landed(ry.at[st, t, pl.ds(0, 128), :], ry_sem.at[8 + st * 2 + t])
            data = split(jnp.transpose(ry[st, t]))
            sx[st, pl.ds(t * 128, 128), :] = dot3(data, (yh[...], yl[...]), NN)
            send_x_tile(st, t)

    def forward_x(st):
        p = dot3((axh[...], axl[...]), split(rx[st]), NN)
        pc, ps = p[:128], p[128:]
        side = iota((128, 128), 1) < 48
        o = pc + jnp.where(side, pltpu.roll(ps, 80, 1), -pltpu.roll(ps, 48, 1))
        sp[st] = o.reshape(32, 4, 128)

    def spectrum(st):
        tmp[...] = rp[st].reshape(128, 128)
        k0 = tmp[pl.ds(0, 64, stride=2), :]
        k1 = tmp[pl.ds(1, 64, stride=2), :]
        roll = lambda v, n: pltpu.roll(v, n, 1)
        re_e = jnp.where(lane < 48, k0, roll(k1, 48))
        im_e = jnp.where(lane < 48, roll(k0, 80), k1)
        re_o = jnp.where(lane < 24, roll(k0, 104), roll(k1, 24))
        im_o = jnp.where(lane < 24, roll(k0, 56), roll(k1, 104))
        live = lane < 72
        re = jnp.where(live, jnp.where(even, re_e, re_o), 0.0)
        im = jnp.where(live, jnp.where(even, im_e, im_o), 0.0)
        return re, im

    def modes(re, im, st):
        roll = lambda v, n: pltpu.roll(v, n, 1)
        within = lambda a, b: (lane >= a) & (lane < b)
        zero = jnp.zeros((64, 128), F32)
        e0 = jnp.where(lane < 48, re, jnp.where(within(48, 96), roll(im, 48), zero))
        e1 = jnp.where(lane < 24, roll(re, 80), jnp.where(within(48, 72), im, zero))
        o0 = jnp.where(
            within(24, 48), roll(re, 24), jnp.where(within(72, 96), roll(im, 72), zero)
        )
        o1 = jnp.where(lane < 48, roll(re, 104), jnp.where(within(48, 96), roll(im, 24), zero))
        tmp[pl.ds(0, 64, stride=2), :] = jnp.where(even, e0, o0)
        tmp[pl.ds(1, 64, stride=2), :] = jnp.where(even, e1, o1)
        sp[st] = tmp[...].reshape(32, 4, 128)

    def inverse_x(st):
        p = dot3((bxh[...], bxl[...]), split(rp[st].reshape(128, 128)), NN)
        pc, ps = p[:512], p[512:]
        side = iota((512, 128), 1) < 48
        sx[st] = pc + jnp.where(side, -pltpu.roll(ps, 80, 1), pltpu.roll(ps, 48, 1))

    def inverse_y(st):
        for t in range(4):
            data = split(rx[st, pl.ds(t * 128, 128), :])
            sy[st, t] = dot3((yh[...], yl[...]), data, NT)

    row64 = iota((64, 128), 0)
    zeroth = (row64 < 16) | ((row64 >= 48) & (row64 < 52))
    weight_z = jnp.where(zeroth & (yy == 0), 1.0 / CELLS, 2.0 / CELLS)

    forward_y(0)

    pws[...] = jnp.zeros_like(pws)
    pws[0:20, 0:20] = pw[...].astype(F32)
    pws[32:33, 0:20] = bias[...]
    ones_e = iota((160, 128), 0) // 8 == iota((160, 128), 1)
    ones_e = jnp.where(ones_e, 1.0, 0.0)
    e = ones_e[:, :32].astype(BF16)
    same_x = lax.rem(iota((160, 160), 0), 8) == lax.rem(iota((160, 160), 1), 8)
    m = pws[0:32, 0:32].astype(BF16)
    t = dot(e, m, NT).astype(BF16)
    pw1[...] = jnp.where(same_x, dot(t, e, NT), 0.0).astype(BF16)
    t = dot(e, m, NN).astype(BF16)
    pw2[...] = jnp.where(same_x, dot(t, e, NT), 0.0).astype(BF16)
    column = jnp.sum(ones_e * pws[32:33, :], axis=1, keepdims=True)
    bb[...] = jnp.broadcast_to(column, (160, 128))
    landed(rx.at[0], rx_sem.at[0])
    forward_x(0)
    send_p(0)

    def widen_weights(c, _):
        wf[c, :, 0:72] = w[c].astype(F32).reshape(120, 72)
        return 0

    wf[...] = jnp.zeros_like(wf)
    lax.fori_loop(0, C, widen_weights, 0, unroll=4)
    landed(rp.at[0], rp_sem.at[0])
    re, im = spectrum(0)
    for kz in range(3):
        for o in range(4):
            for r in range(2):
                at = o * 6 + kz * 2 + r
                sign = 1.0 if r == 0 else -1.0
                most = pl.ds(at, 16, stride=24)
                rest = pl.ds(16 * 24 + at, 4, stride=24)
                u1[most, :] = re[kz * 16 : kz * 16 + 16]
                u1[rest, :] = re[48 + kz * 4 : 52 + kz * 4]
                u2[most, :] = sign * im[kz * 16 : kz * 16 + 16]
                u2[rest, :] = sign * im[48 + kz * 4 : 52 + kz * 4]

    real_row = lax.rem(iota((24, 128), 0), 2) == 0

    def mix(c, acc):
        a, b = acc
        rows = pl.ds(c * 24, 24)
        s1, s2 = u1[rows, :], u2[rows, :]
        sa = jnp.concatenate([jnp.where(real_row, s1, s2)] * 5, axis=0)
        sb = jnp.concatenate([jnp.where(real_row, s2, s1)] * 5, axis=0)
        return a + wf[c] * sa, b + wf[c] * sb

    zero = jnp.zeros((120, 128), F32)
    a, b = lax.fori_loop(0, C, mix, (zero, zero), unroll=4)
    modes(pick(sel_o[...], a) * weight_z, pick(sel_o[...], b) * weight_z, 1)
    send_p(1)

    tz3[0:48, :] = tz[0:48, :]
    tz3[48:96, :] = tz[0:48, :]
    tz3[96:144, :] = tz[48:96, :]

    def widen_cotangent(c, _):
        rows = pl.ds(c * 128, 128)
        v = cot[c].astype(F32).reshape(128, 256)
        cs[0, rows, :] = v[:, :128]
        cs[1, rows, :] = v[:, 128:]
        return 0

    lax.fori_loop(0, C, widen_cotangent, 0, unroll=4)
    landed(rp.at[1], rp_sem.at[1])
    inverse_x(1)
    send_x(1)

    def ahead(y, _):
        f = rows_of(fs, y).astype(BF16)
        fb[y] = f
        pv[y] = dot(pw1[...], f, NN) + jnp.concatenate([bb[...], bb[...]], axis=1)
        return 0

    lax.fori_loop(0, 16, ahead, 0, unroll=2)
    landed(rx.at[1], rx_sem.at[1])
    inverse_y(1)
    send_y(1, 0)
    send_y(1, 1)

    lw[...] = jnp.zeros_like(lw)
    ones_rows = jnp.ones((16, 256), BF16)

    def middle(h, y8, _):
        conv = synthesize_z(1, h, y8)
        y = h * 8 + y8
        f = fb[y]
        v = pv[y] + conv
        square = v * v
        t = jnp.tanh(v * (GELU_A + (GELU_A * GELU_B) * square))
        half = 0.5 + 0.5 * t
        act = v * half
        slope = half + act * (1.0 - half) * (2.0 * GELU_A + (6.0 * GELU_A * GELU_B) * square)
        grad = rows_of(cs, y) * slope
        rows = pl.ds(y, 160, stride=16)
        fs[0, rows, :] = act[:, :128]
        fs[1, rows, :] = act[:, 128:]
        high, low = split(grad)
        gh[y] = high
        gl[y] = low
        f = jnp.concatenate([tz[...], f, ones_rows], axis=0)
        p = dot(f, jnp.concatenate([high, pad_rows], axis=0), NT)
        f = jnp.concatenate([f[0:48], f[96:]], axis=0)
        n = dot(f, jnp.concatenate([low, pad_rows], axis=0), NT)
        lw[...] += p[96:] + n[48:]
        analyze_z(2, h, y8, p[0:48] + p[48:96] + n[0:48])
        return 0

    for h in range(2):
        landed_y(1, h)
        lax.fori_loop(0, 8, functools.partial(middle, h), 0, unroll=8)
        if h == 0:
            send_y(2, 0)
        else:
            send_y_tiles(2)

    row, col = iota((176, 160), 0), iota((176, 160), 1)
    keep = (row >= 160) | (lax.rem(row, 8) == lax.rem(col, 8))
    total = jnp.where(keep, lw[:, 0:160], 0.0)
    row, col = iota((32, 176), 0), iota((32, 176), 1)
    left = ((col < 160) & (col // 8 == row)) | ((row == 20) & (col == 160))
    left = jnp.where(left, 1.0, 0.0).astype(BF16)
    high, low = split(pick(left, total))
    e128 = ones_e.astype(BF16)
    packed = dot(high, e128, NN) + dot(low, e128, NN)
    ls[...] = packed[0:8] + pltpu.roll(packed[8:16], 32, 1) + pltpu.roll(packed[16:24], 64, 1)
    for k in range(1, GY):
        d = lax.rem(yy + k, GY)
        pltpu.make_async_remote_copy(
            src_ref=ls,
            dst_ref=lr.at[yy],
            send_sem=l_sem.at[0],
            recv_sem=l_sem.at[1],
            device_id=(g, d),
            device_id_type=MESH,
        ).start()
    pltpu.make_async_copy(ls, lr.at[yy], l_sem.at[1]).start()

    forward_y(2)

    def write_out(c, _):
        rows = pl.ds(c * 128, 128)
        v = jnp.concatenate([fs[0, rows, :], fs[1, rows, :]], axis=1)
        out_v[c] = v.astype(BF16).reshape(8, 16, 256)
        return 0

    lax.fori_loop(0, C, write_out, 0, unroll=4)
    pltpu.make_async_copy(out_v, out, o_sem.at[0]).start()

    landed(rx.at[2], rx_sem.at[2])
    forward_x(2)
    send_p(2)
    landed(rp.at[2], rp_sem.at[2])
    re, im = spectrum(2)
    re, im = re * weight_z, im * weight_z
    for kz in range(3):
        for r in range(2):
            most = pl.ds(kz * 2 + r, 16, stride=6)
            rest = pl.ds(96 + kz * 2 + r, 4, stride=6)
            one, two = (re, im) if r == 0 else (im, re)
            d1[most, :] = one[kz * 16 : kz * 16 + 16]
            d1[rest, :] = one[48 + kz * 4 : 52 + kz * 4]
            d2[most, :] = two[kz * 16 : kz * 16 + 16]
            d2[rest, :] = two[48 + kz * 4 : 52 + kz * 4]

    even_row = lax.rem(iota((120, 128), 0), 2) == 0

    def unmix(c, _):
        rows = pl.ds(c * 24, 24)
        x1 = d1[...]
        x2 = jnp.where(even_row, d2[...], -d2[...])
        wc = wf[c]
        q1[rows, :] = jnp.sum((wc * x1).reshape(5, 24, 128), axis=0)
        q2[rows, :] = jnp.sum((wc * x2).reshape(5, 24, 128), axis=0)
        return 0

    lax.fori_loop(0, C, unmix, 0, unroll=4)
    modes(pick(sel_c[...], q1[...]), pick(sel_c[...], q2[...]), 3)
    send_p(3)

    def outer(c, _):
        rows = pl.ds(c * 24, 24)
        s1 = jnp.concatenate([u1[rows, :]] * 5, axis=0)
        s2 = jnp.concatenate([u2[rows, :]] * 5, axis=0)
        v = s1 * d1[...] + s2 * d2[...]
        gs_v[c] = v[:, 0:72].reshape(20, 3, 2, 72)
        return 0

    lax.fori_loop(0, C, outer, 0, unroll=2)
    pltpu.make_async_copy(gs_v, gs, o_sem.at[1]).start()

    landed(rp.at[3], rp_sem.at[3])
    inverse_x(3)
    send_x(3)

    def back_ahead(y, _):
        pv[y] = dot(pw2[...], gh[y], NN) + dot(pw2[...], gl[y], NN)
        return 0

    lax.fori_loop(0, 16, back_ahead, 0, unroll=2)
    landed(rx.at[3], rx_sem.at[3])
    inverse_y(3)
    send_y(3, 0)
    send_y(3, 1)

    landed(lr, l_sem.at[1])
    ms[...] = jnp.sum(lr[...], axis=0)

    def share(k, _):
        d = lax.rem(g + k, GX)
        pltpu.make_async_remote_copy(
            src_ref=ms,
            dst_ref=mr.at[g],
            send_sem=l_sem.at[2],
            recv_sem=l_sem.at[3],
            device_id=(d, yy),
            device_id_type=MESH,
        ).start()
        return 0

    lax.fori_loop(1, GX, share, 0)
    pltpu.make_async_copy(ms, mr.at[g], l_sem.at[3]).start()


    def last(h, y8, _):
        y = h * 8 + y8
        back = pv[y] + synthesize_z(3, h, y8)
        rows = pl.ds(y, 160, stride=16)
        cs[0, rows, :] = back[:, :128]
        cs[1, rows, :] = back[:, 128:]
        return 0

    for h in range(2):
        landed_y(3, h)
        lax.fori_loop(0, 8, functools.partial(last, h), 0, unroll=8)

    def write_grad(c, _):
        rows = pl.ds(c * 128, 128)
        v = jnp.concatenate([cs[0, rows, :], cs[1, rows, :]], axis=1)
        gf_v[c] = v.astype(BF16).reshape(8, 16, 256)
        return 0

    landed(mr, l_sem.at[3])
    sums = jnp.sum(mr[...], axis=0) * (CELLS**-0.5)
    small[0:8, :] = sums
    small[8:16, :] = pltpu.roll(sums, 96, 1)
    small[16:24, :] = pltpu.roll(sums, 64, 1)

    for n in range(4):
        lax.fori_loop(n * 5, n * 5 + 5, write_grad, 0, unroll=5)
        part = pl.ds(n * 5, 5)
        pltpu.make_async_copy(gf_v.at[part], gf.at[part], o_sem.at[2 + n]).start()

    for st in range(4):
        part = sy.at[st, :, pl.ds(0, 112), :]
        for h in range(2 if st % 2 == 1 else 1):
            pltpu.make_async_copy(part, part, sy_sem.at[2 * st + h]).wait()
        if st % 2 == 0:
            for t in range(4):
                part = sy.at[st, t, pl.ds(0, 112), :]
                pltpu.make_async_copy(part, part, sy_sem.at[8 + st * 2 + t]).wait()
        part = sx.at[st, pl.ds(0, 31 * 16)]
        pltpu.make_async_copy(part, part, sx_sem.at[st]).wait()
        part = sp.at[st, pl.ds(0, 31)]
        pltpu.make_async_copy(part, part, sp_sem.at[st]).wait()
    part = lr.at[pl.ds(0, 7)]
    pltpu.make_async_copy(part, part, l_sem.at[0]).wait()
    part = mr.at[pl.ds(0, 31)]
    pltpu.make_async_copy(part, part, l_sem.at[2]).wait()
    pltpu.make_async_copy(out_v, out, o_sem.at[0]).wait()
    pltpu.make_async_copy(gs_v, gs, o_sem.at[1]).wait()
    for n in range(4):
        part = pl.ds(n * 5, 5)
        pltpu.make_async_copy(gf_v.at[part], gf.at[part], o_sem.at[2 + n]).wait()


def deliver(out_a, gf_a, gs_a, small, out, gf, gs, gp, gb, out_v, gf_v, gs_v, sems):
    there, back = [], []
    for n in range(4):
        part = pl.ds(n * 5, 5)
        for i, (a, v, b) in enumerate(
            ((out_a, out_v, out), (gf_a, gf_v, gf), (gs_a, gs_v, gs))
        ):
            sem = n * 3 + i
            there.append(pltpu.make_async_copy(a.at[part], v.at[part], sems.at[sem]))
            back.append(pltpu.make_async_copy(v.at[part], b.at[part], sems.at[12 + sem]))
    for copy in there:
        copy.start()
    gp[...] = small[0:C, 0:C]
    gb[...] = small[C : C + 1, 0:C]
    for one, other in zip(there, back):
        one.wait()
        other.start()
    for copy in back:
        copy.wait()


def local(consts, field, cotangent, spectral_weight, pointwise_weight, bias):
    vmem = pl.BlockSpec(memory_space=pltpu.VMEM)
    anywhere = pl.BlockSpec(memory_space=pl.ANY)
    dma = pltpu.SemaphoreType.DMA
    weights = jnp.transpose(spectral_weight, (1, 2, 3, 0, 4))
    scratch = [
        pltpu.VMEM((2, 2560, 128), F32),
        pltpu.VMEM((2, 2560, 128), F32),
        pltpu.VMEM((16, 160, 256), BF16),
        pltpu.VMEM((16, 160, 256), BF16),
        pltpu.VMEM((160, 160), BF16),
        pltpu.VMEM((160, 160), BF16),
        pltpu.VMEM((160, 128), F32),
        pltpu.VMEM((40, 128), F32),
        pltpu.VMEM((4, 4, 256, 128), F32),
        pltpu.VMEM((4, 4, 256, 128), F32),
        pltpu.VMEM((4, 512, 128), F32),
        pltpu.VMEM((4, 512, 128), F32),
        pltpu.VMEM((4, 32, 4, 128), F32),
        pltpu.VMEM((4, 32, 4, 128), F32),
        pltpu.VMEM((20, 120, 128), F32),
        pltpu.VMEM((128, 128), F32),
        pltpu.VMEM((480, 128), F32),
        pltpu.VMEM((480, 128), F32),
        pltpu.VMEM((120, 128), F32),
        pltpu.VMEM((120, 128), F32),
        pltpu.VMEM((480, 128), F32),
        pltpu.VMEM((480, 128), F32),
        pltpu.VMEM((176, 256), F32),
        pltpu.VMEM((8, 128), F32),
        pltpu.VMEM((8, 8, 128), F32),
        pltpu.VMEM((8, 128), F32),
        pltpu.VMEM((32, 8, 128), F32),
        pltpu.VMEM((C, 8, 16, 256), BF16),
        pltpu.VMEM((C, 8, 16, 256), BF16),
        pltpu.VMEM((C, C, 3, 2, 72), F32),
        pltpu.VMEM((16, 160, 256), F32),
        pltpu.VMEM((16, 160, 256), BF16),
        pltpu.VMEM((144, 256), BF16),
        dma((16,)), dma((16,)), dma((4,)), dma((4,)), dma((4,)), dma((4,)), dma((4,)), dma((6,)),
    ]
    out, gf, gs, small = pl.pallas_call(
        kernel,
        out_shape=(
            jax.ShapeDtypeStruct((C, 8, 16, 256), BF16),
            jax.ShapeDtypeStruct((C, 8, 16, 256), BF16),
            jax.ShapeDtypeStruct((C, C, 3, 2, 72), F32),
            jax.ShapeDtypeStruct((24, 128), F32),
        ),
        in_specs=[vmem] * 14,
        out_specs=(anywhere,) * 3 + (vmem,),
        scratch_shapes=scratch,
        compiler_params=pltpu.CompilerParams(
            collective_id=0, has_side_effects=True, vmem_limit_bytes=58 << 20
        ),
        name="fourier_layer",
    )(field, cotangent, weights, pointwise_weight, bias.reshape(1, C), *consts)
    out, gf, gs, gp, gb = pl.pallas_call(
        deliver,
        out_shape=(
            jax.ShapeDtypeStruct((C, 8, 16, 256), BF16),
            jax.ShapeDtypeStruct((C, 8, 16, 256), BF16),
            jax.ShapeDtypeStruct((C, C, 3, 2, 72), F32),
            jax.ShapeDtypeStruct((C, C), F32),
            jax.ShapeDtypeStruct((1, C), F32),
        ),
        in_specs=[anywhere] * 3 + [vmem],
        out_specs=(anywhere,) * 3 + (vmem,) * 2,
        scratch_shapes=[
            pltpu.VMEM((C, 8, 16, 256), BF16),
            pltpu.VMEM((C, 8, 16, 256), BF16),
            pltpu.VMEM((C, C, 3, 2, 72), F32),
            dma((24,)),
        ],
        compiler_params=pltpu.CompilerParams(vmem_limit_bytes=58 << 20),
        name="deliver",
    )(out, gf, gs, small)
    return out, gf, jnp.transpose(gs, (3, 0, 1, 2, 4)), gp, gb.reshape(C)


def solution(mesh):
    consts = [jnp.asarray(t) for t in tables()]
    placed = (
        P(None, "gx", "gy", None),
        P(None, "gx", "gy", None),
        P(None, None, None, "gy", "gx"),
        P(),
        P(),
    )
    return jax.shard_map(
        functools.partial(local, consts),
        mesh=mesh,
        in_specs=placed,
        out_specs=placed,
        check_vma=False,
    )
```
